256 devices in a mesh: shot: 32 (over z, y_hi, core), tm: 8 (over x, y_lo).
Axes of the slice: x: 4, y: 4 (y_hi: 2, y_lo: 2; y = y_hi * 2 + y_lo), z: 8, core: 2. Of those that a mesh axis runs over, the one named last changes fastest.
Arguments:
- blended: float32 [128, 32, 8192], P(None, 'shot', 'tm'), may hold values from -12 to 12
- delays: int32 [32, 2], replicated, may hold values from 0 to 127, as said below
- thresholds: float32 [2, 64], replicated, may hold values from 0.2 to 1.6
Outputs:
- deblended: bfloat16 [128, 64, 8192], P(None, 'shot', 'tm')
The draws below stay inside these ranges and needn't reach their ends.
Inputs may be any that keep to these rules, and one draw needn't show every extreme that they name: delays[e, k] is the delay of source 2 e + k in experiment e; some source has delay 0 and some has delay 128 - 1.
All inputs are finite; a program needn't handle non-finite values.
Results may differ from the reference program's by a relative error of at most 0.0066.
Values may be sent and summed in bfloat16 or wider, within the bound.
A program may use at most 64 MiB of HBM per device.

```python
import math
import jax
import jax.numpy as jnp
from jax import lax

SRC = 64
SRC_EXP = 2
WIN = 256
BLK = 128
ITERS = 2
EXPS = 32
RCV = 128
NT = 8192


def draw_delays(key, part):
    entries = EXPS * SRC_EXP
    initial = jax.random.randint(key, (entries,), 0, BLK)
    highest = jax.random.randint(jax.random.fold_in(key, 11), (), 0, entries)
    stride = jax.random.randint(jax.random.fold_in(key, 12), (), 1, entries)
    lowest = (highest + stride) % entries
    values = initial.at[highest].set(BLK - 1).at[lowest].set(0)
    return values.reshape(EXPS, SRC_EXP).astype(jnp.int32)


def block_levels(stream_key, shape, cuts, smallest, high):
    level = 1.0
    for axis_at, parts in cuts:
        draws = jax.random.uniform(jax.random.fold_in(jax.random.fold_in(stream_key, 6), axis_at), (parts,), jnp.float32, smallest / len(cuts), high / len(cuts))
        level = level * jnp.repeat(jnp.exp(draws), shape[axis_at] // parts).reshape((-1,) + (1,) * (len(shape) - 1 - axis_at))
    return level


def noise(key, dims, width, most, pieces=(), held_as=jnp.bfloat16):
    values = width * jax.random.normal(key, dims, jnp.float32)
    if pieces:
        values = values * block_levels(key, dims, pieces, -0.22, 0.18)
    return jnp.clip(values, -most, most).astype(held_as)


def setup_inputs(seed: int = 0) -> dict:
    key_of = jax.random.split(jax.random.key(seed), 4)
    blended = noise(key_of[0], (RCV, EXPS, NT), 2.0, 12.0, ((1, 32), (2, 8)), jnp.float32)
    delays = draw_delays(jax.random.fold_in(key_of[3], 71), 0)
    thresholds = jnp.clip(jnp.exp(jax.random.uniform(key_of[2], (ITERS, SRC), jnp.float32, math.log(0.2), math.log(1.6))), 0.2, 1.6)
    return dict(blended=blended, delays=delays, thresholds=thresholds)


RELAX = 0.5

def blend_one(estimate, delays):
    samples = estimate.shape[1]
    moment = jnp.arange(samples, dtype=jnp.int32)
    source_rows = estimate.reshape(EXPS, SRC_EXP, samples).astype(jnp.float32)
    anchor = moment[None, None, :] - delays[:, :, None]
    picked = jnp.take_along_axis(source_rows, jnp.clip(anchor, 0, samples - 1).astype(jnp.int32), axis=2)
    picked = jnp.where(anchor >= 0, picked, jnp.zeros_like(picked))
    return lax.optimization_barrier(jnp.sum(picked, axis=1))

def spread_one(residual, delays):
    samples = residual.shape[1]
    moment = jnp.arange(samples, dtype=jnp.int32)
    target = moment[None, None, :] + delays[:, :, None]
    widened = jnp.broadcast_to(residual.astype(jnp.float32)[:, None, :], (EXPS, SRC_EXP, samples))
    picked = jnp.take_along_axis(widened, jnp.clip(target, 0, samples - 1).astype(jnp.int32), axis=2)
    picked = jnp.where(target < samples, picked, jnp.zeros_like(picked))
    return picked.reshape(SRC, samples)

def time_tables():
    first_index = jnp.arange(WIN, dtype=jnp.int32)[:, None]
    second_index = jnp.arange(WIN, dtype=jnp.int32)[None, :]
    angle = (first_index * second_index % WIN).astype(jnp.float32) * (2.0 * math.pi / WIN)
    return (jnp.cos(angle).astype(jnp.bfloat16), jnp.sin(angle).astype(jnp.bfloat16))

def filter_one(update, limits):
    samples = update.shape[1]
    windows = samples // WIN
    cos_table, sin_table = time_tables()
    signal = update.astype(jnp.bfloat16).reshape(SRC * windows, WIN)
    scale = 1.0 / math.sqrt(WIN)
    real_time = jnp.dot(signal, cos_table, preferred_element_type=jnp.float32) * scale
    imag_time = -jnp.dot(signal, sin_table, preferred_element_type=jnp.float32) * scale
    halfway = (real_time + 1j * imag_time).reshape(SRC, windows, WIN)
    coeffs = jnp.fft.fft(halfway, axis=0, norm='ortho')
    magnitude = jnp.abs(coeffs)
    bound = limits[:, None, None]
    factor = jnp.maximum(magnitude - bound, 0.0) / jnp.maximum(magnitude, bound)
    restored = jnp.fft.ifft2(coeffs * factor, axes=(0, 2), norm='ortho')
    return jnp.real(restored).reshape(SRC, samples)

def reference(blended, delays, thresholds):

    def receiver(records):
        estimate = jnp.zeros((SRC, records.shape[1]), jnp.bfloat16)
        for sweep in range(ITERS):
            residual = (records - blend_one(estimate, delays)).astype(jnp.bfloat16)
            update = (estimate.astype(jnp.float32) + RELAX * spread_one(residual, delays)).astype(jnp.bfloat16)
            estimate = filter_one(update, thresholds[sweep]).astype(jnp.bfloat16)
        return estimate
    return lax.map(receiver, blended)
```

```python
import math

import jax
import jax.numpy as jnp
from jax import lax
from jax.sharding import PartitionSpec as P

SRC = 64
SRC_EXP = 2
WIN = 256
BLK = 128
ITERS = 2


RELAX = 0.5


def shifted(array, axis, by):
    count = lax.axis_size(axis)
    pairs = [(i, i + by) for i in range(count) if 0 <= i + by < count]
    return lax.ppermute(array, axis, pairs)


def phase_table(length_first, length_second, period):
    first_index = jnp.arange(length_first, dtype=jnp.int32)[:, None]
    second_index = jnp.arange(length_second, dtype=jnp.int32)[None, :]
    return (first_index * second_index % period).astype(jnp.float32) * (2.0 * math.pi / period)


def make_tables():
    time_angle = phase_table(WIN, WIN, WIN)
    time_scale = 1.0 / math.sqrt(WIN)
    cos_forward = jnp.cos(time_angle).astype(jnp.bfloat16)
    sin_forward = -jnp.sin(time_angle).astype(jnp.bfloat16)
    cos_inverse = jnp.cos(time_angle) * time_scale
    sin_inverse = -jnp.sin(time_angle) * time_scale
    source_angle = phase_table(SRC, SRC, SRC)
    cos_source = jnp.cos(source_angle) / math.sqrt(SRC)
    sin_source = jnp.sin(source_angle) / math.sqrt(SRC)
    return (cos_forward, sin_forward, cos_inverse, sin_inverse, cos_source, sin_source)


def blend(estimate, own_delays):
    receivers, sources, samples = estimate.shape
    blocks = samples // BLK
    experiments = sources // SRC_EXP
    earlier = shifted(estimate[:, :, samples - BLK :], "tm", 1)
    upper = estimate.reshape(receivers, sources, blocks, BLK)
    shifts = own_delays.reshape(-1)
    row_index = jnp.arange(BLK, dtype=jnp.int32)[None, :, None]
    column_index = jnp.arange(BLK, dtype=jnp.int32)[None, None, :]
    select_same = (row_index == column_index - shifts[:, None, None]).astype(jnp.bfloat16)
    select_prior = (row_index == BLK + column_index - shifts[:, None, None]).astype(jnp.bfloat16)
    same = jnp.einsum("rsnb,sbi->rsni", upper, select_same, preferred_element_type=jnp.float32)
    onward = jnp.einsum("rsnb,sbi->rsni", upper, select_prior, preferred_element_type=jnp.float32)
    edge_part = jnp.einsum(
        "rsb,sbi->rsi", earlier, select_prior, preferred_element_type=jnp.float32
    )
    same = jnp.sum(same.reshape(receivers, experiments, SRC_EXP, blocks, BLK), axis=2)
    onward = jnp.sum(onward.reshape(receivers, experiments, SRC_EXP, blocks, BLK), axis=2)
    edge_part = jnp.sum(edge_part.reshape(receivers, experiments, SRC_EXP, BLK), axis=2)
    carried = jnp.concatenate([edge_part[:, :, None], onward[:, :, : blocks - 1]], axis=2)
    return (same + carried).reshape(receivers, experiments, samples)


def spread(residual, own_delays):
    receivers, experiments, samples = residual.shape
    blocks = samples // BLK
    later = shifted(residual[:, :, :BLK], "tm", -1)
    lower = residual.reshape(receivers, experiments, blocks, BLK)
    row_index = jnp.arange(BLK, dtype=jnp.int32)[None, None, :, None]
    column_index = jnp.arange(BLK, dtype=jnp.int32)[None, None, None, :]
    select_same = (row_index == column_index + own_delays[:, :, None, None]).astype(jnp.bfloat16)
    select_next = (row_index + BLK == column_index + own_delays[:, :, None, None]).astype(
        jnp.bfloat16
    )
    same = jnp.einsum("rena,ekai->rekni", lower, select_same, preferred_element_type=jnp.float32)
    backward = jnp.einsum(
        "rena,ekai->rekni", lower, select_next, preferred_element_type=jnp.float32
    )
    edge_part = jnp.einsum("rea,ekai->reki", later, select_next, preferred_element_type=jnp.float32)
    carried = jnp.concatenate([backward[:, :, :, 1:], edge_part[:, :, :, None]], axis=3)
    return (same + carried).reshape(receivers, experiments * SRC_EXP, samples)


def coherence(gathers, limits, tables):
    cos_forward, sin_forward, cos_inverse, sin_inverse, cos_source, sin_source = tables
    receivers, sources, samples = gathers.shape
    windows = samples // WIN
    careful = lax.Precision.HIGH
    scale = 1.0 / math.sqrt(WIN)
    signal = gathers.reshape(receivers * sources * windows, WIN)
    real_time = (jnp.dot(signal, cos_forward, preferred_element_type=jnp.float32) * scale).reshape(
        receivers, sources, samples
    )
    imag_time = (jnp.dot(signal, sin_forward, preferred_element_type=jnp.float32) * scale).reshape(
        receivers, sources, samples
    )

    def mixing(table, field):
        return jnp.einsum(
            "ps,rsx->rpx", table, field, precision=careful, preferred_element_type=jnp.float32
        )

    real_part = mixing(cos_source, real_time) + mixing(sin_source, imag_time)
    imag_part = mixing(cos_source, imag_time) - mixing(sin_source, real_time)
    magnitude = jnp.sqrt(real_part * real_part + imag_part * imag_part)
    bound = limits[None, :, None]
    factor = jnp.maximum(magnitude - bound, 0.0) / jnp.maximum(magnitude, bound)
    kept_real = real_part * factor
    kept_imag = imag_part * factor
    back_real = mixing(cos_source, kept_real) - mixing(sin_source, kept_imag)
    back_imag = mixing(cos_source, kept_imag) + mixing(sin_source, kept_real)
    restored = jnp.dot(
        back_real.reshape(-1, WIN),
        cos_inverse,
        precision=careful,
        preferred_element_type=jnp.float32,
    )
    restored = restored + jnp.dot(
        back_imag.reshape(-1, WIN),
        sin_inverse,
        precision=careful,
        preferred_element_type=jnp.float32,
    )
    return restored.reshape(receivers, sources, samples)


def local(blended, delays, thresholds):
    tables = make_tables()
    records = lax.all_to_all(blended, "shot", split_axis=0, concat_axis=1, tiled=True)
    estimate = None
    for sweep in range(ITERS):
        if sweep == 0:
            residual = records.astype(jnp.bfloat16)
            update = (RELAX * spread(residual, delays)).astype(jnp.bfloat16)
        else:
            residual = (records - blend(estimate, delays)).astype(jnp.bfloat16)
            update = (estimate.astype(jnp.float32) + RELAX * spread(residual, delays)).astype(
                jnp.bfloat16
            )
        estimate = coherence(update, thresholds[sweep], tables).astype(jnp.bfloat16)
    return lax.all_to_all(estimate, "shot", split_axis=1, concat_axis=0, tiled=True)


def solution(mesh):
    return jax.shard_map(
        local,
        mesh=mesh,
        in_specs=(P(None, "shot", "tm"), P(), P()),
        out_specs=P(None, "shot", "tm"),
        check_vma=False,
    )
```

```python
import math

import jax
import jax.numpy as jnp
from jax import lax
from jax.sharding import PartitionSpec as P

SRC = 64
SRC_EXP = 2
WIN = 256
BLK = 128
ITERS = 2


RELAX = 0.5


def shifted(array, axis, by):
    count = lax.axis_size(axis)
    pairs = [(i, i + by) for i in range(count) if 0 <= i + by < count]
    return lax.ppermute(array, axis, pairs)


def phase_table(length_first, length_second, period):
    first_index = jnp.arange(length_first, dtype=jnp.int32)[:, None]
    second_index = jnp.arange(length_second, dtype=jnp.int32)[None, :]
    return (first_index * second_index % period).astype(jnp.float32) * (2.0 * math.pi / period)


def make_tables():
    time_angle = phase_table(WIN, WIN, WIN)
    time_scale = 1.0 / math.sqrt(WIN)
    cos_forward = jnp.cos(time_angle).astype(jnp.bfloat16)
    sin_forward = -jnp.sin(time_angle).astype(jnp.bfloat16)
    cos_inverse = jnp.cos(time_angle) * time_scale
    sin_inverse = -jnp.sin(time_angle) * time_scale
    source_angle = phase_table(SRC, SRC, SRC)
    cos_source = jnp.cos(source_angle) / math.sqrt(SRC)
    sin_source = jnp.sin(source_angle) / math.sqrt(SRC)
    return (cos_forward, sin_forward, cos_inverse, sin_inverse, cos_source, sin_source)


def blend(estimate, own_delays):
    receivers, sources, samples = estimate.shape
    blocks = samples // BLK
    experiments = sources // SRC_EXP
    earlier = shifted(estimate[:, :, samples - BLK :], "tm", 1)
    upper = estimate.reshape(receivers, sources, blocks, BLK)
    shifts = own_delays.reshape(-1)
    row_index = jnp.arange(BLK, dtype=jnp.int32)[None, :, None]
    column_index = jnp.arange(BLK, dtype=jnp.int32)[None, None, :]
    select_same = (row_index == column_index - shifts[:, None, None]).astype(jnp.bfloat16)
    select_prior = (row_index == BLK + column_index - shifts[:, None, None]).astype(jnp.bfloat16)
    same = jnp.einsum("rsnb,sbi->rsni", upper, select_same, preferred_element_type=jnp.float32)
    onward = jnp.einsum("rsnb,sbi->rsni", upper, select_prior, preferred_element_type=jnp.float32)
    edge_part = jnp.einsum(
        "rsb,sbi->rsi", earlier, select_prior, preferred_element_type=jnp.float32
    )
    same = jnp.sum(same.reshape(receivers, experiments, SRC_EXP, blocks, BLK), axis=2)
    onward = jnp.sum(onward.reshape(receivers, experiments, SRC_EXP, blocks, BLK), axis=2)
    edge_part = jnp.sum(edge_part.reshape(receivers, experiments, SRC_EXP, BLK), axis=2)
    carried = jnp.concatenate([edge_part[:, :, None], onward[:, :, : blocks - 1]], axis=2)
    return (same + carried).reshape(receivers, experiments, samples)


def spread(residual, own_delays):
    receivers, experiments, samples = residual.shape
    blocks = samples // BLK
    later = shifted(residual[:, :, :BLK], "tm", -1)
    lower = residual.reshape(receivers, experiments, blocks, BLK)
    row_index = jnp.arange(BLK, dtype=jnp.int32)[None, None, :, None]
    column_index = jnp.arange(BLK, dtype=jnp.int32)[None, None, None, :]
    select_same = (row_index == column_index + own_delays[:, :, None, None]).astype(jnp.bfloat16)
    select_next = (row_index + BLK == column_index + own_delays[:, :, None, None]).astype(
        jnp.bfloat16
    )
    same = jnp.einsum("rena,ekai->rekni", lower, select_same, preferred_element_type=jnp.float32)
    backward = jnp.einsum(
        "rena,ekai->rekni", lower, select_next, preferred_element_type=jnp.float32
    )
    edge_part = jnp.einsum("rea,ekai->reki", later, select_next, preferred_element_type=jnp.float32)
    carried = jnp.concatenate([backward[:, :, :, 1:], edge_part[:, :, :, None]], axis=3)
    return (same + carried).reshape(receivers, experiments * SRC_EXP, samples)


def coherence(gathers, limits, tables):
    cos_forward, sin_forward, cos_inverse, sin_inverse, cos_source, sin_source = tables
    receivers, sources, samples = gathers.shape
    windows = samples // WIN
    careful = lax.Precision.HIGH
    scale = 1.0 / math.sqrt(WIN)
    signal = gathers.reshape(receivers * sources * windows, WIN)
    real_time = (jnp.dot(signal, cos_forward, preferred_element_type=jnp.float32) * scale).reshape(
        receivers, sources, samples
    )
    imag_time = (jnp.dot(signal, sin_forward, preferred_element_type=jnp.float32) * scale).reshape(
        receivers, sources, samples
    )

    def mixing(table, field):
        return jnp.einsum(
            "ps,rsx->rpx", table, field, precision=careful, preferred_element_type=jnp.float32
        )

    real_part = mixing(cos_source, real_time) + mixing(sin_source, imag_time)
    imag_part = mixing(cos_source, imag_time) - mixing(sin_source, real_time)
    magnitude = jnp.sqrt(real_part * real_part + imag_part * imag_part)
    bound = limits[None, :, None]
    factor = jnp.maximum(magnitude - bound, 0.0) / jnp.maximum(magnitude, bound)
    kept_real = real_part * factor
    kept_imag = imag_part * factor
    back_real = mixing(cos_source, kept_real) - mixing(sin_source, kept_imag)
    back_imag = mixing(cos_source, kept_imag) + mixing(sin_source, kept_real)
    restored = jnp.dot(
        back_real.reshape(-1, WIN),
        cos_inverse,
        precision=careful,
        preferred_element_type=jnp.float32,
    )
    restored = restored + jnp.dot(
        back_imag.reshape(-1, WIN),
        sin_inverse,
        precision=careful,
        preferred_element_type=jnp.float32,
    )
    return restored.reshape(receivers, sources, samples)


def local(blended, delays, thresholds):
    tables = make_tables()
    records = lax.all_to_all(
        blended.astype(jnp.bfloat16), "shot", split_axis=0, concat_axis=1, tiled=True
    ).astype(jnp.float32)
    estimate = None
    for sweep in range(ITERS):
        if sweep == 0:
            residual = records.astype(jnp.bfloat16)
            update = (RELAX * spread(residual, delays)).astype(jnp.bfloat16)
        else:
            residual = (records - blend(estimate, delays)).astype(jnp.bfloat16)
            update = (estimate.astype(jnp.float32) + RELAX * spread(residual, delays)).astype(
                jnp.bfloat16
            )
        estimate = coherence(update, thresholds[sweep], tables).astype(jnp.bfloat16)
    return lax.all_to_all(estimate, "shot", split_axis=1, concat_axis=0, tiled=True)


def solution(mesh):
    return jax.shard_map(
        local,
        mesh=mesh,
        in_specs=(P(None, "shot", "tm"), P(), P()),
        out_specs=P(None, "shot", "tm"),
        check_vma=False,
    )
```

```python
import math

import jax
import jax.numpy as jnp
from jax import lax
from jax.experimental import pallas as pl
from jax.experimental.pallas import tpu as pltpu
from jax.sharding import PartitionSpec as P

SRC = 64
SRC_EXP = 2
WIN = 256
BLK = 128
ITERS = 2


RELAX = 0.5


def shifted(array, axis, by):
    count = lax.axis_size(axis)
    pairs = [(i, i + by) for i in range(count) if 0 <= i + by < count]
    return lax.ppermute(array, axis, pairs)


def phase_table(length_first, length_second, period):
    first_index = jnp.arange(length_first, dtype=jnp.int32)[:, None]
    second_index = jnp.arange(length_second, dtype=jnp.int32)[None, :]
    return (first_index * second_index % period).astype(jnp.float32) * (2.0 * math.pi / period)


def make_tables():
    time_angle = phase_table(WIN, WIN, WIN)
    time_scale = 1.0 / math.sqrt(WIN)
    cos_forward = jnp.cos(time_angle).astype(jnp.bfloat16)
    sin_forward = -jnp.sin(time_angle).astype(jnp.bfloat16)
    cos_inverse = jnp.cos(time_angle) * time_scale
    sin_inverse = -jnp.sin(time_angle) * time_scale
    source_angle = phase_table(SRC, SRC, SRC)
    cos_source = jnp.cos(source_angle) / math.sqrt(SRC)
    sin_source = jnp.sin(source_angle) / math.sqrt(SRC)
    return (cos_forward, sin_forward, cos_inverse, sin_inverse, cos_source, sin_source)


def blend(estimate, own_delays):
    receivers, sources, samples = estimate.shape
    blocks = samples // BLK
    experiments = sources // SRC_EXP
    earlier = shifted(estimate[:, :, samples - BLK :], "tm", 1)
    upper = estimate.reshape(receivers, sources, blocks, BLK)
    shifts = own_delays.reshape(-1)
    row_index = jnp.arange(BLK, dtype=jnp.int32)[None, :, None]
    column_index = jnp.arange(BLK, dtype=jnp.int32)[None, None, :]
    select_same = (row_index == column_index - shifts[:, None, None]).astype(jnp.bfloat16)
    select_prior = (row_index == BLK + column_index - shifts[:, None, None]).astype(jnp.bfloat16)
    same = jnp.einsum("rsnb,sbi->rsni", upper, select_same, preferred_element_type=jnp.float32)
    onward = jnp.einsum("rsnb,sbi->rsni", upper, select_prior, preferred_element_type=jnp.float32)
    edge_part = jnp.einsum(
        "rsb,sbi->rsi", earlier, select_prior, preferred_element_type=jnp.float32
    )
    same = jnp.sum(same.reshape(receivers, experiments, SRC_EXP, blocks, BLK), axis=2)
    onward = jnp.sum(onward.reshape(receivers, experiments, SRC_EXP, blocks, BLK), axis=2)
    edge_part = jnp.sum(edge_part.reshape(receivers, experiments, SRC_EXP, BLK), axis=2)
    carried = jnp.concatenate([edge_part[:, :, None], onward[:, :, : blocks - 1]], axis=2)
    return (same + carried).reshape(receivers, experiments, samples)


def spread(residual, own_delays):
    receivers, experiments, samples = residual.shape
    blocks = samples // BLK
    later = shifted(residual[:, :, :BLK], "tm", -1)
    lower = residual.reshape(receivers, experiments, blocks, BLK)
    row_index = jnp.arange(BLK, dtype=jnp.int32)[None, None, :, None]
    column_index = jnp.arange(BLK, dtype=jnp.int32)[None, None, None, :]
    select_same = (row_index == column_index + own_delays[:, :, None, None]).astype(jnp.bfloat16)
    select_next = (row_index + BLK == column_index + own_delays[:, :, None, None]).astype(
        jnp.bfloat16
    )
    same = jnp.einsum("rena,ekai->rekni", lower, select_same, preferred_element_type=jnp.float32)
    backward = jnp.einsum(
        "rena,ekai->rekni", lower, select_next, preferred_element_type=jnp.float32
    )
    edge_part = jnp.einsum("rea,ekai->reki", later, select_next, preferred_element_type=jnp.float32)
    carried = jnp.concatenate([backward[:, :, :, 1:], edge_part[:, :, :, None]], axis=3)
    return (same + carried).reshape(receivers, experiments * SRC_EXP, samples)


def filter_tables():
    time_angle = phase_table(WIN, WIN, WIN)
    time_scale = 1.0 / math.sqrt(WIN)
    forward = jnp.concatenate(
        [jnp.cos(time_angle).astype(jnp.bfloat16), -jnp.sin(time_angle).astype(jnp.bfloat16)],
        axis=1,
    )
    inverse = jnp.concatenate(
        [jnp.cos(time_angle) * time_scale, -jnp.sin(time_angle) * time_scale], axis=0
    )
    source_angle = phase_table(SRC, SRC, SRC)
    cos_source = jnp.cos(source_angle) / math.sqrt(SRC)
    sin_source = jnp.sin(source_angle) / math.sqrt(SRC)
    mix_forward = jnp.block([[cos_source, sin_source], [-sin_source, cos_source]])
    mix_inverse = jnp.block([[cos_source, -sin_source], [sin_source, cos_source]])
    return forward, inverse, mix_forward, mix_inverse


def filter_kernel(u_ref, forward_ref, inverse_ref, mixf_ref, mixi_ref, limit_ref, out_ref):
    sources = u_ref.shape[1]
    windows = u_ref.shape[2] // WIN
    scale = 1.0 / math.sqrt(WIN)
    exact = lax.Precision.HIGHEST
    limit = limit_ref[...]
    for w in range(windows):
        cols = slice(w * WIN, (w + 1) * WIN)
        spectrum = jnp.dot(u_ref[0, :, cols], forward_ref[...], preferred_element_type=jnp.float32)
        spectrum = spectrum * scale
        stacked = jnp.concatenate([spectrum[:, :WIN], spectrum[:, WIN:]], axis=0)
        coeffs = jnp.dot(mixf_ref[...], stacked, precision=exact, preferred_element_type=jnp.float32)
        real_part = coeffs[:sources]
        imag_part = coeffs[sources:]
        magnitude = jnp.sqrt(real_part * real_part + imag_part * imag_part)
        factor = jnp.maximum(magnitude - limit, 0.0) / jnp.maximum(magnitude, limit)
        kept = jnp.concatenate([real_part * factor, imag_part * factor], axis=0)
        back = jnp.dot(mixi_ref[...], kept, precision=exact, preferred_element_type=jnp.float32)
        joined = jnp.concatenate([back[:sources], back[sources:]], axis=1)
        restored = jnp.dot(joined, inverse_ref[...], precision=exact, preferred_element_type=jnp.float32)
        out_ref[0, :, cols] = restored.astype(out_ref.dtype)


def coherence(gathers, limits, tables):
    forward, inverse, mix_forward, mix_inverse = tables
    receivers, sources, samples = gathers.shape
    whole = lambda r: (0, 0)
    return pl.pallas_call(
        filter_kernel,
        grid=(receivers,),
        in_specs=[
            pl.BlockSpec((1, sources, samples), lambda r: (r, 0, 0)),
            pl.BlockSpec(forward.shape, whole),
            pl.BlockSpec(inverse.shape, whole),
            pl.BlockSpec(mix_forward.shape, whole),
            pl.BlockSpec(mix_inverse.shape, whole),
            pl.BlockSpec((sources, 1), whole),
        ],
        out_specs=pl.BlockSpec((1, sources, samples), lambda r: (r, 0, 0)),
        out_shape=jax.ShapeDtypeStruct(gathers.shape, jnp.bfloat16),
    )(gathers, forward, inverse, mix_forward, mix_inverse, limits.reshape(sources, 1))


def local(blended, delays, thresholds):
    tables = filter_tables()
    records = lax.all_to_all(blended, "shot", split_axis=0, concat_axis=1, tiled=True)
    estimate = None
    for sweep in range(ITERS):
        if sweep == 0:
            residual = records.astype(jnp.bfloat16)
            update = (RELAX * spread(residual, delays)).astype(jnp.bfloat16)
        else:
            residual = (records - blend(estimate, delays)).astype(jnp.bfloat16)
            update = (estimate.astype(jnp.float32) + RELAX * spread(residual, delays)).astype(
                jnp.bfloat16
            )
        estimate = coherence(update, thresholds[sweep], tables).astype(jnp.bfloat16)
    return lax.all_to_all(estimate, "shot", split_axis=1, concat_axis=0, tiled=True)


def solution(mesh):
    return jax.shard_map(
        local,
        mesh=mesh,
        in_specs=(P(None, "shot", "tm"), P(), P()),
        out_specs=P(None, "shot", "tm"),
        check_vma=False,
    )
```

```python
import math

import jax
import jax.numpy as jnp
from jax import lax
from jax.experimental import pallas as pl
from jax.experimental.pallas import tpu as pltpu
from jax.sharding import PartitionSpec as P

SRC = 64
SRC_EXP = 2
WIN = 256
BLK = 128
ITERS = 2


RELAX = 0.5


def shifted(array, axis, by):
    count = lax.axis_size(axis)
    pairs = [(i, i + by) for i in range(count) if 0 <= i + by < count]
    return lax.ppermute(array, axis, pairs)


def phase_table(length_first, length_second, period):
    first_index = jnp.arange(length_first, dtype=jnp.int32)[:, None]
    second_index = jnp.arange(length_second, dtype=jnp.int32)[None, :]
    return (first_index * second_index % period).astype(jnp.float32) * (2.0 * math.pi / period)


def make_tables():
    time_angle = phase_table(WIN, WIN, WIN)
    time_scale = 1.0 / math.sqrt(WIN)
    cos_forward = jnp.cos(time_angle).astype(jnp.bfloat16)
    sin_forward = -jnp.sin(time_angle).astype(jnp.bfloat16)
    cos_inverse = jnp.cos(time_angle) * time_scale
    sin_inverse = -jnp.sin(time_angle) * time_scale
    source_angle = phase_table(SRC, SRC, SRC)
    cos_source = jnp.cos(source_angle) / math.sqrt(SRC)
    sin_source = jnp.sin(source_angle) / math.sqrt(SRC)
    return (cos_forward, sin_forward, cos_inverse, sin_inverse, cos_source, sin_source)


def blend(estimate, own_delays):
    receivers, sources, samples = estimate.shape
    blocks = samples // BLK
    experiments = sources // SRC_EXP
    earlier = shifted(estimate[:, :, samples - BLK :], "tm", 1)
    upper = estimate.reshape(receivers, sources, blocks, BLK)
    shifts = own_delays.reshape(-1)
    row_index = jnp.arange(BLK, dtype=jnp.int32)[None, :, None]
    column_index = jnp.arange(BLK, dtype=jnp.int32)[None, None, :]
    select_same = (row_index == column_index - shifts[:, None, None]).astype(jnp.bfloat16)
    select_prior = (row_index == BLK + column_index - shifts[:, None, None]).astype(jnp.bfloat16)
    same = jnp.einsum("rsnb,sbi->rsni", upper, select_same, preferred_element_type=jnp.float32)
    onward = jnp.einsum("rsnb,sbi->rsni", upper, select_prior, preferred_element_type=jnp.float32)
    edge_part = jnp.einsum(
        "rsb,sbi->rsi", earlier, select_prior, preferred_element_type=jnp.float32
    )
    same = jnp.sum(same.reshape(receivers, experiments, SRC_EXP, blocks, BLK), axis=2)
    onward = jnp.sum(onward.reshape(receivers, experiments, SRC_EXP, blocks, BLK), axis=2)
    edge_part = jnp.sum(edge_part.reshape(receivers, experiments, SRC_EXP, BLK), axis=2)
    carried = jnp.concatenate([edge_part[:, :, None], onward[:, :, : blocks - 1]], axis=2)
    return (same + carried).reshape(receivers, experiments, samples)


def spread(residual, own_delays):
    receivers, experiments, samples = residual.shape
    blocks = samples // BLK
    later = shifted(residual[:, :, :BLK], "tm", -1)
    lower = residual.reshape(receivers, experiments, blocks, BLK)
    row_index = jnp.arange(BLK, dtype=jnp.int32)[None, None, :, None]
    column_index = jnp.arange(BLK, dtype=jnp.int32)[None, None, None, :]
    select_same = (row_index == column_index + own_delays[:, :, None, None]).astype(jnp.bfloat16)
    select_next = (row_index + BLK == column_index + own_delays[:, :, None, None]).astype(
        jnp.bfloat16
    )
    same = jnp.einsum("rena,ekai->rekni", lower, select_same, preferred_element_type=jnp.float32)
    backward = jnp.einsum(
        "rena,ekai->rekni", lower, select_next, preferred_element_type=jnp.float32
    )
    edge_part = jnp.einsum("rea,ekai->reki", later, select_next, preferred_element_type=jnp.float32)
    carried = jnp.concatenate([backward[:, :, :, 1:], edge_part[:, :, :, None]], axis=3)
    return (same + carried).reshape(receivers, experiments * SRC_EXP, samples)


def split(value):
    high = value.astype(jnp.bfloat16)
    return high, (value - high.astype(jnp.float32)).astype(jnp.bfloat16)


def filter_tables():
    time_angle = phase_table(WIN, WIN, WIN)
    time_scale = 1.0 / math.sqrt(WIN)
    forward = jnp.concatenate(
        [jnp.cos(time_angle).astype(jnp.bfloat16), -jnp.sin(time_angle).astype(jnp.bfloat16)],
        axis=1,
    )
    inverse_high, inverse_low = split(
        jnp.concatenate([jnp.cos(time_angle) * time_scale, -jnp.sin(time_angle) * time_scale], 0)
    )
    inverse = jnp.concatenate([inverse_high, inverse_high, inverse_low], axis=0)
    source_angle = phase_table(SRC, SRC, SRC)
    cos_source = jnp.cos(source_angle) / math.sqrt(SRC)
    sin_source = jnp.sin(source_angle) / math.sqrt(SRC)
    mix_forward = split(jnp.block([[cos_source, sin_source], [-sin_source, cos_source]]))
    mix_inverse = split(jnp.block([[cos_source, -sin_source], [sin_source, cos_source]]))
    return forward, inverse, mix_forward, mix_inverse


def mix(table, value):
    table_high, table_low = table
    value_high, value_low = split(value)
    stacked = jnp.concatenate([value_high, value_low, value_high], axis=0)
    joined = jnp.concatenate([table_high, table_high, table_low], axis=1)
    return jnp.dot(joined, stacked, preferred_element_type=jnp.float32)


def filter_kernel(
    u_ref, forward_ref, inverse_ref, mfh_ref, mfl_ref, mih_ref, mil_ref, limit_ref, out_ref
):
    receivers, sources, samples = u_ref.shape
    windows = samples // WIN
    groups = [(r, w) for r in range(receivers) for w in range(windows)]
    scale = 1.0 / math.sqrt(WIN)
    rows = jnp.concatenate(
        [u_ref[r, :, w * WIN : (w + 1) * WIN] for r, w in groups], axis=0
    )
    spectrum = jnp.dot(rows, forward_ref[...], preferred_element_type=jnp.float32) * scale
    block = lambda g: slice(g * sources, (g + 1) * sources)
    field = jnp.concatenate(
        [
            jnp.concatenate([spectrum[block(g), :WIN], spectrum[block(g), WIN:]], axis=0)
            for g in range(len(groups))
        ],
        axis=1,
    )
    coeffs = mix((mfh_ref[...], mfl_ref[...]), field)
    real_part = coeffs[:sources]
    imag_part = coeffs[sources:]
    limit = limit_ref[...]
    magnitude = jnp.sqrt(real_part * real_part + imag_part * imag_part)
    factor = jnp.maximum(magnitude - limit, 0.0) / jnp.maximum(magnitude, limit)
    kept = jnp.concatenate([real_part * factor, imag_part * factor], axis=0)
    back = mix((mih_ref[...], mil_ref[...]), kept)
    lanes = lambda g: slice(g * WIN, (g + 1) * WIN)
    joined = jnp.concatenate(
        [
            jnp.concatenate([back[:sources, lanes(g)], back[sources:, lanes(g)]], axis=1)
            for g in range(len(groups))
        ],
        axis=0,
    )
    joined_high, joined_low = split(joined)
    restored = jnp.dot(
        jnp.concatenate([joined_high, joined_low, joined_high], axis=1),
        inverse_ref[...],
        preferred_element_type=jnp.float32,
    )
    for g, (r, w) in enumerate(groups):
        out_ref[r, :, w * WIN : (w + 1) * WIN] = restored[block(g)].astype(out_ref.dtype)


def coherence(gathers, limits, tables):
    forward, inverse, mix_forward, mix_inverse = tables
    receivers, sources, samples = gathers.shape
    vmem = pl.BlockSpec(memory_space=pltpu.VMEM)
    return pl.pallas_call(
        filter_kernel,
        in_specs=[vmem] * 8,
        out_specs=vmem,
        out_shape=jax.ShapeDtypeStruct(gathers.shape, jnp.bfloat16),
        compiler_params=pltpu.CompilerParams(vmem_limit_bytes=48 * 1024 * 1024),
    )(gathers, forward, inverse, *mix_forward, *mix_inverse, limits.reshape(sources, 1))


def local(blended, delays, thresholds):
    tables = filter_tables()
    records = lax.all_to_all(blended, "shot", split_axis=0, concat_axis=1, tiled=True)
    estimate = None
    for sweep in range(ITERS):
        if sweep == 0:
            residual = records.astype(jnp.bfloat16)
            update = (RELAX * spread(residual, delays)).astype(jnp.bfloat16)
        else:
            residual = (records - blend(estimate, delays)).astype(jnp.bfloat16)
            update = (estimate.astype(jnp.float32) + RELAX * spread(residual, delays)).astype(
                jnp.bfloat16
            )
        estimate = coherence(update, thresholds[sweep], tables).astype(jnp.bfloat16)
    return lax.all_to_all(estimate, "shot", split_axis=1, concat_axis=0, tiled=True)


def solution(mesh):
    return jax.shard_map(
        local,
        mesh=mesh,
        in_specs=(P(None, "shot", "tm"), P(), P()),
        out_specs=P(None, "shot", "tm"),
        check_vma=False,
    )
```

```python
import math

import jax
import ml_dtypes
import numpy as np
import jax.numpy as jnp
from jax import lax
from jax.experimental import pallas as pl
from jax.experimental.pallas import tpu as pltpu
from jax.sharding import PartitionSpec as P

SRC = 64
SRC_EXP = 2
WIN = 256
BLK = 128
ITERS = 2


RELAX = 0.5


def shifted(array, axis, by):
    count = lax.axis_size(axis)
    pairs = [(i, i + by) for i in range(count) if 0 <= i + by < count]
    return lax.ppermute(array, axis, pairs)


def phase_table(length_first, length_second, period):
    first_index = jnp.arange(length_first, dtype=jnp.int32)[:, None]
    second_index = jnp.arange(length_second, dtype=jnp.int32)[None, :]
    return (first_index * second_index % period).astype(jnp.float32) * (2.0 * math.pi / period)


def make_tables():
    time_angle = phase_table(WIN, WIN, WIN)
    time_scale = 1.0 / math.sqrt(WIN)
    cos_forward = jnp.cos(time_angle).astype(jnp.bfloat16)
    sin_forward = -jnp.sin(time_angle).astype(jnp.bfloat16)
    cos_inverse = jnp.cos(time_angle) * time_scale
    sin_inverse = -jnp.sin(time_angle) * time_scale
    source_angle = phase_table(SRC, SRC, SRC)
    cos_source = jnp.cos(source_angle) / math.sqrt(SRC)
    sin_source = jnp.sin(source_angle) / math.sqrt(SRC)
    return (cos_forward, sin_forward, cos_inverse, sin_inverse, cos_source, sin_source)


def blend(estimate, own_delays):
    receivers, sources, samples = estimate.shape
    blocks = samples // BLK
    experiments = sources // SRC_EXP
    earlier = shifted(estimate[:, :, samples - BLK :], "tm", 1)
    upper = estimate.reshape(receivers, sources, blocks, BLK)
    shifts = own_delays.reshape(-1)
    row_index = jnp.arange(BLK, dtype=jnp.int32)[None, :, None]
    column_index = jnp.arange(BLK, dtype=jnp.int32)[None, None, :]
    select_same = (row_index == column_index - shifts[:, None, None]).astype(jnp.bfloat16)
    select_prior = (row_index == BLK + column_index - shifts[:, None, None]).astype(jnp.bfloat16)
    same = jnp.einsum("rsnb,sbi->rsni", upper, select_same, preferred_element_type=jnp.float32)
    onward = jnp.einsum("rsnb,sbi->rsni", upper, select_prior, preferred_element_type=jnp.float32)
    edge_part = jnp.einsum(
        "rsb,sbi->rsi", earlier, select_prior, preferred_element_type=jnp.float32
    )
    same = jnp.sum(same.reshape(receivers, experiments, SRC_EXP, blocks, BLK), axis=2)
    onward = jnp.sum(onward.reshape(receivers, experiments, SRC_EXP, blocks, BLK), axis=2)
    edge_part = jnp.sum(edge_part.reshape(receivers, experiments, SRC_EXP, BLK), axis=2)
    carried = jnp.concatenate([edge_part[:, :, None], onward[:, :, : blocks - 1]], axis=2)
    return (same + carried).reshape(receivers, experiments, samples)


def spread(residual, own_delays):
    receivers, experiments, samples = residual.shape
    blocks = samples // BLK
    later = shifted(residual[:, :, :BLK], "tm", -1)
    lower = residual.reshape(receivers, experiments, blocks, BLK)
    row_index = jnp.arange(BLK, dtype=jnp.int32)[None, None, :, None]
    column_index = jnp.arange(BLK, dtype=jnp.int32)[None, None, None, :]
    select_same = (row_index == column_index + own_delays[:, :, None, None]).astype(jnp.bfloat16)
    select_next = (row_index + BLK == column_index + own_delays[:, :, None, None]).astype(
        jnp.bfloat16
    )
    same = jnp.einsum("rena,ekai->rekni", lower, select_same, preferred_element_type=jnp.float32)
    backward = jnp.einsum(
        "rena,ekai->rekni", lower, select_next, preferred_element_type=jnp.float32
    )
    edge_part = jnp.einsum("rea,ekai->reki", later, select_next, preferred_element_type=jnp.float32)
    carried = jnp.concatenate([backward[:, :, :, 1:], edge_part[:, :, :, None]], axis=3)
    return (same + carried).reshape(receivers, experiments * SRC_EXP, samples)


def split(value):
    high = value.astype(jnp.bfloat16)
    return high, (value - high.astype(jnp.float32)).astype(jnp.bfloat16)


def exact_split(value):
    high = value.astype(ml_dtypes.bfloat16)
    low = (value - high.astype(np.float64)).astype(ml_dtypes.bfloat16)
    return jnp.asarray(high), jnp.asarray(low)


def filter_tables():
    time_angle = phase_table(WIN, WIN, WIN)
    forward = jnp.concatenate(
        [jnp.cos(time_angle).astype(jnp.bfloat16), -jnp.sin(time_angle).astype(jnp.bfloat16)],
        axis=1,
    )
    turn = lambda n: (np.arange(n)[:, None] * np.arange(n)[None, :] % n) * (2.0 * np.pi / n)
    time_turn = turn(WIN)
    inverse_high, inverse_low = exact_split(
        np.concatenate([np.cos(time_turn), -np.sin(time_turn)], axis=0) / math.sqrt(WIN)
    )
    inverse = jnp.concatenate([inverse_high, inverse_high, inverse_low], axis=0)
    source_turn = turn(SRC)
    cos_source = np.cos(source_turn) / math.sqrt(SRC)
    sin_source = np.sin(source_turn) / math.sqrt(SRC)
    mix_forward = exact_split(np.block([[cos_source, sin_source], [-sin_source, cos_source]]))
    mix_inverse = exact_split(np.block([[cos_source, -sin_source], [sin_source, cos_source]]))
    return forward, inverse, mix_forward, mix_inverse


def mix(table, value):
    table_high, table_low = table
    value_high, value_low = split(value)
    stacked = jnp.concatenate([value_high, value_low, value_high], axis=0)
    joined = jnp.concatenate([table_high, table_high, table_low], axis=1)
    return jnp.dot(joined, stacked, preferred_element_type=jnp.float32)


def filter_kernel(
    u_ref, forward_ref, inverse_ref, mfh_ref, mfl_ref, mih_ref, mil_ref, limit_ref, out_ref
):
    receivers, sources, samples = u_ref.shape
    windows = samples // WIN
    groups = [(r, w) for r in range(receivers) for w in range(windows)]
    scale = 1.0 / math.sqrt(WIN)
    rows = jnp.concatenate(
        [u_ref[r, :, w * WIN : (w + 1) * WIN] for r, w in groups], axis=0
    )
    spectrum = jnp.dot(rows, forward_ref[...], preferred_element_type=jnp.float32) * scale
    block = lambda g: slice(g * sources, (g + 1) * sources)
    field = jnp.concatenate(
        [
            jnp.concatenate([spectrum[block(g), :WIN], spectrum[block(g), WIN:]], axis=0)
            for g in range(len(groups))
        ],
        axis=1,
    )
    coeffs = mix((mfh_ref[...], mfl_ref[...]), field)
    real_part = coeffs[:sources]
    imag_part = coeffs[sources:]
    limit = limit_ref[...]
    magnitude = jnp.sqrt(real_part * real_part + imag_part * imag_part)
    factor = jnp.maximum(magnitude - limit, 0.0) / jnp.maximum(magnitude, limit)
    kept = jnp.concatenate([real_part * factor, imag_part * factor], axis=0)
    back = mix((mih_ref[...], mil_ref[...]), kept)
    lanes = lambda g: slice(g * WIN, (g + 1) * WIN)
    joined = jnp.concatenate(
        [
            jnp.concatenate([back[:sources, lanes(g)], back[sources:, lanes(g)]], axis=1)
            for g in range(len(groups))
        ],
        axis=0,
    )
    joined_high, joined_low = split(joined)
    restored = jnp.dot(
        jnp.concatenate([joined_high, joined_low, joined_high], axis=1),
        inverse_ref[...],
        preferred_element_type=jnp.float32,
    )
    for g, (r, w) in enumerate(groups):
        out_ref[r, :, w * WIN : (w + 1) * WIN] = restored[block(g)].astype(out_ref.dtype)


def coherence(gathers, limits, tables):
    forward, inverse, mix_forward, mix_inverse = tables
    receivers, sources, samples = gathers.shape
    vmem = pl.BlockSpec(memory_space=pltpu.VMEM)
    return pl.pallas_call(
        filter_kernel,
        in_specs=[vmem] * 8,
        out_specs=vmem,
        out_shape=jax.ShapeDtypeStruct(gathers.shape, jnp.bfloat16),
        compiler_params=pltpu.CompilerParams(vmem_limit_bytes=48 * 1024 * 1024),
    )(gathers, forward, inverse, *mix_forward, *mix_inverse, limits.reshape(sources, 1))


def local(blended, delays, thresholds):
    tables = filter_tables()
    records = lax.all_to_all(blended, "shot", split_axis=0, concat_axis=1, tiled=True)
    estimate = None
    for sweep in range(ITERS):
        if sweep == 0:
            residual = records.astype(jnp.bfloat16)
            update = (RELAX * spread(residual, delays)).astype(jnp.bfloat16)
        else:
            residual = (records - blend(estimate, delays)).astype(jnp.bfloat16)
            update = (estimate.astype(jnp.float32) + RELAX * spread(residual, delays)).astype(
                jnp.bfloat16
            )
        estimate = coherence(update, thresholds[sweep], tables).astype(jnp.bfloat16)
    return lax.all_to_all(estimate, "shot", split_axis=1, concat_axis=0, tiled=True)


def solution(mesh):
    return jax.shard_map(
        local,
        mesh=mesh,
        in_specs=(P(None, "shot", "tm"), P(), P()),
        out_specs=P(None, "shot", "tm"),
        check_vma=False,
    )
```

```python
import functools
import math

import jax
import ml_dtypes
import numpy as np
import jax.numpy as jnp
from jax import lax
from jax.experimental import pallas as pl
from jax.experimental.pallas import tpu as pltpu
from jax.sharding import PartitionSpec as P

SRC = 64
SRC_EXP = 2
WIN = 256
BLK = 128
ITERS = 2


RELAX = 0.5


def shifted(array, axis, by):
    count = lax.axis_size(axis)
    pairs = [(i, i + by) for i in range(count) if 0 <= i + by < count]
    return lax.ppermute(array, axis, pairs)


def phase_table(length_first, length_second, period):
    first_index = jnp.arange(length_first, dtype=jnp.int32)[:, None]
    second_index = jnp.arange(length_second, dtype=jnp.int32)[None, :]
    return (first_index * second_index % period).astype(jnp.float32) * (2.0 * math.pi / period)


def make_tables():
    time_angle = phase_table(WIN, WIN, WIN)
    time_scale = 1.0 / math.sqrt(WIN)
    cos_forward = jnp.cos(time_angle).astype(jnp.bfloat16)
    sin_forward = -jnp.sin(time_angle).astype(jnp.bfloat16)
    cos_inverse = jnp.cos(time_angle) * time_scale
    sin_inverse = -jnp.sin(time_angle) * time_scale
    source_angle = phase_table(SRC, SRC, SRC)
    cos_source = jnp.cos(source_angle) / math.sqrt(SRC)
    sin_source = jnp.sin(source_angle) / math.sqrt(SRC)
    return (cos_forward, sin_forward, cos_inverse, sin_inverse, cos_source, sin_source)


def blend(estimate, own_delays):
    receivers, sources, samples = estimate.shape
    blocks = samples // BLK
    experiments = sources // SRC_EXP
    earlier = shifted(estimate[:, :, samples - BLK :], "tm", 1)
    upper = estimate.reshape(receivers, sources, blocks, BLK)
    shifts = own_delays.reshape(-1)
    row_index = jnp.arange(BLK, dtype=jnp.int32)[None, :, None]
    column_index = jnp.arange(BLK, dtype=jnp.int32)[None, None, :]
    select_same = (row_index == column_index - shifts[:, None, None]).astype(jnp.bfloat16)
    select_prior = (row_index == BLK + column_index - shifts[:, None, None]).astype(jnp.bfloat16)
    same = jnp.einsum("rsnb,sbi->rsni", upper, select_same, preferred_element_type=jnp.float32)
    onward = jnp.einsum("rsnb,sbi->rsni", upper, select_prior, preferred_element_type=jnp.float32)
    edge_part = jnp.einsum(
        "rsb,sbi->rsi", earlier, select_prior, preferred_element_type=jnp.float32
    )
    same = jnp.sum(same.reshape(receivers, experiments, SRC_EXP, blocks, BLK), axis=2)
    onward = jnp.sum(onward.reshape(receivers, experiments, SRC_EXP, blocks, BLK), axis=2)
    edge_part = jnp.sum(edge_part.reshape(receivers, experiments, SRC_EXP, BLK), axis=2)
    carried = jnp.concatenate([edge_part[:, :, None], onward[:, :, : blocks - 1]], axis=2)
    return (same + carried).reshape(receivers, experiments, samples)


def spread(residual, own_delays):
    receivers, experiments, samples = residual.shape
    blocks = samples // BLK
    later = shifted(residual[:, :, :BLK], "tm", -1)
    lower = residual.reshape(receivers, experiments, blocks, BLK)
    row_index = jnp.arange(BLK, dtype=jnp.int32)[None, None, :, None]
    column_index = jnp.arange(BLK, dtype=jnp.int32)[None, None, None, :]
    select_same = (row_index == column_index + own_delays[:, :, None, None]).astype(jnp.bfloat16)
    select_next = (row_index + BLK == column_index + own_delays[:, :, None, None]).astype(
        jnp.bfloat16
    )
    same = jnp.einsum("rena,ekai->rekni", lower, select_same, preferred_element_type=jnp.float32)
    backward = jnp.einsum(
        "rena,ekai->rekni", lower, select_next, preferred_element_type=jnp.float32
    )
    edge_part = jnp.einsum("rea,ekai->reki", later, select_next, preferred_element_type=jnp.float32)
    carried = jnp.concatenate([backward[:, :, :, 1:], edge_part[:, :, :, None]], axis=3)
    return (same + carried).reshape(receivers, experiments * SRC_EXP, samples)


def split(value):
    high = value.astype(jnp.bfloat16)
    return high, (value - high.astype(jnp.float32)).astype(jnp.bfloat16)


def exact_split(value):
    high = value.astype(ml_dtypes.bfloat16)
    low = (value - high.astype(np.float64)).astype(ml_dtypes.bfloat16)
    return jnp.asarray(high), jnp.asarray(low)


def filter_tables():
    time_angle = phase_table(WIN, WIN, WIN)
    forward = jnp.concatenate(
        [jnp.cos(time_angle).astype(jnp.bfloat16), -jnp.sin(time_angle).astype(jnp.bfloat16)],
        axis=1,
    )
    turn = lambda n: (np.arange(n)[:, None] * np.arange(n)[None, :] % n) * (2.0 * np.pi / n)
    time_turn = turn(WIN)
    inverse_high, inverse_low = exact_split(
        np.concatenate([np.cos(time_turn), -np.sin(time_turn)], axis=0) / math.sqrt(WIN)
    )
    inverse = jnp.concatenate([inverse_high, inverse_high, inverse_low], axis=0)
    source_turn = turn(SRC)
    cos_source = np.cos(source_turn) / math.sqrt(SRC)
    sin_source = np.sin(source_turn) / math.sqrt(SRC)
    mix_forward = exact_split(np.block([[cos_source, sin_source], [-sin_source, cos_source]]))
    mix_inverse = exact_split(np.block([[cos_source, -sin_source], [sin_source, cos_source]]))
    return forward, inverse, mix_forward, mix_inverse


def mix(table, value):
    table_high, table_low = table
    value_high, value_low = split(value)
    stacked = jnp.concatenate([value_high, value_low, value_high], axis=0)
    joined = jnp.concatenate([table_high, table_high, table_low], axis=1)
    return jnp.dot(joined, stacked, preferred_element_type=jnp.float32)


def filter_kernel(
    u_ref, forward_ref, inverse_ref, mfh_ref, mfl_ref, mih_ref, mil_ref, limit_ref, out_ref
):
    receivers, sources, samples = u_ref.shape
    windows = samples // WIN
    groups = [(r, w) for r in range(receivers) for w in range(windows)]
    scale = 1.0 / math.sqrt(WIN)
    rows = jnp.concatenate(
        [u_ref[r, :, w * WIN : (w + 1) * WIN] for r, w in groups], axis=0
    )
    spectrum = jnp.dot(rows, forward_ref[...], preferred_element_type=jnp.float32) * scale
    block = lambda g: slice(g * sources, (g + 1) * sources)
    field = jnp.concatenate(
        [
            jnp.concatenate([spectrum[block(g), :WIN], spectrum[block(g), WIN:]], axis=0)
            for g in range(len(groups))
        ],
        axis=1,
    )
    coeffs = mix((mfh_ref[...], mfl_ref[...]), field)
    real_part = coeffs[:sources]
    imag_part = coeffs[sources:]
    limit = limit_ref[...]
    magnitude = jnp.sqrt(real_part * real_part + imag_part * imag_part)
    factor = jnp.maximum(magnitude - limit, 0.0) / jnp.maximum(magnitude, limit)
    kept = jnp.concatenate([real_part * factor, imag_part * factor], axis=0)
    back = mix((mih_ref[...], mil_ref[...]), kept)
    lanes = lambda g: slice(g * WIN, (g + 1) * WIN)
    joined = jnp.concatenate(
        [
            jnp.concatenate([back[:sources, lanes(g)], back[sources:, lanes(g)]], axis=1)
            for g in range(len(groups))
        ],
        axis=0,
    )
    joined_high, joined_low = split(joined)
    restored = jnp.dot(
        jnp.concatenate([joined_high, joined_low, joined_high], axis=1),
        inverse_ref[...],
        preferred_element_type=jnp.float32,
    )
    for g, (r, w) in enumerate(groups):
        out_ref[r, :, w * WIN : (w + 1) * WIN] = restored[block(g)].astype(out_ref.dtype)


def coherence(gathers, limits, tables):
    forward, inverse, mix_forward, mix_inverse = tables
    receivers, sources, samples = gathers.shape
    vmem = pl.BlockSpec(memory_space=pltpu.VMEM)
    return pl.pallas_call(
        filter_kernel,
        in_specs=[vmem] * 8,
        out_specs=vmem,
        out_shape=jax.ShapeDtypeStruct(gathers.shape, jnp.bfloat16),
        compiler_params=pltpu.CompilerParams(vmem_limit_bytes=48 * 1024 * 1024),
    )(gathers, forward, inverse, *mix_forward, *mix_inverse, limits.reshape(sources, 1))


def exchange_kernel(count, outgoing, incoming, src_ref, out_ref, send_sem, recv_sem, own_sem):
    me = lax.axis_index("shot")
    row = lax.axis_index("tm")
    barrier = pltpu.get_barrier_semaphore()

    def greet(step, carry):
        peer = lax.rem(me + step, count)
        pl.semaphore_signal(barrier, 1, device_id=(peer, row), device_id_type=pl.DeviceIdType.MESH)
        return carry

    lax.fori_loop(1, count, greet, 0)
    pl.semaphore_wait(barrier, count - 1)
    own = pltpu.make_async_copy(src_ref.at[outgoing(me)], out_ref.at[incoming(me)], own_sem)
    own.start()

    def remote(peer, sender):
        return pltpu.make_async_remote_copy(
            src_ref=src_ref.at[outgoing(peer)],
            dst_ref=out_ref.at[incoming(sender)],
            send_sem=send_sem.at[peer],
            recv_sem=recv_sem.at[sender],
            device_id=(peer, row),
            device_id_type=pl.DeviceIdType.MESH,
        )

    def send(step, carry):
        remote(lax.rem(me + step, count), me).start()
        return carry

    lax.fori_loop(1, count, send, 0)

    def finish(step, carry):
        peer = lax.rem(me + step, count)
        remote(peer, me).wait_send()
        remote(me, peer).wait_recv()
        return carry

    lax.fori_loop(1, count, finish, 0)
    own.wait()


def exchange(value, out_shape, outgoing, incoming):
    count = lax.axis_size("shot")
    anywhere = pl.BlockSpec(memory_space=pl.ANY)
    return pl.pallas_call(
        functools.partial(exchange_kernel, count, outgoing, incoming),
        in_specs=[anywhere],
        out_specs=anywhere,
        out_shape=jax.ShapeDtypeStruct(out_shape, value.dtype),
        scratch_shapes=[
            pltpu.SemaphoreType.DMA((count,)),
            pltpu.SemaphoreType.DMA((count,)),
            pltpu.SemaphoreType.DMA,
        ],
        compiler_params=pltpu.CompilerParams(collective_id=0, has_side_effects=True),
    )(value)


def to_sources(estimate):
    receivers, sources, samples = estimate.shape
    count = lax.axis_size("shot")
    own = sources // count
    return exchange(
        estimate,
        (receivers * count, own, samples),
        lambda peer: (slice(None), pl.ds(peer * own, own), slice(None)),
        lambda sender: (pl.ds(sender * receivers, receivers), slice(None), slice(None)),
    )


def local(blended, delays, thresholds):
    tables = filter_tables()
    records = lax.all_to_all(blended, "shot", split_axis=0, concat_axis=1, tiled=True)
    estimate = None
    for sweep in range(ITERS):
        if sweep == 0:
            residual = records.astype(jnp.bfloat16)
            update = (RELAX * spread(residual, delays)).astype(jnp.bfloat16)
        else:
            residual = (records - blend(estimate, delays)).astype(jnp.bfloat16)
            update = (estimate.astype(jnp.float32) + RELAX * spread(residual, delays)).astype(
                jnp.bfloat16
            )
        estimate = coherence(update, thresholds[sweep], tables)
    return to_sources(estimate)


def solution(mesh):
    return jax.shard_map(
        local,
        mesh=mesh,
        in_specs=(P(None, "shot", "tm"), P(), P()),
        out_specs=P(None, "shot", "tm"),
        check_vma=False,
    )
```

```python
import functools
import math

import jax
import ml_dtypes
import numpy as np
import jax.numpy as jnp
from jax import lax
from jax.experimental import pallas as pl
from jax.experimental.pallas import tpu as pltpu
from jax.sharding import PartitionSpec as P

SRC = 64
SRC_EXP = 2
WIN = 256
BLK = 128
ITERS = 2


RELAX = 0.5


def shifted(array, axis, by):
    count = lax.axis_size(axis)
    pairs = [(i, i + by) for i in range(count) if 0 <= i + by < count]
    return lax.ppermute(array, axis, pairs)


def phase_table(length_first, length_second, period):
    first_index = jnp.arange(length_first, dtype=jnp.int32)[:, None]
    second_index = jnp.arange(length_second, dtype=jnp.int32)[None, :]
    return (first_index * second_index % period).astype(jnp.float32) * (2.0 * math.pi / period)


def make_tables():
    time_angle = phase_table(WIN, WIN, WIN)
    time_scale = 1.0 / math.sqrt(WIN)
    cos_forward = jnp.cos(time_angle).astype(jnp.bfloat16)
    sin_forward = -jnp.sin(time_angle).astype(jnp.bfloat16)
    cos_inverse = jnp.cos(time_angle) * time_scale
    sin_inverse = -jnp.sin(time_angle) * time_scale
    source_angle = phase_table(SRC, SRC, SRC)
    cos_source = jnp.cos(source_angle) / math.sqrt(SRC)
    sin_source = jnp.sin(source_angle) / math.sqrt(SRC)
    return (cos_forward, sin_forward, cos_inverse, sin_inverse, cos_source, sin_source)


def blend(estimate, own_delays):
    receivers, sources, samples = estimate.shape
    blocks = samples // BLK
    experiments = sources // SRC_EXP
    earlier = shifted(estimate[:, :, samples - BLK :], "tm", 1)
    upper = estimate.reshape(receivers, sources, blocks, BLK)
    shifts = own_delays.reshape(-1)
    row_index = jnp.arange(BLK, dtype=jnp.int32)[None, :, None]
    column_index = jnp.arange(BLK, dtype=jnp.int32)[None, None, :]
    select_same = (row_index == column_index - shifts[:, None, None]).astype(jnp.bfloat16)
    select_prior = (row_index == BLK + column_index - shifts[:, None, None]).astype(jnp.bfloat16)
    same = jnp.einsum("rsnb,sbi->rsni", upper, select_same, preferred_element_type=jnp.float32)
    onward = jnp.einsum("rsnb,sbi->rsni", upper, select_prior, preferred_element_type=jnp.float32)
    edge_part = jnp.einsum(
        "rsb,sbi->rsi", earlier, select_prior, preferred_element_type=jnp.float32
    )
    same = jnp.sum(same.reshape(receivers, experiments, SRC_EXP, blocks, BLK), axis=2)
    onward = jnp.sum(onward.reshape(receivers, experiments, SRC_EXP, blocks, BLK), axis=2)
    edge_part = jnp.sum(edge_part.reshape(receivers, experiments, SRC_EXP, BLK), axis=2)
    carried = jnp.concatenate([edge_part[:, :, None], onward[:, :, : blocks - 1]], axis=2)
    return (same + carried).reshape(receivers, experiments, samples)


def spread(residual, own_delays):
    receivers, experiments, samples = residual.shape
    blocks = samples // BLK
    later = shifted(residual[:, :, :BLK], "tm", -1)
    lower = residual.reshape(receivers, experiments, blocks, BLK)
    row_index = jnp.arange(BLK, dtype=jnp.int32)[None, None, :, None]
    column_index = jnp.arange(BLK, dtype=jnp.int32)[None, None, None, :]
    select_same = (row_index == column_index + own_delays[:, :, None, None]).astype(jnp.bfloat16)
    select_next = (row_index + BLK == column_index + own_delays[:, :, None, None]).astype(
        jnp.bfloat16
    )
    same = jnp.einsum("rena,ekai->rekni", lower, select_same, preferred_element_type=jnp.float32)
    backward = jnp.einsum(
        "rena,ekai->rekni", lower, select_next, preferred_element_type=jnp.float32
    )
    edge_part = jnp.einsum("rea,ekai->reki", later, select_next, preferred_element_type=jnp.float32)
    carried = jnp.concatenate([backward[:, :, :, 1:], edge_part[:, :, :, None]], axis=3)
    return (same + carried).reshape(receivers, experiments * SRC_EXP, samples)


def split(value):
    high = value.astype(jnp.bfloat16)
    return high, (value - high.astype(jnp.float32)).astype(jnp.bfloat16)


def exact_split(value):
    high = value.astype(ml_dtypes.bfloat16)
    low = (value - high.astype(np.float64)).astype(ml_dtypes.bfloat16)
    return jnp.asarray(high), jnp.asarray(low)


def filter_tables():
    time_angle = phase_table(WIN, WIN, WIN)
    forward = jnp.concatenate(
        [jnp.cos(time_angle).astype(jnp.bfloat16), -jnp.sin(time_angle).astype(jnp.bfloat16)],
        axis=1,
    )
    turn = lambda n: (np.arange(n)[:, None] * np.arange(n)[None, :] % n) * (2.0 * np.pi / n)
    time_turn = turn(WIN)
    inverse_high, inverse_low = exact_split(
        np.concatenate([np.cos(time_turn), -np.sin(time_turn)], axis=0) / math.sqrt(WIN)
    )
    inverse = jnp.concatenate([inverse_high, inverse_high, inverse_low], axis=0)
    source_turn = turn(SRC)
    cos_source = np.cos(source_turn) / math.sqrt(SRC)
    sin_source = np.sin(source_turn) / math.sqrt(SRC)
    mix_forward = exact_split(np.block([[cos_source, sin_source], [-sin_source, cos_source]]))
    mix_inverse = exact_split(np.block([[cos_source, -sin_source], [sin_source, cos_source]]))
    return forward, inverse, mix_forward, mix_inverse


def mix(table, value):
    table_high, table_low = table
    value_high, value_low = split(value)
    stacked = jnp.concatenate([value_high, value_low, value_high], axis=0)
    joined = jnp.concatenate([table_high, table_high, table_low], axis=1)
    return jnp.dot(joined, stacked, preferred_element_type=jnp.float32)


def filter_kernel(
    u_ref, forward_ref, inverse_ref, mfh_ref, mfl_ref, mih_ref, mil_ref, limit_ref, out_ref
):
    receivers, sources, samples = u_ref.shape
    windows = samples // WIN
    groups = [(r, w) for r in range(receivers) for w in range(windows)]
    scale = 1.0 / math.sqrt(WIN)
    rows = jnp.concatenate(
        [u_ref[r, :, w * WIN : (w + 1) * WIN] for r, w in groups], axis=0
    )
    spectrum = jnp.dot(rows, forward_ref[...], preferred_element_type=jnp.float32) * scale
    block = lambda g: slice(g * sources, (g + 1) * sources)
    field = jnp.concatenate(
        [
            jnp.concatenate([spectrum[block(g), :WIN], spectrum[block(g), WIN:]], axis=0)
            for g in range(len(groups))
        ],
        axis=1,
    )
    coeffs = mix((mfh_ref[...], mfl_ref[...]), field)
    real_part = coeffs[:sources]
    imag_part = coeffs[sources:]
    limit = limit_ref[...]
    magnitude = jnp.sqrt(real_part * real_part + imag_part * imag_part)
    factor = jnp.maximum(magnitude - limit, 0.0) / jnp.maximum(magnitude, limit)
    kept = jnp.concatenate([real_part * factor, imag_part * factor], axis=0)
    back = mix((mih_ref[...], mil_ref[...]), kept)
    lanes = lambda g: slice(g * WIN, (g + 1) * WIN)
    joined = jnp.concatenate(
        [
            jnp.concatenate([back[:sources, lanes(g)], back[sources:, lanes(g)]], axis=1)
            for g in range(len(groups))
        ],
        axis=0,
    )
    joined_high, joined_low = split(joined)
    restored = jnp.dot(
        jnp.concatenate([joined_high, joined_low, joined_high], axis=1),
        inverse_ref[...],
        preferred_element_type=jnp.float32,
    )
    for g, (r, w) in enumerate(groups):
        out_ref[r, :, w * WIN : (w + 1) * WIN] = restored[block(g)].astype(out_ref.dtype)


def coherence(gathers, limits, tables):
    forward, inverse, mix_forward, mix_inverse = tables
    receivers, sources, samples = gathers.shape
    vmem = pl.BlockSpec(memory_space=pltpu.VMEM)
    return pl.pallas_call(
        filter_kernel,
        in_specs=[vmem] * 8,
        out_specs=vmem,
        out_shape=jax.ShapeDtypeStruct(gathers.shape, jnp.bfloat16),
        compiler_params=pltpu.CompilerParams(vmem_limit_bytes=48 * 1024 * 1024),
    )(gathers, forward, inverse, *mix_forward, *mix_inverse, limits.reshape(sources, 1))


def exchange_kernel(count, outgoing, incoming, src_ref, out_ref, send_sem, recv_sem, own_sem):
    me = lax.axis_index("shot")
    row = lax.axis_index("tm")
    barrier = pltpu.get_barrier_semaphore()

    def greet(step, carry):
        peer = lax.rem(me + step, count)
        pl.semaphore_signal(barrier, 1, device_id=(peer, row), device_id_type=pl.DeviceIdType.MESH)
        return carry

    lax.fori_loop(1, count, greet, 0)
    pl.semaphore_wait(barrier, count - 1)
    own = pltpu.make_async_copy(src_ref.at[outgoing(me)], out_ref.at[incoming(me)], own_sem)
    own.start()

    def remote(peer, sender):
        return pltpu.make_async_remote_copy(
            src_ref=src_ref.at[outgoing(peer)],
            dst_ref=out_ref.at[incoming(sender)],
            send_sem=send_sem.at[peer],
            recv_sem=recv_sem.at[sender],
            device_id=(peer, row),
            device_id_type=pl.DeviceIdType.MESH,
        )

    def send(step, carry):
        remote(lax.rem(me + step, count), me).start()
        return carry

    lax.fori_loop(1, count, send, 0)

    def finish(step, carry):
        peer = lax.rem(me + step, count)
        remote(peer, me).wait_send()
        remote(me, peer).wait_recv()
        return carry

    lax.fori_loop(1, count, finish, 0)
    own.wait()


def exchange(value, out_shape, outgoing, incoming, tag):
    count = lax.axis_size("shot")
    anywhere = pl.BlockSpec(memory_space=pl.ANY)
    return pl.pallas_call(
        functools.partial(exchange_kernel, count, outgoing, incoming),
        in_specs=[anywhere],
        out_specs=anywhere,
        out_shape=jax.ShapeDtypeStruct(out_shape, value.dtype),
        scratch_shapes=[
            pltpu.SemaphoreType.DMA((count,)),
            pltpu.SemaphoreType.DMA((count,)),
            pltpu.SemaphoreType.DMA,
        ],
        compiler_params=pltpu.CompilerParams(collective_id=tag, has_side_effects=True),
    )(value)


def to_sources(estimate):
    receivers, sources, samples = estimate.shape
    count = lax.axis_size("shot")
    own = sources // count
    return exchange(
        estimate,
        (receivers * count, own, samples),
        lambda peer: (slice(None), pl.ds(peer * own, own), slice(None)),
        lambda sender: (pl.ds(sender * receivers, receivers), slice(None), slice(None)),
        0,
    )


def to_receivers(records):
    receivers, own, samples = records.shape
    count = lax.axis_size("shot")
    part = receivers // count
    return exchange(
        records,
        (part, own * count, samples),
        lambda peer: (pl.ds(peer * part, part), slice(None), slice(None)),
        lambda sender: (slice(None), pl.ds(sender * own, own), slice(None)),
        1,
    )


def local(blended, delays, thresholds):
    tables = filter_tables()
    records = to_receivers(blended)
    estimate = None
    for sweep in range(ITERS):
        if sweep == 0:
            residual = records.astype(jnp.bfloat16)
            update = (RELAX * spread(residual, delays)).astype(jnp.bfloat16)
        else:
            residual = (records - blend(estimate, delays)).astype(jnp.bfloat16)
            update = (estimate.astype(jnp.float32) + RELAX * spread(residual, delays)).astype(
                jnp.bfloat16
            )
        estimate = coherence(update, thresholds[sweep], tables)
    return to_sources(estimate)


def solution(mesh):
    return jax.shard_map(
        local,
        mesh=mesh,
        in_specs=(P(None, "shot", "tm"), P(), P()),
        out_specs=P(None, "shot", "tm"),
        check_vma=False,
    )
```

```python
import functools
import math

import jax
import ml_dtypes
import numpy as np
import jax.numpy as jnp
from jax import lax
from jax.experimental import pallas as pl
from jax.experimental.pallas import tpu as pltpu
from jax.sharding import PartitionSpec as P

SRC = 64
SRC_EXP = 2
WIN = 256
BLK = 128
ITERS = 2


RELAX = 0.5


def shifted(array, axis, by):
    count = lax.axis_size(axis)
    pairs = [(i, i + by) for i in range(count) if 0 <= i + by < count]
    return lax.ppermute(array, axis, pairs)


def phase_table(length_first, length_second, period):
    first_index = jnp.arange(length_first, dtype=jnp.int32)[:, None]
    second_index = jnp.arange(length_second, dtype=jnp.int32)[None, :]
    return (first_index * second_index % period).astype(jnp.float32) * (2.0 * math.pi / period)


def make_tables():
    time_angle = phase_table(WIN, WIN, WIN)
    time_scale = 1.0 / math.sqrt(WIN)
    cos_forward = jnp.cos(time_angle).astype(jnp.bfloat16)
    sin_forward = -jnp.sin(time_angle).astype(jnp.bfloat16)
    cos_inverse = jnp.cos(time_angle) * time_scale
    sin_inverse = -jnp.sin(time_angle) * time_scale
    source_angle = phase_table(SRC, SRC, SRC)
    cos_source = jnp.cos(source_angle) / math.sqrt(SRC)
    sin_source = jnp.sin(source_angle) / math.sqrt(SRC)
    return (cos_forward, sin_forward, cos_inverse, sin_inverse, cos_source, sin_source)


def blend(estimate, earlier, own_delays):
    receivers, sources, samples = estimate.shape
    blocks = samples // BLK
    experiments = sources // SRC_EXP
    upper = estimate.reshape(receivers, sources, blocks, BLK)
    shifts = own_delays.reshape(-1)
    row_index = jnp.arange(BLK, dtype=jnp.int32)[None, :, None]
    column_index = jnp.arange(BLK, dtype=jnp.int32)[None, None, :]
    select_same = (row_index == column_index - shifts[:, None, None]).astype(jnp.bfloat16)
    select_prior = (row_index == BLK + column_index - shifts[:, None, None]).astype(jnp.bfloat16)
    same = jnp.einsum("rsnb,sbi->rsni", upper, select_same, preferred_element_type=jnp.float32)
    onward = jnp.einsum("rsnb,sbi->rsni", upper, select_prior, preferred_element_type=jnp.float32)
    edge_part = jnp.einsum(
        "rsb,sbi->rsi", earlier, select_prior, preferred_element_type=jnp.float32
    )
    same = jnp.sum(same.reshape(receivers, experiments, SRC_EXP, blocks, BLK), axis=2)
    onward = jnp.sum(onward.reshape(receivers, experiments, SRC_EXP, blocks, BLK), axis=2)
    edge_part = jnp.sum(edge_part.reshape(receivers, experiments, SRC_EXP, BLK), axis=2)
    carried = jnp.concatenate([edge_part[:, :, None], onward[:, :, : blocks - 1]], axis=2)
    return (same + carried).reshape(receivers, experiments, samples)


def spread(residual, later, own_delays):
    receivers, experiments, samples = residual.shape
    blocks = samples // BLK
    lower = residual.reshape(receivers, experiments, blocks, BLK)
    row_index = jnp.arange(BLK, dtype=jnp.int32)[None, None, :, None]
    column_index = jnp.arange(BLK, dtype=jnp.int32)[None, None, None, :]
    select_same = (row_index == column_index + own_delays[:, :, None, None]).astype(jnp.bfloat16)
    select_next = (row_index + BLK == column_index + own_delays[:, :, None, None]).astype(
        jnp.bfloat16
    )
    same = jnp.einsum("rena,ekai->rekni", lower, select_same, preferred_element_type=jnp.float32)
    backward = jnp.einsum(
        "rena,ekai->rekni", lower, select_next, preferred_element_type=jnp.float32
    )
    edge_part = jnp.einsum("rea,ekai->reki", later, select_next, preferred_element_type=jnp.float32)
    carried = jnp.concatenate([backward[:, :, :, 1:], edge_part[:, :, :, None]], axis=3)
    return (same + carried).reshape(receivers, experiments * SRC_EXP, samples)


def split(value):
    high = value.astype(jnp.bfloat16)
    return high, (value - high.astype(jnp.float32)).astype(jnp.bfloat16)


def exact_split(value):
    high = value.astype(ml_dtypes.bfloat16)
    low = (value - high.astype(np.float64)).astype(ml_dtypes.bfloat16)
    return jnp.asarray(high), jnp.asarray(low)


def filter_tables():
    turn = lambda n: (np.arange(n)[:, None] * np.arange(n)[None, :] % n) * (2.0 * np.pi / n)
    time_turn = turn(WIN)
    forward = jnp.asarray(
        np.concatenate([np.cos(time_turn), -np.sin(time_turn)], axis=1).astype(ml_dtypes.bfloat16)
    )
    inverse_high, inverse_low = exact_split(
        np.concatenate([np.cos(time_turn), -np.sin(time_turn)], axis=0) / math.sqrt(WIN)
    )
    inverse = jnp.concatenate([inverse_high, inverse_high, inverse_low], axis=0)
    source_turn = turn(SRC)
    cos_source = np.cos(source_turn) / math.sqrt(SRC)
    sin_source = np.sin(source_turn) / math.sqrt(SRC)
    mix_forward = exact_split(np.block([[cos_source, sin_source], [-sin_source, cos_source]]))
    mix_inverse = exact_split(np.block([[cos_source, -sin_source], [sin_source, cos_source]]))
    return forward, inverse, mix_forward, mix_inverse


def mix(table, value):
    table_high, table_low = table
    value_high, value_low = split(value)
    stacked = jnp.concatenate([value_high, value_low, value_high], axis=0)
    joined = jnp.concatenate([table_high, table_high, table_low], axis=1)
    return jnp.dot(joined, stacked, preferred_element_type=jnp.float32)


def filter_kernel(
    u_ref, forward_ref, inverse_ref, mfh_ref, mfl_ref, mih_ref, mil_ref, limit_ref, out_ref
):
    receivers, sources, samples = u_ref.shape
    windows = samples // WIN
    groups = [(r, w) for r in range(receivers) for w in range(windows)]
    scale = 1.0 / math.sqrt(WIN)
    rows = jnp.concatenate(
        [u_ref[r, :, w * WIN : (w + 1) * WIN] for r, w in groups], axis=0
    )
    spectrum = jnp.dot(rows, forward_ref[...], preferred_element_type=jnp.float32) * scale
    block = lambda g: slice(g * sources, (g + 1) * sources)
    field = jnp.concatenate(
        [
            jnp.concatenate([spectrum[block(g), :WIN], spectrum[block(g), WIN:]], axis=0)
            for g in range(len(groups))
        ],
        axis=1,
    )
    coeffs = mix((mfh_ref[...], mfl_ref[...]), field)
    real_part = coeffs[:sources]
    imag_part = coeffs[sources:]
    limit = limit_ref[...]
    magnitude = jnp.sqrt(real_part * real_part + imag_part * imag_part)
    factor = jnp.maximum(magnitude - limit, 0.0) / jnp.maximum(magnitude, limit)
    kept = jnp.concatenate([real_part * factor, imag_part * factor], axis=0)
    back = mix((mih_ref[...], mil_ref[...]), kept)
    lanes = lambda g: slice(g * WIN, (g + 1) * WIN)
    joined = jnp.concatenate(
        [
            jnp.concatenate([back[:sources, lanes(g)], back[sources:, lanes(g)]], axis=1)
            for g in range(len(groups))
        ],
        axis=0,
    )
    joined_high, joined_low = split(joined)
    restored = jnp.dot(
        jnp.concatenate([joined_high, joined_low, joined_high], axis=1),
        inverse_ref[...],
        preferred_element_type=jnp.float32,
    )
    for g, (r, w) in enumerate(groups):
        out_ref[r, :, w * WIN : (w + 1) * WIN] = restored[block(g)].astype(out_ref.dtype)


def coherence(gathers, limits, tables):
    forward, inverse, mix_forward, mix_inverse = tables
    receivers, sources, samples = gathers.shape
    vmem = pl.BlockSpec(memory_space=pltpu.VMEM)
    return pl.pallas_call(
        filter_kernel,
        in_specs=[vmem] * 8,
        out_specs=vmem,
        out_shape=jax.ShapeDtypeStruct(gathers.shape, jnp.bfloat16),
        compiler_params=pltpu.CompilerParams(vmem_limit_bytes=48 * 1024 * 1024),
    )(gathers, forward, inverse, *mix_forward, *mix_inverse, limits.reshape(sources, 1))


def exchange_kernel(count, outgoing, incoming, src_ref, out_ref, send_sem, recv_sem, own_sem):
    me = lax.axis_index("shot")
    row = lax.axis_index("tm")
    barrier = pltpu.get_barrier_semaphore()

    def greet(step, carry):
        peer = lax.rem(me + step, count)
        pl.semaphore_signal(barrier, 1, device_id=(peer, row), device_id_type=pl.DeviceIdType.MESH)
        return carry

    lax.fori_loop(1, count, greet, 0)
    pl.semaphore_wait(barrier, count - 1)
    own = pltpu.make_async_copy(src_ref.at[outgoing(me)], out_ref.at[incoming(me)], own_sem)
    own.start()

    def remote(peer, sender):
        return pltpu.make_async_remote_copy(
            src_ref=src_ref.at[outgoing(peer)],
            dst_ref=out_ref.at[incoming(sender)],
            send_sem=send_sem.at[peer],
            recv_sem=recv_sem.at[sender],
            device_id=(peer, row),
            device_id_type=pl.DeviceIdType.MESH,
        )

    def send(step, carry):
        remote(lax.rem(me + step, count), me).start()
        return carry

    lax.fori_loop(1, count, send, 0)

    def finish(step, carry):
        peer = lax.rem(me + step, count)
        remote(peer, me).wait_send()
        remote(me, peer).wait_recv()
        return carry

    lax.fori_loop(1, count, finish, 0)
    own.wait()


def exchange(value, out_shape, outgoing, incoming, tag):
    count = lax.axis_size("shot")
    anywhere = pl.BlockSpec(memory_space=pl.ANY)
    return pl.pallas_call(
        functools.partial(exchange_kernel, count, outgoing, incoming),
        in_specs=[anywhere],
        out_specs=anywhere,
        out_shape=jax.ShapeDtypeStruct(out_shape, value.dtype),
        scratch_shapes=[
            pltpu.SemaphoreType.DMA((count,)),
            pltpu.SemaphoreType.DMA((count,)),
            pltpu.SemaphoreType.DMA,
        ],
        compiler_params=pltpu.CompilerParams(collective_id=tag, has_side_effects=True),
    )(value)


def to_sources(estimate):
    receivers, sources, samples = estimate.shape
    count = lax.axis_size("shot")
    own = sources // count
    return exchange(
        estimate,
        (receivers * count, own, samples),
        lambda peer: (slice(None), pl.ds(peer * own, own), slice(None)),
        lambda sender: (pl.ds(sender * receivers, receivers), slice(None), slice(None)),
        0,
    )


def to_receivers(records):
    receivers, own, samples = records.shape
    count = lax.axis_size("shot")
    part = receivers // count
    return exchange(
        records,
        (part, own * count, samples),
        lambda peer: (pl.ds(peer * part, part), slice(None), slice(None)),
        lambda sender: (slice(None), pl.ds(sender * own, own), slice(None)),
        1,
    )


def local(blended, delays, thresholds):
    tables = filter_tables()
    records = to_receivers(blended)
    samples = records.shape[2]
    following = shifted(records[:, :, :BLK], "tm", -1)
    residual = records.astype(jnp.bfloat16)
    update = (RELAX * spread(residual, following.astype(jnp.bfloat16), delays)).astype(jnp.bfloat16)
    estimate = coherence(update, thresholds[0], tables)
    before = shifted(estimate[:, :, samples - BLK :], "tm", 1)
    after = shifted(estimate[:, :, :BLK], "tm", -1)
    blended_part = blend(jnp.concatenate([estimate, after], axis=2), before, delays)
    residual = (jnp.concatenate([records, following], axis=2) - blended_part).astype(jnp.bfloat16)
    last = lax.axis_index("tm") == lax.axis_size("tm") - 1
    tail = jnp.where(last, jnp.zeros_like(residual[:, :, samples:]), residual[:, :, samples:])
    update = (
        estimate.astype(jnp.float32) + RELAX * spread(residual[:, :, :samples], tail, delays)
    ).astype(jnp.bfloat16)
    estimate = coherence(update, thresholds[1], tables)
    return to_sources(estimate)


def solution(mesh):
    return jax.shard_map(
        local,
        mesh=mesh,
        in_specs=(P(None, "shot", "tm"), P(), P()),
        out_specs=P(None, "shot", "tm"),
        check_vma=False,
    )
```

```python
import functools
import math

import jax
import ml_dtypes
import numpy as np
import jax.numpy as jnp
from jax import lax
from jax.experimental import pallas as pl
from jax.experimental.pallas import tpu as pltpu
from jax.sharding import PartitionSpec as P

SRC = 64
SRC_EXP = 2
WIN = 256
BLK = 128
ITERS = 2


RELAX = 0.5


def shifted(array, axis, by):
    count = lax.axis_size(axis)
    pairs = [(i, i + by) for i in range(count) if 0 <= i + by < count]
    return lax.ppermute(array, axis, pairs)


def phase_table(length_first, length_second, period):
    first_index = jnp.arange(length_first, dtype=jnp.int32)[:, None]
    second_index = jnp.arange(length_second, dtype=jnp.int32)[None, :]
    return (first_index * second_index % period).astype(jnp.float32) * (2.0 * math.pi / period)


def make_tables():
    time_angle = phase_table(WIN, WIN, WIN)
    time_scale = 1.0 / math.sqrt(WIN)
    cos_forward = jnp.cos(time_angle).astype(jnp.bfloat16)
    sin_forward = -jnp.sin(time_angle).astype(jnp.bfloat16)
    cos_inverse = jnp.cos(time_angle) * time_scale
    sin_inverse = -jnp.sin(time_angle) * time_scale
    source_angle = phase_table(SRC, SRC, SRC)
    cos_source = jnp.cos(source_angle) / math.sqrt(SRC)
    sin_source = jnp.sin(source_angle) / math.sqrt(SRC)
    return (cos_forward, sin_forward, cos_inverse, sin_inverse, cos_source, sin_source)


def blend(estimate, own_delays):
    receivers, sources, samples = estimate.shape
    blocks = samples // BLK
    experiments = sources // SRC_EXP
    earlier = shifted(estimate[:, :, samples - BLK :], "tm", 1)
    upper = estimate.reshape(receivers, sources, blocks, BLK)
    shifts = own_delays.reshape(-1)
    row_index = jnp.arange(BLK, dtype=jnp.int32)[None, :, None]
    column_index = jnp.arange(BLK, dtype=jnp.int32)[None, None, :]
    select_same = (row_index == column_index - shifts[:, None, None]).astype(jnp.bfloat16)
    select_prior = (row_index == BLK + column_index - shifts[:, None, None]).astype(jnp.bfloat16)
    same = jnp.einsum("rsnb,sbi->rsni", upper, select_same, preferred_element_type=jnp.float32)
    onward = jnp.einsum("rsnb,sbi->rsni", upper, select_prior, preferred_element_type=jnp.float32)
    edge_part = jnp.einsum(
        "rsb,sbi->rsi", earlier, select_prior, preferred_element_type=jnp.float32
    )
    same = jnp.sum(same.reshape(receivers, experiments, SRC_EXP, blocks, BLK), axis=2)
    onward = jnp.sum(onward.reshape(receivers, experiments, SRC_EXP, blocks, BLK), axis=2)
    edge_part = jnp.sum(edge_part.reshape(receivers, experiments, SRC_EXP, BLK), axis=2)
    carried = jnp.concatenate([edge_part[:, :, None], onward[:, :, : blocks - 1]], axis=2)
    return (same + carried).reshape(receivers, experiments, samples)


def spread(residual, own_delays):
    receivers, experiments, samples = residual.shape
    blocks = samples // BLK
    later = shifted(residual[:, :, :BLK], "tm", -1)
    lower = residual.reshape(receivers, experiments, blocks, BLK)
    row_index = jnp.arange(BLK, dtype=jnp.int32)[None, None, :, None]
    column_index = jnp.arange(BLK, dtype=jnp.int32)[None, None, None, :]
    select_same = (row_index == column_index + own_delays[:, :, None, None]).astype(jnp.bfloat16)
    select_next = (row_index + BLK == column_index + own_delays[:, :, None, None]).astype(
        jnp.bfloat16
    )
    same = jnp.einsum("rena,ekai->rekni", lower, select_same, preferred_element_type=jnp.float32)
    backward = jnp.einsum(
        "rena,ekai->rekni", lower, select_next, preferred_element_type=jnp.float32
    )
    edge_part = jnp.einsum("rea,ekai->reki", later, select_next, preferred_element_type=jnp.float32)
    carried = jnp.concatenate([backward[:, :, :, 1:], edge_part[:, :, :, None]], axis=3)
    return (same + carried).reshape(receivers, experiments * SRC_EXP, samples)


def split(value):
    high = value.astype(jnp.bfloat16)
    return high, (value - high.astype(jnp.float32)).astype(jnp.bfloat16)


def exact_split(value):
    high = value.astype(ml_dtypes.bfloat16)
    low = (value - high.astype(np.float64)).astype(ml_dtypes.bfloat16)
    return jnp.asarray(high), jnp.asarray(low)


def filter_tables():
    time_angle = phase_table(WIN, WIN, WIN)
    forward = jnp.concatenate(
        [jnp.cos(time_angle).astype(jnp.bfloat16), -jnp.sin(time_angle).astype(jnp.bfloat16)],
        axis=1,
    )
    turn = lambda n: (np.arange(n)[:, None] * np.arange(n)[None, :] % n) * (2.0 * np.pi / n)
    time_turn = turn(WIN)
    inverse_high, inverse_low = exact_split(
        np.concatenate([np.cos(time_turn), -np.sin(time_turn)], axis=0) / math.sqrt(WIN)
    )
    inverse = jnp.concatenate([inverse_high, inverse_high, inverse_low], axis=0)
    source_turn = turn(SRC)
    cos_source = np.cos(source_turn) / math.sqrt(SRC)
    sin_source = np.sin(source_turn) / math.sqrt(SRC)
    mix_forward = exact_split(np.block([[cos_source, sin_source], [-sin_source, cos_source]]))
    mix_inverse = exact_split(np.block([[cos_source, -sin_source], [sin_source, cos_source]]))
    return forward, inverse, mix_forward, mix_inverse


def mix(table, value):
    table_high, table_low = table
    value_high, value_low = split(value)
    stacked = jnp.concatenate([value_high, value_low, value_high], axis=0)
    joined = jnp.concatenate([table_high, table_high, table_low], axis=1)
    return jnp.dot(joined, stacked, preferred_element_type=jnp.float32)


def filter_block(u_ref, first, count, tables, out_ref):
    forward_ref, inverse_ref, mfh_ref, mfl_ref, mih_ref, mil_ref, limit_ref = tables
    sources, samples = u_ref.shape[1:]
    windows = samples // WIN
    groups = [(r, w) for r in range(first, first + count) for w in range(windows)]
    scale = 1.0 / math.sqrt(WIN)
    rows = jnp.concatenate(
        [u_ref[r, :, w * WIN : (w + 1) * WIN] for r, w in groups], axis=0
    )
    spectrum = jnp.dot(rows, forward_ref[...], preferred_element_type=jnp.float32) * scale
    block = lambda g: slice(g * sources, (g + 1) * sources)
    field = jnp.concatenate(
        [
            jnp.concatenate([spectrum[block(g), :WIN], spectrum[block(g), WIN:]], axis=0)
            for g in range(len(groups))
        ],
        axis=1,
    )
    coeffs = mix((mfh_ref[...], mfl_ref[...]), field)
    real_part = coeffs[:sources]
    imag_part = coeffs[sources:]
    limit = limit_ref[...]
    magnitude = jnp.sqrt(real_part * real_part + imag_part * imag_part)
    factor = jnp.maximum(magnitude - limit, 0.0) / jnp.maximum(magnitude, limit)
    kept = jnp.concatenate([real_part * factor, imag_part * factor], axis=0)
    back = mix((mih_ref[...], mil_ref[...]), kept)
    lanes = lambda g: slice(g * WIN, (g + 1) * WIN)
    joined = jnp.concatenate(
        [
            jnp.concatenate([back[:sources, lanes(g)], back[sources:, lanes(g)]], axis=1)
            for g in range(len(groups))
        ],
        axis=0,
    )
    joined_high, joined_low = split(joined)
    restored = jnp.dot(
        jnp.concatenate([joined_high, joined_low, joined_high], axis=1),
        inverse_ref[...],
        preferred_element_type=jnp.float32,
    )
    for g, (r, w) in enumerate(groups):
        out_ref[r, :, w * WIN : (w + 1) * WIN] = restored[block(g)].astype(out_ref.dtype)


def filter_kernel(u_ref, *refs):
    filter_block(u_ref, 0, u_ref.shape[0], refs[:7], refs[7])


def filter_send_kernel(count, halves, u_ref, *refs):
    tables = refs[:7]
    out_ref, done_ref, send_sem, recv_sem, own_sem = refs[7:]
    receivers, sources, samples = u_ref.shape
    own = sources // count
    per = receivers // halves
    me = lax.axis_index("shot")
    row = lax.axis_index("tm")
    barrier = pltpu.get_barrier_semaphore()

    def greet(step, carry):
        peer = lax.rem(me + step, count)
        pl.semaphore_signal(barrier, 1, device_id=(peer, row), device_id_type=pl.DeviceIdType.MESH)
        return carry

    lax.fori_loop(1, count, greet, 0)

    def remote(half, peer, sender):
        return pltpu.make_async_remote_copy(
            src_ref=done_ref.at[pl.ds(half * per, per), pl.ds(peer * own, own), :],
            dst_ref=out_ref.at[pl.ds(sender * receivers + half * per, per), :, :],
            send_sem=send_sem.at[half, peer],
            recv_sem=recv_sem.at[half, sender],
            device_id=(peer, row),
            device_id_type=pl.DeviceIdType.MESH,
        )

    locals_ = []
    for half in range(halves):
        filter_block(u_ref, half * per, per, tables, done_ref)
        if half == 0:
            pl.semaphore_wait(barrier, count - 1)
        mine = pltpu.make_async_copy(
            done_ref.at[pl.ds(half * per, per), pl.ds(me * own, own), :],
            out_ref.at[pl.ds(me * receivers + half * per, per), :, :],
            own_sem.at[half],
        )
        mine.start()
        locals_.append(mine)

        def send(step, carry, half=half):
            remote(half, lax.rem(me + step, count), me).start()
            return carry

        lax.fori_loop(1, count, send, 0)

    for half in range(halves):

        def finish(step, carry, half=half):
            peer = lax.rem(me + step, count)
            remote(half, peer, me).wait_send()
            remote(half, me, peer).wait_recv()
            return carry

        lax.fori_loop(1, count, finish, 0)
        locals_[half].wait()


def filter_and_send(gathers, limits, tables):
    forward, inverse, mix_forward, mix_inverse = tables
    receivers, sources, samples = gathers.shape
    count = lax.axis_size("shot")
    halves = 2
    vmem = pl.BlockSpec(memory_space=pltpu.VMEM)
    return pl.pallas_call(
        functools.partial(filter_send_kernel, count, halves),
        in_specs=[vmem] * 8,
        out_specs=pl.BlockSpec(memory_space=pl.ANY),
        out_shape=jax.ShapeDtypeStruct(
            (receivers * count, sources // count, samples), jnp.bfloat16
        ),
        scratch_shapes=[
            pltpu.VMEM(gathers.shape, jnp.bfloat16),
            pltpu.SemaphoreType.DMA((halves, count)),
            pltpu.SemaphoreType.DMA((halves, count)),
            pltpu.SemaphoreType.DMA((halves,)),
        ],
        compiler_params=pltpu.CompilerParams(
            collective_id=2, has_side_effects=True, vmem_limit_bytes=48 * 1024 * 1024
        ),
    )(gathers, forward, inverse, *mix_forward, *mix_inverse, limits.reshape(sources, 1))


def coherence(gathers, limits, tables):
    forward, inverse, mix_forward, mix_inverse = tables
    receivers, sources, samples = gathers.shape
    vmem = pl.BlockSpec(memory_space=pltpu.VMEM)
    return pl.pallas_call(
        filter_kernel,
        in_specs=[vmem] * 8,
        out_specs=vmem,
        out_shape=jax.ShapeDtypeStruct(gathers.shape, jnp.bfloat16),
        compiler_params=pltpu.CompilerParams(vmem_limit_bytes=48 * 1024 * 1024),
    )(gathers, forward, inverse, *mix_forward, *mix_inverse, limits.reshape(sources, 1))


def exchange_kernel(count, outgoing, incoming, src_ref, out_ref, send_sem, recv_sem, own_sem):
    me = lax.axis_index("shot")
    row = lax.axis_index("tm")
    barrier = pltpu.get_barrier_semaphore()

    def greet(step, carry):
        peer = lax.rem(me + step, count)
        pl.semaphore_signal(barrier, 1, device_id=(peer, row), device_id_type=pl.DeviceIdType.MESH)
        return carry

    lax.fori_loop(1, count, greet, 0)
    pl.semaphore_wait(barrier, count - 1)
    own = pltpu.make_async_copy(src_ref.at[outgoing(me)], out_ref.at[incoming(me)], own_sem)
    own.start()

    def remote(peer, sender):
        return pltpu.make_async_remote_copy(
            src_ref=src_ref.at[outgoing(peer)],
            dst_ref=out_ref.at[incoming(sender)],
            send_sem=send_sem.at[peer],
            recv_sem=recv_sem.at[sender],
            device_id=(peer, row),
            device_id_type=pl.DeviceIdType.MESH,
        )

    def send(step, carry):
        remote(lax.rem(me + step, count), me).start()
        return carry

    lax.fori_loop(1, count, send, 0)

    def finish(step, carry):
        peer = lax.rem(me + step, count)
        remote(peer, me).wait_send()
        remote(me, peer).wait_recv()
        return carry

    lax.fori_loop(1, count, finish, 0)
    own.wait()


def exchange(value, out_shape, outgoing, incoming, tag):
    count = lax.axis_size("shot")
    anywhere = pl.BlockSpec(memory_space=pl.ANY)
    return pl.pallas_call(
        functools.partial(exchange_kernel, count, outgoing, incoming),
        in_specs=[anywhere],
        out_specs=anywhere,
        out_shape=jax.ShapeDtypeStruct(out_shape, value.dtype),
        scratch_shapes=[
            pltpu.SemaphoreType.DMA((count,)),
            pltpu.SemaphoreType.DMA((count,)),
            pltpu.SemaphoreType.DMA,
        ],
        compiler_params=pltpu.CompilerParams(collective_id=tag, has_side_effects=True),
    )(value)


def to_sources(estimate):
    receivers, sources, samples = estimate.shape
    count = lax.axis_size("shot")
    own = sources // count
    return exchange(
        estimate,
        (receivers * count, own, samples),
        lambda peer: (slice(None), pl.ds(peer * own, own), slice(None)),
        lambda sender: (pl.ds(sender * receivers, receivers), slice(None), slice(None)),
        0,
    )


def to_receivers(records):
    receivers, own, samples = records.shape
    count = lax.axis_size("shot")
    part = receivers // count
    return exchange(
        records,
        (part, own * count, samples),
        lambda peer: (pl.ds(peer * part, part), slice(None), slice(None)),
        lambda sender: (slice(None), pl.ds(sender * own, own), slice(None)),
        1,
    )


def local(blended, delays, thresholds):
    tables = filter_tables()
    records = to_receivers(blended)
    estimate = None
    for sweep in range(ITERS):
        if sweep == 0:
            residual = records.astype(jnp.bfloat16)
            update = (RELAX * spread(residual, delays)).astype(jnp.bfloat16)
        else:
            residual = (records - blend(estimate, delays)).astype(jnp.bfloat16)
            update = (estimate.astype(jnp.float32) + RELAX * spread(residual, delays)).astype(
                jnp.bfloat16
            )
        if sweep == ITERS - 1:
            return filter_and_send(update, thresholds[sweep], tables)
        estimate = coherence(update, thresholds[sweep], tables)


def solution(mesh):
    return jax.shard_map(
        local,
        mesh=mesh,
        in_specs=(P(None, "shot", "tm"), P(), P()),
        out_specs=P(None, "shot", "tm"),
        check_vma=False,
    )
```

```python
import functools
import math

import jax
import ml_dtypes
import numpy as np
import jax.numpy as jnp
from jax import lax
from jax.experimental import pallas as pl
from jax.experimental.pallas import tpu as pltpu
from jax.sharding import PartitionSpec as P

SRC = 64
SRC_EXP = 2
WIN = 256
BLK = 128
ITERS = 2


RELAX = 0.5


def shifted(array, axis, by):
    count = lax.axis_size(axis)
    pairs = [(i, i + by) for i in range(count) if 0 <= i + by < count]
    return lax.ppermute(array, axis, pairs)


def phase_table(length_first, length_second, period):
    first_index = jnp.arange(length_first, dtype=jnp.int32)[:, None]
    second_index = jnp.arange(length_second, dtype=jnp.int32)[None, :]
    return (first_index * second_index % period).astype(jnp.float32) * (2.0 * math.pi / period)


def make_tables():
    time_angle = phase_table(WIN, WIN, WIN)
    time_scale = 1.0 / math.sqrt(WIN)
    cos_forward = jnp.cos(time_angle).astype(jnp.bfloat16)
    sin_forward = -jnp.sin(time_angle).astype(jnp.bfloat16)
    cos_inverse = jnp.cos(time_angle) * time_scale
    sin_inverse = -jnp.sin(time_angle) * time_scale
    source_angle = phase_table(SRC, SRC, SRC)
    cos_source = jnp.cos(source_angle) / math.sqrt(SRC)
    sin_source = jnp.sin(source_angle) / math.sqrt(SRC)
    return (cos_forward, sin_forward, cos_inverse, sin_inverse, cos_source, sin_source)


def blend(estimate, earlier, own_delays):
    receivers, sources, samples = estimate.shape
    blocks = samples // BLK
    experiments = sources // SRC_EXP
    upper = estimate.reshape(receivers, sources, blocks, BLK)
    shifts = own_delays.reshape(-1)
    row_index = jnp.arange(BLK, dtype=jnp.int32)[None, :, None]
    column_index = jnp.arange(BLK, dtype=jnp.int32)[None, None, :]
    select_same = (row_index == column_index - shifts[:, None, None]).astype(jnp.bfloat16)
    select_prior = (row_index == BLK + column_index - shifts[:, None, None]).astype(jnp.bfloat16)
    same = jnp.einsum("rsnb,sbi->rsni", upper, select_same, preferred_element_type=jnp.float32)
    onward = jnp.einsum("rsnb,sbi->rsni", upper, select_prior, preferred_element_type=jnp.float32)
    edge_part = jnp.einsum(
        "rsb,sbi->rsi", earlier, select_prior, preferred_element_type=jnp.float32
    )
    same = jnp.sum(same.reshape(receivers, experiments, SRC_EXP, blocks, BLK), axis=2)
    onward = jnp.sum(onward.reshape(receivers, experiments, SRC_EXP, blocks, BLK), axis=2)
    edge_part = jnp.sum(edge_part.reshape(receivers, experiments, SRC_EXP, BLK), axis=2)
    carried = jnp.concatenate([edge_part[:, :, None], onward[:, :, : blocks - 1]], axis=2)
    return (same + carried).reshape(receivers, experiments, samples)


def spread(residual, later, own_delays):
    receivers, experiments, samples = residual.shape
    blocks = samples // BLK
    lower = residual.reshape(receivers, experiments, blocks, BLK)
    row_index = jnp.arange(BLK, dtype=jnp.int32)[None, None, :, None]
    column_index = jnp.arange(BLK, dtype=jnp.int32)[None, None, None, :]
    select_same = (row_index == column_index + own_delays[:, :, None, None]).astype(jnp.bfloat16)
    select_next = (row_index + BLK == column_index + own_delays[:, :, None, None]).astype(
        jnp.bfloat16
    )
    same = jnp.einsum("rena,ekai->rekni", lower, select_same, preferred_element_type=jnp.float32)
    backward = jnp.einsum(
        "rena,ekai->rekni", lower, select_next, preferred_element_type=jnp.float32
    )
    edge_part = jnp.einsum("rea,ekai->reki", later, select_next, preferred_element_type=jnp.float32)
    carried = jnp.concatenate([backward[:, :, :, 1:], edge_part[:, :, :, None]], axis=3)
    return (same + carried).reshape(receivers, experiments * SRC_EXP, samples)


def split(value):
    high = value.astype(jnp.bfloat16)
    return high, (value - high.astype(jnp.float32)).astype(jnp.bfloat16)


def exact_split(value):
    high = value.astype(ml_dtypes.bfloat16)
    low = (value - high.astype(np.float64)).astype(ml_dtypes.bfloat16)
    return jnp.asarray(high), jnp.asarray(low)


def filter_tables():
    time_angle = phase_table(WIN, WIN, WIN)
    forward = jnp.concatenate(
        [jnp.cos(time_angle).astype(jnp.bfloat16), -jnp.sin(time_angle).astype(jnp.bfloat16)],
        axis=1,
    )
    turn = lambda n: (np.arange(n)[:, None] * np.arange(n)[None, :] % n) * (2.0 * np.pi / n)
    time_turn = turn(WIN)
    inverse_high, inverse_low = exact_split(
        np.concatenate([np.cos(time_turn), -np.sin(time_turn)], axis=0) / math.sqrt(WIN)
    )
    inverse = jnp.concatenate([inverse_high, inverse_high, inverse_low], axis=0)
    source_turn = turn(SRC)
    cos_source = np.cos(source_turn) / math.sqrt(SRC)
    sin_source = np.sin(source_turn) / math.sqrt(SRC)
    mix_forward = exact_split(np.block([[cos_source, sin_source], [-sin_source, cos_source]]))
    mix_inverse = exact_split(np.block([[cos_source, -sin_source], [sin_source, cos_source]]))
    return forward, inverse, mix_forward, mix_inverse


def mix(table, value):
    table_high, table_low = table
    value_high, value_low = split(value)
    stacked = jnp.concatenate([value_high, value_low, value_high], axis=0)
    joined = jnp.concatenate([table_high, table_high, table_low], axis=1)
    return jnp.dot(joined, stacked, preferred_element_type=jnp.float32)


def filter_block(u_ref, first, count, tables, out_ref):
    forward_ref, inverse_ref, mfh_ref, mfl_ref, mih_ref, mil_ref, limit_ref = tables
    sources, samples = u_ref.shape[1:]
    windows = samples // WIN
    groups = [(r, w) for r in range(first, first + count) for w in range(windows)]
    scale = 1.0 / math.sqrt(WIN)
    rows = jnp.concatenate(
        [u_ref[r, :, w * WIN : (w + 1) * WIN] for r, w in groups], axis=0
    )
    spectrum = jnp.dot(rows, forward_ref[...], preferred_element_type=jnp.float32) * scale
    block = lambda g: slice(g * sources, (g + 1) * sources)
    field = jnp.concatenate(
        [
            jnp.concatenate([spectrum[block(g), :WIN], spectrum[block(g), WIN:]], axis=0)
            for g in range(len(groups))
        ],
        axis=1,
    )
    coeffs = mix((mfh_ref[...], mfl_ref[...]), field)
    real_part = coeffs[:sources]
    imag_part = coeffs[sources:]
    limit = limit_ref[...]
    magnitude = jnp.sqrt(real_part * real_part + imag_part * imag_part)
    factor = jnp.maximum(magnitude - limit, 0.0) / jnp.maximum(magnitude, limit)
    kept = jnp.concatenate([real_part * factor, imag_part * factor], axis=0)
    back = mix((mih_ref[...], mil_ref[...]), kept)
    lanes = lambda g: slice(g * WIN, (g + 1) * WIN)
    joined = jnp.concatenate(
        [
            jnp.concatenate([back[:sources, lanes(g)], back[sources:, lanes(g)]], axis=1)
            for g in range(len(groups))
        ],
        axis=0,
    )
    joined_high, joined_low = split(joined)
    restored = jnp.dot(
        jnp.concatenate([joined_high, joined_low, joined_high], axis=1),
        inverse_ref[...],
        preferred_element_type=jnp.float32,
    )
    for g, (r, w) in enumerate(groups):
        out_ref[r, :, w * WIN : (w + 1) * WIN] = restored[block(g)].astype(out_ref.dtype)


def filter_kernel(u_ref, *refs):
    filter_block(u_ref, 0, u_ref.shape[0], refs[:7], refs[7])


def filter_halo_kernel(stages, u_ref, *refs):
    tables = refs[:7]
    out_ref, before_ref, after_ref, send_sem, recv_sem = refs[7:]
    samples = u_ref.shape[2]
    shot = lax.axis_index("shot")
    row = lax.axis_index("tm")
    has_prev = row > 0
    has_next = row < stages - 1
    barrier = pltpu.get_barrier_semaphore()
    mesh_id = pl.DeviceIdType.MESH

    @pl.when(has_prev)
    def _():
        pl.semaphore_signal(barrier, 1, device_id=(shot, row - 1), device_id_type=mesh_id)

    @pl.when(has_next)
    def _():
        pl.semaphore_signal(barrier, 1, device_id=(shot, row + 1), device_id_type=mesh_id)

    filter_block(u_ref, 0, u_ref.shape[0], tables, out_ref)
    pl.semaphore_wait(barrier, has_prev.astype(jnp.int32) + has_next.astype(jnp.int32))

    def to_prev():
        return pltpu.make_async_remote_copy(
            src_ref=out_ref.at[:, :, pl.ds(0, BLK)],
            dst_ref=after_ref,
            send_sem=send_sem.at[0],
            recv_sem=recv_sem.at[0],
            device_id=(shot, row - 1),
            device_id_type=mesh_id,
        )

    def to_next():
        return pltpu.make_async_remote_copy(
            src_ref=out_ref.at[:, :, pl.ds(samples - BLK, BLK)],
            dst_ref=before_ref,
            send_sem=send_sem.at[1],
            recv_sem=recv_sem.at[1],
            device_id=(shot, row + 1),
            device_id_type=mesh_id,
        )

    pl.when(has_prev)(lambda: to_prev().start())
    pl.when(has_next)(lambda: to_next().start())

    @pl.when(has_prev)
    def _():
        to_prev().wait_send()
        to_next().wait_recv()

    @pl.when(has_next)
    def _():
        to_next().wait_send()
        to_prev().wait_recv()


def filter_with_halos(gathers, limits, tables):
    forward, inverse, mix_forward, mix_inverse = tables
    receivers, sources, samples = gathers.shape
    stages = lax.axis_size("tm")
    vmem = pl.BlockSpec(memory_space=pltpu.VMEM)
    anywhere = pl.BlockSpec(memory_space=pl.ANY)
    edge = jax.ShapeDtypeStruct((receivers, sources, BLK), jnp.bfloat16)
    return pl.pallas_call(
        functools.partial(filter_halo_kernel, stages),
        in_specs=[vmem] * 8,
        out_specs=(vmem, anywhere, anywhere),
        out_shape=(jax.ShapeDtypeStruct(gathers.shape, jnp.bfloat16), edge, edge),
        scratch_shapes=[pltpu.SemaphoreType.DMA((2,)), pltpu.SemaphoreType.DMA((2,))],
        compiler_params=pltpu.CompilerParams(
            collective_id=3, has_side_effects=True, vmem_limit_bytes=48 * 1024 * 1024
        ),
    )(gathers, forward, inverse, *mix_forward, *mix_inverse, limits.reshape(sources, 1))


def filter_send_kernel(count, halves, u_ref, *refs):
    tables = refs[:7]
    out_ref, done_ref, send_sem, recv_sem, own_sem = refs[7:]
    receivers, sources, samples = u_ref.shape
    own = sources // count
    per = receivers // halves
    me = lax.axis_index("shot")
    row = lax.axis_index("tm")
    barrier = pltpu.get_barrier_semaphore()

    def greet(step, carry):
        peer = lax.rem(me + step, count)
        pl.semaphore_signal(barrier, 1, device_id=(peer, row), device_id_type=pl.DeviceIdType.MESH)
        return carry

    lax.fori_loop(1, count, greet, 0)

    def remote(half, peer, sender):
        return pltpu.make_async_remote_copy(
            src_ref=done_ref.at[pl.ds(half * per, per), pl.ds(peer * own, own), :],
            dst_ref=out_ref.at[pl.ds(sender * receivers + half * per, per), :, :],
            send_sem=send_sem.at[half, peer],
            recv_sem=recv_sem.at[half, sender],
            device_id=(peer, row),
            device_id_type=pl.DeviceIdType.MESH,
        )

    locals_ = []
    for half in range(halves):
        filter_block(u_ref, half * per, per, tables, done_ref)
        if half == 0:
            pl.semaphore_wait(barrier, count - 1)
        mine = pltpu.make_async_copy(
            done_ref.at[pl.ds(half * per, per), pl.ds(me * own, own), :],
            out_ref.at[pl.ds(me * receivers + half * per, per), :, :],
            own_sem.at[half],
        )
        mine.start()
        locals_.append(mine)

        def send(step, carry, half=half):
            remote(half, lax.rem(me + step, count), me).start()
            return carry

        lax.fori_loop(1, count, send, 0)

    for half in range(halves):

        def finish(step, carry, half=half):
            peer = lax.rem(me + step, count)
            remote(half, peer, me).wait_send()
            remote(half, me, peer).wait_recv()
            return carry

        lax.fori_loop(1, count, finish, 0)
        locals_[half].wait()


def filter_and_send(gathers, limits, tables):
    forward, inverse, mix_forward, mix_inverse = tables
    receivers, sources, samples = gathers.shape
    count = lax.axis_size("shot")
    halves = 2
    vmem = pl.BlockSpec(memory_space=pltpu.VMEM)
    return pl.pallas_call(
        functools.partial(filter_send_kernel, count, halves),
        in_specs=[vmem] * 8,
        out_specs=pl.BlockSpec(memory_space=pl.ANY),
        out_shape=jax.ShapeDtypeStruct(
            (receivers * count, sources // count, samples), jnp.bfloat16
        ),
        scratch_shapes=[
            pltpu.VMEM(gathers.shape, jnp.bfloat16),
            pltpu.SemaphoreType.DMA((halves, count)),
            pltpu.SemaphoreType.DMA((halves, count)),
            pltpu.SemaphoreType.DMA((halves,)),
        ],
        compiler_params=pltpu.CompilerParams(
            collective_id=2, has_side_effects=True, vmem_limit_bytes=48 * 1024 * 1024
        ),
    )(gathers, forward, inverse, *mix_forward, *mix_inverse, limits.reshape(sources, 1))


def coherence(gathers, limits, tables):
    forward, inverse, mix_forward, mix_inverse = tables
    receivers, sources, samples = gathers.shape
    vmem = pl.BlockSpec(memory_space=pltpu.VMEM)
    return pl.pallas_call(
        filter_kernel,
        in_specs=[vmem] * 8,
        out_specs=vmem,
        out_shape=jax.ShapeDtypeStruct(gathers.shape, jnp.bfloat16),
        compiler_params=pltpu.CompilerParams(vmem_limit_bytes=48 * 1024 * 1024),
    )(gathers, forward, inverse, *mix_forward, *mix_inverse, limits.reshape(sources, 1))


def exchange_kernel(count, outgoing, incoming, src_ref, out_ref, send_sem, recv_sem, own_sem):
    me = lax.axis_index("shot")
    row = lax.axis_index("tm")
    barrier = pltpu.get_barrier_semaphore()

    def greet(step, carry):
        peer = lax.rem(me + step, count)
        pl.semaphore_signal(barrier, 1, device_id=(peer, row), device_id_type=pl.DeviceIdType.MESH)
        return carry

    lax.fori_loop(1, count, greet, 0)
    pl.semaphore_wait(barrier, count - 1)
    own = pltpu.make_async_copy(src_ref.at[outgoing(me)], out_ref.at[incoming(me)], own_sem)
    own.start()

    def remote(peer, sender):
        return pltpu.make_async_remote_copy(
            src_ref=src_ref.at[outgoing(peer)],
            dst_ref=out_ref.at[incoming(sender)],
            send_sem=send_sem.at[peer],
            recv_sem=recv_sem.at[sender],
            device_id=(peer, row),
            device_id_type=pl.DeviceIdType.MESH,
        )

    def send(step, carry):
        remote(lax.rem(me + step, count), me).start()
        return carry

    lax.fori_loop(1, count, send, 0)

    def finish(step, carry):
        peer = lax.rem(me + step, count)
        remote(peer, me).wait_send()
        remote(me, peer).wait_recv()
        return carry

    lax.fori_loop(1, count, finish, 0)
    own.wait()


def exchange(value, out_shape, outgoing, incoming, tag):
    count = lax.axis_size("shot")
    anywhere = pl.BlockSpec(memory_space=pl.ANY)
    return pl.pallas_call(
        functools.partial(exchange_kernel, count, outgoing, incoming),
        in_specs=[anywhere],
        out_specs=anywhere,
        out_shape=jax.ShapeDtypeStruct(out_shape, value.dtype),
        scratch_shapes=[
            pltpu.SemaphoreType.DMA((count,)),
            pltpu.SemaphoreType.DMA((count,)),
            pltpu.SemaphoreType.DMA,
        ],
        compiler_params=pltpu.CompilerParams(collective_id=tag, has_side_effects=True),
    )(value)


def to_sources(estimate):
    receivers, sources, samples = estimate.shape
    count = lax.axis_size("shot")
    own = sources // count
    return exchange(
        estimate,
        (receivers * count, own, samples),
        lambda peer: (slice(None), pl.ds(peer * own, own), slice(None)),
        lambda sender: (pl.ds(sender * receivers, receivers), slice(None), slice(None)),
        0,
    )


def to_receivers(records):
    receivers, own, samples = records.shape
    count = lax.axis_size("shot")
    part = receivers // count
    return exchange(
        records,
        (part, own * count, samples),
        lambda peer: (pl.ds(peer * part, part), slice(None), slice(None)),
        lambda sender: (slice(None), pl.ds(sender * own, own), slice(None)),
        1,
    )


def local(blended, delays, thresholds):
    tables = filter_tables()
    records = to_receivers(blended)
    samples = records.shape[2]
    row = lax.axis_index("tm")
    following = shifted(records[:, :, :BLK], "tm", -1)
    residual = records.astype(jnp.bfloat16)
    update = (RELAX * spread(residual, following.astype(jnp.bfloat16), delays)).astype(jnp.bfloat16)
    estimate, before, after = filter_with_halos(update, thresholds[0], tables)
    before = jnp.where(row == 0, jnp.zeros_like(before), before)
    last = row == lax.axis_size("tm") - 1
    after = jnp.where(last, jnp.zeros_like(after), after)
    blended_part = blend(jnp.concatenate([estimate, after], axis=2), before, delays)
    residual = (jnp.concatenate([records, following], axis=2) - blended_part).astype(jnp.bfloat16)
    tail = jnp.where(last, jnp.zeros_like(residual[:, :, samples:]), residual[:, :, samples:])
    update = (
        estimate.astype(jnp.float32) + RELAX * spread(residual[:, :, :samples], tail, delays)
    ).astype(jnp.bfloat16)
    return filter_and_send(update, thresholds[1], tables)


def solution(mesh):
    return jax.shard_map(
        local,
        mesh=mesh,
        in_specs=(P(None, "shot", "tm"), P(), P()),
        out_specs=P(None, "shot", "tm"),
        check_vma=False,
    )
```

```python
import functools
import math

import jax
import ml_dtypes
import numpy as np
import jax.numpy as jnp
from jax import lax
from jax.experimental import pallas as pl
from jax.experimental.pallas import tpu as pltpu
from jax.sharding import PartitionSpec as P

SRC = 64
SRC_EXP = 2
WIN = 256
BLK = 128
ITERS = 2


RELAX = 0.5


def shifted(array, axis, by):
    count = lax.axis_size(axis)
    pairs = [(i, i + by) for i in range(count) if 0 <= i + by < count]
    return lax.ppermute(array, axis, pairs)


def blend(estimate, earlier, own_delays):
    receivers, sources, samples = estimate.shape
    blocks = samples // BLK
    experiments = sources // SRC_EXP
    upper = estimate.reshape(receivers, sources, blocks, BLK)
    shifts = own_delays.reshape(-1)
    row_index = jnp.arange(BLK, dtype=jnp.int32)[None, :, None]
    column_index = jnp.arange(BLK, dtype=jnp.int32)[None, None, :]
    select_same = (row_index == column_index - shifts[:, None, None]).astype(jnp.bfloat16)
    select_prior = (row_index == BLK + column_index - shifts[:, None, None]).astype(jnp.bfloat16)
    same = jnp.einsum("rsnb,sbi->rsni", upper, select_same, preferred_element_type=jnp.float32)
    onward = jnp.einsum("rsnb,sbi->rsni", upper, select_prior, preferred_element_type=jnp.float32)
    edge_part = jnp.einsum(
        "rsb,sbi->rsi", earlier, select_prior, preferred_element_type=jnp.float32
    )
    same = jnp.sum(same.reshape(receivers, experiments, SRC_EXP, blocks, BLK), axis=2)
    onward = jnp.sum(onward.reshape(receivers, experiments, SRC_EXP, blocks, BLK), axis=2)
    edge_part = jnp.sum(edge_part.reshape(receivers, experiments, SRC_EXP, BLK), axis=2)
    carried = jnp.concatenate([edge_part[:, :, None], onward[:, :, : blocks - 1]], axis=2)
    return (same + carried).reshape(receivers, experiments, samples)


def spread(residual, later, own_delays):
    receivers, experiments, samples = residual.shape
    blocks = samples // BLK
    lower = residual.reshape(receivers, experiments, blocks, BLK)
    row_index = jnp.arange(BLK, dtype=jnp.int32)[None, None, :, None]
    column_index = jnp.arange(BLK, dtype=jnp.int32)[None, None, None, :]
    select_same = (row_index == column_index + own_delays[:, :, None, None]).astype(jnp.bfloat16)
    select_next = (row_index + BLK == column_index + own_delays[:, :, None, None]).astype(
        jnp.bfloat16
    )
    same = jnp.einsum("rena,ekai->rekni", lower, select_same, preferred_element_type=jnp.float32)
    backward = jnp.einsum(
        "rena,ekai->rekni", lower, select_next, preferred_element_type=jnp.float32
    )
    edge_part = jnp.einsum("rea,ekai->reki", later, select_next, preferred_element_type=jnp.float32)
    carried = jnp.concatenate([backward[:, :, :, 1:], edge_part[:, :, :, None]], axis=3)
    return (same + carried).reshape(receivers, experiments * SRC_EXP, samples)


def split(value):
    high = value.astype(jnp.bfloat16)
    return high, (value - high.astype(jnp.float32)).astype(jnp.bfloat16)


def exact_split(value):
    high = value.astype(ml_dtypes.bfloat16)
    low = (value - high.astype(np.float64)).astype(ml_dtypes.bfloat16)
    return jnp.asarray(high), jnp.asarray(low)


def filter_tables():
    turn = lambda n: (np.arange(n)[:, None] * np.arange(n)[None, :] % n) * (2.0 * np.pi / n)
    time_turn = turn(WIN)
    forward = jnp.asarray(
        np.concatenate([np.cos(time_turn), -np.sin(time_turn)], axis=1).astype(ml_dtypes.bfloat16)
    )
    inverse_high, inverse_low = exact_split(
        np.concatenate([np.cos(time_turn), -np.sin(time_turn)], axis=0) / math.sqrt(WIN)
    )
    inverse = jnp.concatenate([inverse_high, inverse_high, inverse_low], axis=0)
    source_turn = turn(SRC)
    cos_source = np.cos(source_turn) / math.sqrt(SRC)
    sin_source = np.sin(source_turn) / math.sqrt(SRC)
    mix_forward = exact_split(np.block([[cos_source, sin_source], [-sin_source, cos_source]]))
    mix_inverse = exact_split(np.block([[cos_source, -sin_source], [sin_source, cos_source]]))
    return forward, inverse, mix_forward, mix_inverse


def mix(table, value):
    table_high, table_low = table
    value_high, value_low = split(value)
    stacked = jnp.concatenate([value_high, value_low, value_high], axis=0)
    joined = jnp.concatenate([table_high, table_high, table_low], axis=1)
    return jnp.dot(joined, stacked, preferred_element_type=jnp.float32)


def filter_block(u_ref, first, count, tables, out_ref):
    forward_ref, inverse_ref, mfh_ref, mfl_ref, mih_ref, mil_ref, limit_ref = tables
    sources, samples = u_ref.shape[1:]
    windows = samples // WIN
    groups = [(r, w) for r in range(first, first + count) for w in range(windows)]
    scale = 1.0 / math.sqrt(WIN)
    rows = jnp.concatenate(
        [u_ref[r, :, w * WIN : (w + 1) * WIN] for r, w in groups], axis=0
    )
    spectrum = jnp.dot(rows, forward_ref[...], preferred_element_type=jnp.float32) * scale
    block = lambda g: slice(g * sources, (g + 1) * sources)
    field = jnp.concatenate(
        [
            jnp.concatenate([spectrum[block(g), :WIN], spectrum[block(g), WIN:]], axis=0)
            for g in range(len(groups))
        ],
        axis=1,
    )
    coeffs = mix((mfh_ref[...], mfl_ref[...]), field)
    real_part = coeffs[:sources]
    imag_part = coeffs[sources:]
    limit = limit_ref[...]
    magnitude = jnp.sqrt(real_part * real_part + imag_part * imag_part)
    factor = jnp.maximum(magnitude - limit, 0.0) / jnp.maximum(magnitude, limit)
    kept = jnp.concatenate([real_part * factor, imag_part * factor], axis=0)
    back = mix((mih_ref[...], mil_ref[...]), kept)
    lanes = lambda g: slice(g * WIN, (g + 1) * WIN)
    joined = jnp.concatenate(
        [
            jnp.concatenate([back[:sources, lanes(g)], back[sources:, lanes(g)]], axis=1)
            for g in range(len(groups))
        ],
        axis=0,
    )
    joined_high, joined_low = split(joined)
    restored = jnp.dot(
        jnp.concatenate([joined_high, joined_low, joined_high], axis=1),
        inverse_ref[...],
        preferred_element_type=jnp.float32,
    )
    for g, (r, w) in enumerate(groups):
        out_ref[r, :, w * WIN : (w + 1) * WIN] = restored[block(g)].astype(out_ref.dtype)


def filter_kernel(u_ref, *refs):
    filter_block(u_ref, 0, u_ref.shape[0], refs[:7], refs[7])


def filter_halo_kernel(stages, u_ref, *refs):
    tables = refs[:7]
    out_ref, before_ref, after_ref, send_sem, recv_sem = refs[7:]
    samples = u_ref.shape[2]
    shot = lax.axis_index("shot")
    row = lax.axis_index("tm")
    has_prev = row > 0
    has_next = row < stages - 1
    barrier = pltpu.get_barrier_semaphore()
    mesh_id = pl.DeviceIdType.MESH

    @pl.when(has_prev)
    def _():
        pl.semaphore_signal(barrier, 1, device_id=(shot, row - 1), device_id_type=mesh_id)

    @pl.when(has_next)
    def _():
        pl.semaphore_signal(barrier, 1, device_id=(shot, row + 1), device_id_type=mesh_id)

    filter_block(u_ref, 0, u_ref.shape[0], tables, out_ref)
    pl.semaphore_wait(barrier, has_prev.astype(jnp.int32) + has_next.astype(jnp.int32))

    def to_prev():
        return pltpu.make_async_remote_copy(
            src_ref=out_ref.at[:, :, pl.ds(0, BLK)],
            dst_ref=after_ref,
            send_sem=send_sem.at[0],
            recv_sem=recv_sem.at[0],
            device_id=(shot, row - 1),
            device_id_type=mesh_id,
        )

    def to_next():
        return pltpu.make_async_remote_copy(
            src_ref=out_ref.at[:, :, pl.ds(samples - BLK, BLK)],
            dst_ref=before_ref,
            send_sem=send_sem.at[1],
            recv_sem=recv_sem.at[1],
            device_id=(shot, row + 1),
            device_id_type=mesh_id,
        )

    pl.when(has_prev)(lambda: to_prev().start())
    pl.when(has_next)(lambda: to_next().start())

    @pl.when(has_prev)
    def _():
        to_prev().wait_send()
        to_next().wait_recv()

    @pl.when(has_next)
    def _():
        to_next().wait_send()
        to_prev().wait_recv()


def filter_with_halos(gathers, limits, tables):
    forward, inverse, mix_forward, mix_inverse = tables
    receivers, sources, samples = gathers.shape
    stages = lax.axis_size("tm")
    vmem = pl.BlockSpec(memory_space=pltpu.VMEM)
    anywhere = pl.BlockSpec(memory_space=pl.ANY)
    edge = jax.ShapeDtypeStruct((receivers, sources, BLK), jnp.bfloat16)
    return pl.pallas_call(
        functools.partial(filter_halo_kernel, stages),
        in_specs=[vmem] * 8,
        out_specs=(vmem, anywhere, anywhere),
        out_shape=(jax.ShapeDtypeStruct(gathers.shape, jnp.bfloat16), edge, edge),
        scratch_shapes=[pltpu.SemaphoreType.DMA((2,)), pltpu.SemaphoreType.DMA((2,))],
        compiler_params=pltpu.CompilerParams(
            collective_id=3, has_side_effects=True, vmem_limit_bytes=48 * 1024 * 1024
        ),
    )(gathers, forward, inverse, *mix_forward, *mix_inverse, limits.reshape(sources, 1))


def filter_send_kernel(count, halves, u_ref, *refs):
    tables = refs[:7]
    out_ref, done_ref, send_sem, recv_sem, own_sem = refs[7:]
    receivers, sources, samples = u_ref.shape
    own = sources // count
    per = receivers // halves
    me = lax.axis_index("shot")
    row = lax.axis_index("tm")
    barrier = pltpu.get_barrier_semaphore()

    def greet(step, carry):
        peer = lax.rem(me + step, count)
        pl.semaphore_signal(barrier, 1, device_id=(peer, row), device_id_type=pl.DeviceIdType.MESH)
        return carry

    lax.fori_loop(1, count, greet, 0)

    def remote(half, peer, sender):
        return pltpu.make_async_remote_copy(
            src_ref=done_ref.at[pl.ds(half * per, per), pl.ds(peer * own, own), :],
            dst_ref=out_ref.at[pl.ds(sender * receivers + half * per, per), :, :],
            send_sem=send_sem.at[half, peer],
            recv_sem=recv_sem.at[half, sender],
            device_id=(peer, row),
            device_id_type=pl.DeviceIdType.MESH,
        )

    locals_ = []
    for half in range(halves):
        filter_block(u_ref, half * per, per, tables, done_ref)
        if half == 0:
            pl.semaphore_wait(barrier, count - 1)
        mine = pltpu.make_async_copy(
            done_ref.at[pl.ds(half * per, per), pl.ds(me * own, own), :],
            out_ref.at[pl.ds(me * receivers + half * per, per), :, :],
            own_sem.at[half],
        )
        mine.start()
        locals_.append(mine)

        def send(step, carry, half=half):
            remote(half, lax.rem(me + step, count), me).start()
            return carry

        lax.fori_loop(1, count, send, 0)

    for half in range(halves):

        def finish(step, carry, half=half):
            peer = lax.rem(me + step, count)
            remote(half, peer, me).wait_send()
            remote(half, me, peer).wait_recv()
            return carry

        lax.fori_loop(1, count, finish, 0)
        locals_[half].wait()


def filter_and_send(gathers, limits, tables):
    forward, inverse, mix_forward, mix_inverse = tables
    receivers, sources, samples = gathers.shape
    count = lax.axis_size("shot")
    halves = 2
    vmem = pl.BlockSpec(memory_space=pltpu.VMEM)
    return pl.pallas_call(
        functools.partial(filter_send_kernel, count, halves),
        in_specs=[vmem] * 8,
        out_specs=pl.BlockSpec(memory_space=pl.ANY),
        out_shape=jax.ShapeDtypeStruct(
            (receivers * count, sources // count, samples), jnp.bfloat16
        ),
        scratch_shapes=[
            pltpu.VMEM(gathers.shape, jnp.bfloat16),
            pltpu.SemaphoreType.DMA((halves, count)),
            pltpu.SemaphoreType.DMA((halves, count)),
            pltpu.SemaphoreType.DMA((halves,)),
        ],
        compiler_params=pltpu.CompilerParams(
            collective_id=2, has_side_effects=True, vmem_limit_bytes=48 * 1024 * 1024
        ),
    )(gathers, forward, inverse, *mix_forward, *mix_inverse, limits.reshape(sources, 1))


def coherence(gathers, limits, tables):
    forward, inverse, mix_forward, mix_inverse = tables
    receivers, sources, samples = gathers.shape
    vmem = pl.BlockSpec(memory_space=pltpu.VMEM)
    return pl.pallas_call(
        filter_kernel,
        in_specs=[vmem] * 8,
        out_specs=vmem,
        out_shape=jax.ShapeDtypeStruct(gathers.shape, jnp.bfloat16),
        compiler_params=pltpu.CompilerParams(vmem_limit_bytes=48 * 1024 * 1024),
    )(gathers, forward, inverse, *mix_forward, *mix_inverse, limits.reshape(sources, 1))


def exchange_kernel(count, outgoing, incoming, src_ref, out_ref, send_sem, recv_sem, own_sem):
    me = lax.axis_index("shot")
    row = lax.axis_index("tm")
    barrier = pltpu.get_barrier_semaphore()

    def greet(step, carry):
        peer = lax.rem(me + step, count)
        pl.semaphore_signal(barrier, 1, device_id=(peer, row), device_id_type=pl.DeviceIdType.MESH)
        return carry

    lax.fori_loop(1, count, greet, 0)
    pl.semaphore_wait(barrier, count - 1)
    own = pltpu.make_async_copy(src_ref.at[outgoing(me)], out_ref.at[incoming(me)], own_sem)
    own.start()

    def remote(peer, sender):
        return pltpu.make_async_remote_copy(
            src_ref=src_ref.at[outgoing(peer)],
            dst_ref=out_ref.at[incoming(sender)],
            send_sem=send_sem.at[peer],
            recv_sem=recv_sem.at[sender],
            device_id=(peer, row),
            device_id_type=pl.DeviceIdType.MESH,
        )

    def send(step, carry):
        remote(lax.rem(me + step, count), me).start()
        return carry

    lax.fori_loop(1, count, send, 0)

    def finish(step, carry):
        peer = lax.rem(me + step, count)
        remote(peer, me).wait_send()
        remote(me, peer).wait_recv()
        return carry

    lax.fori_loop(1, count, finish, 0)
    own.wait()


def exchange(value, out_shape, outgoing, incoming, tag):
    count = lax.axis_size("shot")
    anywhere = pl.BlockSpec(memory_space=pl.ANY)
    return pl.pallas_call(
        functools.partial(exchange_kernel, count, outgoing, incoming),
        in_specs=[anywhere],
        out_specs=anywhere,
        out_shape=jax.ShapeDtypeStruct(out_shape, value.dtype),
        scratch_shapes=[
            pltpu.SemaphoreType.DMA((count,)),
            pltpu.SemaphoreType.DMA((count,)),
            pltpu.SemaphoreType.DMA,
        ],
        compiler_params=pltpu.CompilerParams(collective_id=tag, has_side_effects=True),
    )(value)


def to_sources(estimate):
    receivers, sources, samples = estimate.shape
    count = lax.axis_size("shot")
    own = sources // count
    return exchange(
        estimate,
        (receivers * count, own, samples),
        lambda peer: (slice(None), pl.ds(peer * own, own), slice(None)),
        lambda sender: (pl.ds(sender * receivers, receivers), slice(None), slice(None)),
        0,
    )


def to_receivers(records):
    receivers, own, samples = records.shape
    count = lax.axis_size("shot")
    part = receivers // count
    return exchange(
        records,
        (part, own * count, samples),
        lambda peer: (pl.ds(peer * part, part), slice(None), slice(None)),
        lambda sender: (slice(None), pl.ds(sender * own, own), slice(None)),
        1,
    )


def local(blended, delays, thresholds):
    tables = filter_tables()
    records = to_receivers(blended)
    samples = records.shape[2]
    row = lax.axis_index("tm")
    following = shifted(records[:, :, :BLK], "tm", -1)
    residual = records.astype(jnp.bfloat16)
    update = (RELAX * spread(residual, following.astype(jnp.bfloat16), delays)).astype(jnp.bfloat16)
    estimate, before, after = filter_with_halos(update, thresholds[0], tables)
    before = jnp.where(row == 0, jnp.zeros_like(before), before)
    last = row == lax.axis_size("tm") - 1
    after = jnp.where(last, jnp.zeros_like(after), after)
    blended_part = blend(jnp.concatenate([estimate, after], axis=2), before, delays)
    residual = (jnp.concatenate([records, following], axis=2) - blended_part).astype(jnp.bfloat16)
    tail = jnp.where(last, jnp.zeros_like(residual[:, :, samples:]), residual[:, :, samples:])
    update = (
        estimate.astype(jnp.float32) + RELAX * spread(residual[:, :, :samples], tail, delays)
    ).astype(jnp.bfloat16)
    return filter_and_send(update, thresholds[1], tables)


def solution(mesh):
    return jax.shard_map(
        local,
        mesh=mesh,
        in_specs=(P(None, "shot", "tm"), P(), P()),
        out_specs=P(None, "shot", "tm"),
        check_vma=False,
    )
```

```python
import functools
import math

import jax
import ml_dtypes
import numpy as np
import jax.numpy as jnp
from jax import lax
from jax.experimental import pallas as pl
from jax.experimental.pallas import tpu as pltpu
from jax.sharding import PartitionSpec as P

SRC = 64
SRC_EXP = 2
WIN = 256
BLK = 128
ITERS = 2


RELAX = 0.5


def shifted(array, axis, by):
    count = lax.axis_size(axis)
    pairs = [(i, i + by) for i in range(count) if 0 <= i + by < count]
    return lax.ppermute(array, axis, pairs)


def blend(estimate, earlier, own_delays):
    receivers, sources, samples = estimate.shape
    blocks = samples // BLK
    experiments = sources // SRC_EXP
    upper = estimate.reshape(receivers, sources, blocks, BLK)
    shifts = own_delays.reshape(-1)
    row_index = jnp.arange(BLK, dtype=jnp.int32)[None, :, None]
    column_index = jnp.arange(BLK, dtype=jnp.int32)[None, None, :]
    select_same = (row_index == column_index - shifts[:, None, None]).astype(jnp.bfloat16)
    select_prior = (row_index == BLK + column_index - shifts[:, None, None]).astype(jnp.bfloat16)
    same = jnp.einsum("rsnb,sbi->rsni", upper, select_same, preferred_element_type=jnp.float32)
    onward = jnp.einsum("rsnb,sbi->rsni", upper, select_prior, preferred_element_type=jnp.float32)
    edge_part = jnp.einsum(
        "rsb,sbi->rsi", earlier, select_prior, preferred_element_type=jnp.float32
    )
    same = jnp.sum(same.reshape(receivers, experiments, SRC_EXP, blocks, BLK), axis=2)
    onward = jnp.sum(onward.reshape(receivers, experiments, SRC_EXP, blocks, BLK), axis=2)
    edge_part = jnp.sum(edge_part.reshape(receivers, experiments, SRC_EXP, BLK), axis=2)
    carried = jnp.concatenate([edge_part[:, :, None], onward[:, :, : blocks - 1]], axis=2)
    return (same + carried).reshape(receivers, experiments, samples)


def spread(residual, later, own_delays):
    receivers, experiments, samples = residual.shape
    blocks = samples // BLK
    lower = residual.reshape(receivers, experiments, blocks, BLK)
    row_index = jnp.arange(BLK, dtype=jnp.int32)[None, None, :, None]
    column_index = jnp.arange(BLK, dtype=jnp.int32)[None, None, None, :]
    select_same = (row_index == column_index + own_delays[:, :, None, None]).astype(jnp.bfloat16)
    select_next = (row_index + BLK == column_index + own_delays[:, :, None, None]).astype(
        jnp.bfloat16
    )
    same = jnp.einsum("rena,ekai->rekni", lower, select_same, preferred_element_type=jnp.float32)
    backward = jnp.einsum(
        "rena,ekai->rekni", lower, select_next, preferred_element_type=jnp.float32
    )
    edge_part = jnp.einsum("rea,ekai->reki", later, select_next, preferred_element_type=jnp.float32)
    carried = jnp.concatenate([backward[:, :, :, 1:], edge_part[:, :, :, None]], axis=3)
    return (same + carried).reshape(receivers, experiments * SRC_EXP, samples)


def split(value):
    high = value.astype(jnp.bfloat16)
    return high, (value - high.astype(jnp.float32)).astype(jnp.bfloat16)


def exact_split(value):
    high = value.astype(ml_dtypes.bfloat16)
    low = (value - high.astype(np.float64)).astype(ml_dtypes.bfloat16)
    return jnp.asarray(high), jnp.asarray(low)


def filter_tables():
    turn = lambda n: (np.arange(n)[:, None] * np.arange(n)[None, :] % n) * (2.0 * np.pi / n)
    time_turn = turn(WIN)
    forward = jnp.asarray(
        np.concatenate([np.cos(time_turn), -np.sin(time_turn)], axis=1).astype(ml_dtypes.bfloat16)
    )
    inverse_high, inverse_low = exact_split(
        np.concatenate([np.cos(time_turn), -np.sin(time_turn)], axis=0) / math.sqrt(WIN)
    )
    inverse = jnp.concatenate([inverse_high, inverse_high, inverse_low], axis=0)
    source_turn = turn(SRC)
    cos_source = np.cos(source_turn) / math.sqrt(SRC)
    sin_source = np.sin(source_turn) / math.sqrt(SRC)
    mix_forward = exact_split(np.block([[cos_source, sin_source], [-sin_source, cos_source]]))
    mix_inverse = exact_split(np.block([[cos_source, -sin_source], [sin_source, cos_source]]))
    return forward, inverse, mix_forward, mix_inverse


def mix(table, value):
    table_high, table_low = table
    value_high, value_low = split(value)
    stacked = jnp.concatenate([value_high, value_low, value_high], axis=0)
    joined = jnp.concatenate([table_high, table_high, table_low], axis=1)
    return jnp.dot(joined, stacked, preferred_element_type=jnp.float32)


def filter_block(u_ref, first, count, tables, out_ref):
    forward_ref, inverse_ref, mfh_ref, mfl_ref, mih_ref, mil_ref, limit_ref = tables
    sources, samples = u_ref.shape[1:]
    windows = samples // WIN
    groups = [(r, w) for r in range(first, first + count) for w in range(windows)]
    scale = 1.0 / math.sqrt(WIN)
    rows = jnp.concatenate(
        [u_ref[r, :, w * WIN : (w + 1) * WIN] for r, w in groups], axis=0
    )
    spectrum = jnp.dot(rows, forward_ref[...], preferred_element_type=jnp.float32) * scale
    block = lambda g: slice(g * sources, (g + 1) * sources)
    field = jnp.concatenate(
        [
            jnp.concatenate([spectrum[block(g), :WIN], spectrum[block(g), WIN:]], axis=0)
            for g in range(len(groups))
        ],
        axis=1,
    )
    coeffs = mix((mfh_ref[...], mfl_ref[...]), field)
    real_part = coeffs[:sources]
    imag_part = coeffs[sources:]
    limit = limit_ref[...]
    magnitude = jnp.sqrt(real_part * real_part + imag_part * imag_part)
    factor = jnp.maximum(magnitude - limit, 0.0) / jnp.maximum(magnitude, limit)
    kept = jnp.concatenate([real_part * factor, imag_part * factor], axis=0)
    back = mix((mih_ref[...], mil_ref[...]), kept)
    lanes = lambda g: slice(g * WIN, (g + 1) * WIN)
    joined = jnp.concatenate(
        [
            jnp.concatenate([back[:sources, lanes(g)], back[sources:, lanes(g)]], axis=1)
            for g in range(len(groups))
        ],
        axis=0,
    )
    joined_high, joined_low = split(joined)
    restored = jnp.dot(
        jnp.concatenate([joined_high, joined_low, joined_high], axis=1),
        inverse_ref[...],
        preferred_element_type=jnp.float32,
    )
    for g, (r, w) in enumerate(groups):
        out_ref[r, :, w * WIN : (w + 1) * WIN] = restored[block(g)].astype(out_ref.dtype)


def spread_update(res_ref, shift_ref, dup_ref, est_ref, u_ref):
    receivers, sources, samples = u_ref.shape
    width = res_ref.shape[2]
    shift = shift_ref[...]
    for r in range(receivers):
        moved = jnp.dot(dup_ref[...], res_ref[r], preferred_element_type=jnp.float32)
        for bit in range((BLK - 1).bit_length()):
            amount = 1 << bit
            rolled = pltpu.roll(moved, width - amount, 1)
            moved = jnp.where((shift & amount) != 0, rolled, moved)
        value = RELAX * moved[:, :samples]
        if est_ref is not None:
            value = est_ref[r].astype(jnp.float32) + value
        u_ref[r] = value.astype(u_ref.dtype)


def spread_inputs(residual, delays):
    experiments = residual.shape[1]
    dup = (np.arange(experiments * SRC_EXP)[:, None] // SRC_EXP == np.arange(experiments)[None, :])
    return [residual, delays.reshape(-1, 1), jnp.asarray(dup.astype(ml_dtypes.bfloat16))]


def filter_kernel(u_ref, *refs):
    filter_block(u_ref, 0, u_ref.shape[0], refs[:7], refs[7])


def filter_halo_kernel(stages, res_ref, shift_ref, dup_ref, *refs):
    tables = refs[:7]
    out_ref, before_ref, after_ref, u_ref, send_sem, recv_sem = refs[7:]
    samples = u_ref.shape[2]
    shot = lax.axis_index("shot")
    row = lax.axis_index("tm")
    has_prev = row > 0
    has_next = row < stages - 1
    barrier = pltpu.get_barrier_semaphore()
    mesh_id = pl.DeviceIdType.MESH

    @pl.when(has_prev)
    def _():
        pl.semaphore_signal(barrier, 1, device_id=(shot, row - 1), device_id_type=mesh_id)

    @pl.when(has_next)
    def _():
        pl.semaphore_signal(barrier, 1, device_id=(shot, row + 1), device_id_type=mesh_id)

    spread_update(res_ref, shift_ref, dup_ref, None, u_ref)
    filter_block(u_ref, 0, u_ref.shape[0], tables, out_ref)
    pl.semaphore_wait(barrier, has_prev.astype(jnp.int32) + has_next.astype(jnp.int32))

    def to_prev():
        return pltpu.make_async_remote_copy(
            src_ref=out_ref.at[:, :, pl.ds(0, BLK)],
            dst_ref=after_ref,
            send_sem=send_sem.at[0],
            recv_sem=recv_sem.at[0],
            device_id=(shot, row - 1),
            device_id_type=mesh_id,
        )

    def to_next():
        return pltpu.make_async_remote_copy(
            src_ref=out_ref.at[:, :, pl.ds(samples - BLK, BLK)],
            dst_ref=before_ref,
            send_sem=send_sem.at[1],
            recv_sem=recv_sem.at[1],
            device_id=(shot, row + 1),
            device_id_type=mesh_id,
        )

    pl.when(has_prev)(lambda: to_prev().start())
    pl.when(has_next)(lambda: to_next().start())

    @pl.when(has_prev)
    def _():
        to_prev().wait_send()
        to_next().wait_recv()

    @pl.when(has_next)
    def _():
        to_next().wait_send()
        to_prev().wait_recv()


def filter_with_halos(residual, delays, limits, tables):
    forward, inverse, mix_forward, mix_inverse = tables
    receivers = residual.shape[0]
    sources = delays.size
    samples = residual.shape[2] - BLK
    stages = lax.axis_size("tm")
    vmem = pl.BlockSpec(memory_space=pltpu.VMEM)
    anywhere = pl.BlockSpec(memory_space=pl.ANY)
    edge = jax.ShapeDtypeStruct((receivers, sources, BLK), jnp.bfloat16)
    return pl.pallas_call(
        functools.partial(filter_halo_kernel, stages),
        in_specs=[vmem] * 10,
        out_specs=(vmem, anywhere, anywhere),
        out_shape=(jax.ShapeDtypeStruct((receivers, sources, samples), jnp.bfloat16), edge, edge),
        scratch_shapes=[
            pltpu.VMEM((receivers, sources, samples), jnp.bfloat16),
            pltpu.SemaphoreType.DMA((2,)),
            pltpu.SemaphoreType.DMA((2,)),
        ],
        compiler_params=pltpu.CompilerParams(
            collective_id=3, has_side_effects=True, vmem_limit_bytes=48 * 1024 * 1024
        ),
    )(
        *spread_inputs(residual, delays),
        forward, inverse, *mix_forward, *mix_inverse, limits.reshape(sources, 1),
    )


def filter_send_kernel(count, halves, est_ref, res_ref, shift_ref, dup_ref, *refs):
    tables = refs[:7]
    out_ref, done_ref, u_ref, send_sem, recv_sem, own_sem = refs[7:]
    receivers, sources, samples = u_ref.shape
    own = sources // count
    per = receivers // halves
    me = lax.axis_index("shot")
    row = lax.axis_index("tm")
    barrier = pltpu.get_barrier_semaphore()

    def greet(step, carry):
        peer = lax.rem(me + step, count)
        pl.semaphore_signal(barrier, 1, device_id=(peer, row), device_id_type=pl.DeviceIdType.MESH)
        return carry

    lax.fori_loop(1, count, greet, 0)
    spread_update(res_ref, shift_ref, dup_ref, est_ref, u_ref)

    def remote(half, peer, sender):
        return pltpu.make_async_remote_copy(
            src_ref=done_ref.at[pl.ds(half * per, per), pl.ds(peer * own, own), :],
            dst_ref=out_ref.at[pl.ds(sender * receivers + half * per, per), :, :],
            send_sem=send_sem.at[half, peer],
            recv_sem=recv_sem.at[half, sender],
            device_id=(peer, row),
            device_id_type=pl.DeviceIdType.MESH,
        )

    locals_ = []
    for half in range(halves):
        filter_block(u_ref, half * per, per, tables, done_ref)
        if half == 0:
            pl.semaphore_wait(barrier, count - 1)
        mine = pltpu.make_async_copy(
            done_ref.at[pl.ds(half * per, per), pl.ds(me * own, own), :],
            out_ref.at[pl.ds(me * receivers + half * per, per), :, :],
            own_sem.at[half],
        )
        mine.start()
        locals_.append(mine)

        def send(step, carry, half=half):
            remote(half, lax.rem(me + step, count), me).start()
            return carry

        lax.fori_loop(1, count, send, 0)

    for half in range(halves):

        def finish(step, carry, half=half):
            peer = lax.rem(me + step, count)
            remote(half, peer, me).wait_send()
            remote(half, me, peer).wait_recv()
            return carry

        lax.fori_loop(1, count, finish, 0)
        locals_[half].wait()


def filter_and_send(estimate, residual, delays, limits, tables):
    forward, inverse, mix_forward, mix_inverse = tables
    receivers, sources, samples = estimate.shape
    count = lax.axis_size("shot")
    halves = 2
    vmem = pl.BlockSpec(memory_space=pltpu.VMEM)
    return pl.pallas_call(
        functools.partial(filter_send_kernel, count, halves),
        in_specs=[vmem] * 11,
        out_specs=pl.BlockSpec(memory_space=pl.ANY),
        out_shape=jax.ShapeDtypeStruct(
            (receivers * count, sources // count, samples), jnp.bfloat16
        ),
        scratch_shapes=[
            pltpu.VMEM(estimate.shape, jnp.bfloat16),
            pltpu.VMEM(estimate.shape, jnp.bfloat16),
            pltpu.SemaphoreType.DMA((halves, count)),
            pltpu.SemaphoreType.DMA((halves, count)),
            pltpu.SemaphoreType.DMA((halves,)),
        ],
        compiler_params=pltpu.CompilerParams(
            collective_id=2, has_side_effects=True, vmem_limit_bytes=48 * 1024 * 1024
        ),
    )(
        estimate,
        *spread_inputs(residual, delays),
        forward, inverse, *mix_forward, *mix_inverse, limits.reshape(sources, 1),
    )


def coherence(gathers, limits, tables):
    forward, inverse, mix_forward, mix_inverse = tables
    receivers, sources, samples = gathers.shape
    vmem = pl.BlockSpec(memory_space=pltpu.VMEM)
    return pl.pallas_call(
        filter_kernel,
        in_specs=[vmem] * 8,
        out_specs=vmem,
        out_shape=jax.ShapeDtypeStruct(gathers.shape, jnp.bfloat16),
        compiler_params=pltpu.CompilerParams(vmem_limit_bytes=48 * 1024 * 1024),
    )(gathers, forward, inverse, *mix_forward, *mix_inverse, limits.reshape(sources, 1))


def exchange_kernel(count, outgoing, incoming, src_ref, out_ref, send_sem, recv_sem, own_sem):
    me = lax.axis_index("shot")
    row = lax.axis_index("tm")
    barrier = pltpu.get_barrier_semaphore()

    def greet(step, carry):
        peer = lax.rem(me + step, count)
        pl.semaphore_signal(barrier, 1, device_id=(peer, row), device_id_type=pl.DeviceIdType.MESH)
        return carry

    lax.fori_loop(1, count, greet, 0)
    pl.semaphore_wait(barrier, count - 1)
    own = pltpu.make_async_copy(src_ref.at[outgoing(me)], out_ref.at[incoming(me)], own_sem)
    own.start()

    def remote(peer, sender):
        return pltpu.make_async_remote_copy(
            src_ref=src_ref.at[outgoing(peer)],
            dst_ref=out_ref.at[incoming(sender)],
            send_sem=send_sem.at[peer],
            recv_sem=recv_sem.at[sender],
            device_id=(peer, row),
            device_id_type=pl.DeviceIdType.MESH,
        )

    def send(step, carry):
        remote(lax.rem(me + step, count), me).start()
        return carry

    lax.fori_loop(1, count, send, 0)

    def finish(step, carry):
        peer = lax.rem(me + step, count)
        remote(peer, me).wait_send()
        remote(me, peer).wait_recv()
        return carry

    lax.fori_loop(1, count, finish, 0)
    own.wait()


def exchange(value, out_shape, outgoing, incoming, tag):
    count = lax.axis_size("shot")
    anywhere = pl.BlockSpec(memory_space=pl.ANY)
    return pl.pallas_call(
        functools.partial(exchange_kernel, count, outgoing, incoming),
        in_specs=[anywhere],
        out_specs=anywhere,
        out_shape=jax.ShapeDtypeStruct(out_shape, value.dtype),
        scratch_shapes=[
            pltpu.SemaphoreType.DMA((count,)),
            pltpu.SemaphoreType.DMA((count,)),
            pltpu.SemaphoreType.DMA,
        ],
        compiler_params=pltpu.CompilerParams(collective_id=tag, has_side_effects=True),
    )(value)


def to_sources(estimate):
    receivers, sources, samples = estimate.shape
    count = lax.axis_size("shot")
    own = sources // count
    return exchange(
        estimate,
        (receivers * count, own, samples),
        lambda peer: (slice(None), pl.ds(peer * own, own), slice(None)),
        lambda sender: (pl.ds(sender * receivers, receivers), slice(None), slice(None)),
        0,
    )


def to_receivers(records):
    receivers, own, samples = records.shape
    count = lax.axis_size("shot")
    part = receivers // count
    return exchange(
        records,
        (part, own * count, samples),
        lambda peer: (pl.ds(peer * part, part), slice(None), slice(None)),
        lambda sender: (slice(None), pl.ds(sender * own, own), slice(None)),
        1,
    )


def local(blended, delays, thresholds):
    tables = filter_tables()
    records = to_receivers(blended)
    samples = records.shape[2]
    row = lax.axis_index("tm")
    following = shifted(records[:, :, :BLK], "tm", -1)
    extended = jnp.concatenate([records, following], axis=2)
    estimate, before, after = filter_with_halos(
        extended.astype(jnp.bfloat16), delays, thresholds[0], tables
    )
    before = jnp.where(row == 0, jnp.zeros_like(before), before)
    last = row == lax.axis_size("tm") - 1
    after = jnp.where(last, jnp.zeros_like(after), after)
    blended_part = blend(jnp.concatenate([estimate, after], axis=2), before, delays)
    residual = (extended - blended_part).astype(jnp.bfloat16)
    keep = jnp.logical_or(jnp.arange(samples + BLK) < samples, jnp.logical_not(last))
    residual = jnp.where(keep[None, None, :], residual, jnp.zeros_like(residual))
    return filter_and_send(estimate, residual, delays, thresholds[1], tables)


def solution(mesh):
    return jax.shard_map(
        local,
        mesh=mesh,
        in_specs=(P(None, "shot", "tm"), P(), P()),
        out_specs=P(None, "shot", "tm"),
        check_vma=False,
    )
```

```python
import functools
import math

import jax
import ml_dtypes
import numpy as np
import jax.numpy as jnp
from jax import lax
from jax.experimental import pallas as pl
from jax.experimental.pallas import tpu as pltpu
from jax.sharding import PartitionSpec as P

SRC = 64
SRC_EXP = 2
WIN = 256
BLK = 128
ITERS = 2


RELAX = 0.5


def shifted(array, axis, by):
    count = lax.axis_size(axis)
    pairs = [(i, i + by) for i in range(count) if 0 <= i + by < count]
    return lax.ppermute(array, axis, pairs)


def blend(estimate, earlier, own_delays):
    receivers, sources, samples = estimate.shape
    blocks = samples // BLK
    experiments = sources // SRC_EXP
    upper = estimate.reshape(receivers, sources, blocks, BLK)
    shifts = own_delays.reshape(-1)
    row_index = jnp.arange(BLK, dtype=jnp.int32)[None, :, None]
    column_index = jnp.arange(BLK, dtype=jnp.int32)[None, None, :]
    select_same = (row_index == column_index - shifts[:, None, None]).astype(jnp.bfloat16)
    select_prior = (row_index == BLK + column_index - shifts[:, None, None]).astype(jnp.bfloat16)
    same = jnp.einsum("rsnb,sbi->rsni", upper, select_same, preferred_element_type=jnp.float32)
    onward = jnp.einsum("rsnb,sbi->rsni", upper, select_prior, preferred_element_type=jnp.float32)
    edge_part = jnp.einsum(
        "rsb,sbi->rsi", earlier, select_prior, preferred_element_type=jnp.float32
    )
    same = jnp.sum(same.reshape(receivers, experiments, SRC_EXP, blocks, BLK), axis=2)
    onward = jnp.sum(onward.reshape(receivers, experiments, SRC_EXP, blocks, BLK), axis=2)
    edge_part = jnp.sum(edge_part.reshape(receivers, experiments, SRC_EXP, BLK), axis=2)
    carried = jnp.concatenate([edge_part[:, :, None], onward[:, :, : blocks - 1]], axis=2)
    return (same + carried).reshape(receivers, experiments, samples)


def spread(residual, later, own_delays):
    receivers, experiments, samples = residual.shape
    blocks = samples // BLK
    lower = residual.reshape(receivers, experiments, blocks, BLK)
    row_index = jnp.arange(BLK, dtype=jnp.int32)[None, None, :, None]
    column_index = jnp.arange(BLK, dtype=jnp.int32)[None, None, None, :]
    select_same = (row_index == column_index + own_delays[:, :, None, None]).astype(jnp.bfloat16)
    select_next = (row_index + BLK == column_index + own_delays[:, :, None, None]).astype(
        jnp.bfloat16
    )
    same = jnp.einsum("rena,ekai->rekni", lower, select_same, preferred_element_type=jnp.float32)
    backward = jnp.einsum(
        "rena,ekai->rekni", lower, select_next, preferred_element_type=jnp.float32
    )
    edge_part = jnp.einsum("rea,ekai->reki", later, select_next, preferred_element_type=jnp.float32)
    carried = jnp.concatenate([backward[:, :, :, 1:], edge_part[:, :, :, None]], axis=3)
    return (same + carried).reshape(receivers, experiments * SRC_EXP, samples)


def split(value):
    high = value.astype(jnp.bfloat16)
    return high, (value - high.astype(jnp.float32)).astype(jnp.bfloat16)


def exact_split(value):
    high = value.astype(ml_dtypes.bfloat16)
    low = (value - high.astype(np.float64)).astype(ml_dtypes.bfloat16)
    return jnp.asarray(high), jnp.asarray(low)


def filter_tables():
    turn = lambda n: (np.arange(n)[:, None] * np.arange(n)[None, :] % n) * (2.0 * np.pi / n)
    time_turn = turn(WIN)
    forward = jnp.asarray(
        np.concatenate([np.cos(time_turn), -np.sin(time_turn)], axis=1).astype(ml_dtypes.bfloat16)
    )
    inverse_high, inverse_low = exact_split(
        np.concatenate([np.cos(time_turn), -np.sin(time_turn)], axis=0) / math.sqrt(WIN)
    )
    inverse = jnp.concatenate([inverse_high, inverse_high, inverse_low], axis=0)
    source_turn = turn(SRC)
    cos_source = np.cos(source_turn) / math.sqrt(SRC)
    sin_source = np.sin(source_turn) / math.sqrt(SRC)
    mix_forward = exact_split(np.block([[cos_source, sin_source], [-sin_source, cos_source]]))
    mix_inverse = exact_split(np.block([[cos_source, -sin_source], [sin_source, cos_source]]))
    return forward, inverse, mix_forward, mix_inverse


def mix(table, value):
    table_high, table_low = table
    value_high, value_low = split(value)
    stacked = jnp.concatenate([value_high, value_low, value_high], axis=0)
    joined = jnp.concatenate([table_high, table_high, table_low], axis=1)
    return jnp.dot(joined, stacked, preferred_element_type=jnp.float32)


def filter_block(u_ref, first, count, tables, out_ref):
    forward_ref, inverse_ref, mfh_ref, mfl_ref, mih_ref, mil_ref, limit_ref = tables
    sources, samples = u_ref.shape[1:]
    windows = samples // WIN
    groups = [(r, w) for r in range(first, first + count) for w in range(windows)]
    scale = 1.0 / math.sqrt(WIN)
    rows = jnp.concatenate(
        [u_ref[r, :, w * WIN : (w + 1) * WIN] for r, w in groups], axis=0
    )
    spectrum = jnp.dot(rows, forward_ref[...], preferred_element_type=jnp.float32) * scale
    block = lambda g: slice(g * sources, (g + 1) * sources)
    field = jnp.concatenate(
        [
            jnp.concatenate([spectrum[block(g), :WIN], spectrum[block(g), WIN:]], axis=0)
            for g in range(len(groups))
        ],
        axis=1,
    )
    coeffs = mix((mfh_ref[...], mfl_ref[...]), field)
    real_part = coeffs[:sources]
    imag_part = coeffs[sources:]
    limit = limit_ref[...]
    magnitude = jnp.sqrt(real_part * real_part + imag_part * imag_part)
    factor = jnp.maximum(magnitude - limit, 0.0) / jnp.maximum(magnitude, limit)
    kept = jnp.concatenate([real_part * factor, imag_part * factor], axis=0)
    back = mix((mih_ref[...], mil_ref[...]), kept)
    lanes = lambda g: slice(g * WIN, (g + 1) * WIN)
    joined = jnp.concatenate(
        [
            jnp.concatenate([back[:sources, lanes(g)], back[sources:, lanes(g)]], axis=1)
            for g in range(len(groups))
        ],
        axis=0,
    )
    joined_high, joined_low = split(joined)
    restored = jnp.dot(
        jnp.concatenate([joined_high, joined_low, joined_high], axis=1),
        inverse_ref[...],
        preferred_element_type=jnp.float32,
    )
    for g, (r, w) in enumerate(groups):
        out_ref[r, :, w * WIN : (w + 1) * WIN] = restored[block(g)].astype(out_ref.dtype)


def blend_residual(rec_ref, est_ref, before_ref, after_ref, shift_ref, pair_ref, last, res_ref):
    receivers, experiments, width = rec_ref.shape
    shift = shift_ref[...]
    lane = lax.broadcasted_iota(jnp.int32, (experiments, width), 1)
    drop = jnp.logical_and(lane >= width - BLK, last)
    for r in range(receivers):
        moved = jnp.concatenate([before_ref[r], est_ref[r], after_ref[r]], axis=1).astype(jnp.float32)
        full = moved.shape[1]
        for bit in range((BLK - 1).bit_length()):
            amount = 1 << bit
            moved = jnp.where((shift & amount) != 0, pltpu.roll(moved, amount, 1), moved)
        summed = jnp.dot(
            pair_ref[...], moved[:, full - width :].astype(jnp.bfloat16),
            preferred_element_type=jnp.float32,
        )
        residual = (rec_ref[r] - summed).astype(res_ref.dtype)
        res_ref[r] = jnp.where(drop, jnp.zeros_like(residual), residual)


def spread_update(res_ref, shift_ref, dup_ref, est_ref, u_ref):
    receivers, sources, samples = u_ref.shape
    width = res_ref.shape[2]
    shift = shift_ref[...]
    for r in range(receivers):
        moved = jnp.dot(dup_ref[...], res_ref[r], preferred_element_type=jnp.float32)
        for bit in range((BLK - 1).bit_length()):
            amount = 1 << bit
            rolled = pltpu.roll(moved, width - amount, 1)
            moved = jnp.where((shift & amount) != 0, rolled, moved)
        value = RELAX * moved[:, :samples]
        if est_ref is not None:
            value = est_ref[r].astype(jnp.float32) + value
        u_ref[r] = value.astype(u_ref.dtype)


def pairing(experiments):
    source = np.arange(experiments * SRC_EXP)[:, None] // SRC_EXP
    return (source == np.arange(experiments)[None, :]).astype(ml_dtypes.bfloat16)


def spread_inputs(residual, delays):
    return [residual, delays.reshape(-1, 1), jnp.asarray(pairing(residual.shape[1]))]


def filter_kernel(u_ref, *refs):
    filter_block(u_ref, 0, u_ref.shape[0], refs[:7], refs[7])


def filter_halo_kernel(stages, res_ref, shift_ref, dup_ref, *refs):
    tables = refs[:7]
    out_ref, before_ref, after_ref, u_ref, send_sem, recv_sem = refs[7:]
    samples = u_ref.shape[2]
    shot = lax.axis_index("shot")
    row = lax.axis_index("tm")
    has_prev = row > 0
    has_next = row < stages - 1
    barrier = pltpu.get_barrier_semaphore()
    mesh_id = pl.DeviceIdType.MESH

    @pl.when(has_prev)
    def _():
        pl.semaphore_signal(barrier, 1, device_id=(shot, row - 1), device_id_type=mesh_id)

    @pl.when(has_next)
    def _():
        pl.semaphore_signal(barrier, 1, device_id=(shot, row + 1), device_id_type=mesh_id)

    spread_update(res_ref, shift_ref, dup_ref, None, u_ref)
    filter_block(u_ref, 0, u_ref.shape[0], tables, out_ref)
    pl.semaphore_wait(barrier, has_prev.astype(jnp.int32) + has_next.astype(jnp.int32))

    def to_prev():
        return pltpu.make_async_remote_copy(
            src_ref=out_ref.at[:, :, pl.ds(0, BLK)],
            dst_ref=after_ref,
            send_sem=send_sem.at[0],
            recv_sem=recv_sem.at[0],
            device_id=(shot, row - 1),
            device_id_type=mesh_id,
        )

    def to_next():
        return pltpu.make_async_remote_copy(
            src_ref=out_ref.at[:, :, pl.ds(samples - BLK, BLK)],
            dst_ref=before_ref,
            send_sem=send_sem.at[1],
            recv_sem=recv_sem.at[1],
            device_id=(shot, row + 1),
            device_id_type=mesh_id,
        )

    pl.when(has_prev)(lambda: to_prev().start())
    pl.when(has_next)(lambda: to_next().start())

    @pl.when(has_prev)
    def _():
        to_prev().wait_send()
        to_next().wait_recv()

    @pl.when(has_next)
    def _():
        to_next().wait_send()
        to_prev().wait_recv()


def filter_with_halos(residual, delays, limits, tables):
    forward, inverse, mix_forward, mix_inverse = tables
    receivers = residual.shape[0]
    sources = delays.size
    samples = residual.shape[2] - BLK
    stages = lax.axis_size("tm")
    vmem = pl.BlockSpec(memory_space=pltpu.VMEM)
    anywhere = pl.BlockSpec(memory_space=pl.ANY)
    edge = jax.ShapeDtypeStruct((receivers, sources, BLK), jnp.bfloat16)
    return pl.pallas_call(
        functools.partial(filter_halo_kernel, stages),
        in_specs=[vmem] * 10,
        out_specs=(vmem, anywhere, anywhere),
        out_shape=(jax.ShapeDtypeStruct((receivers, sources, samples), jnp.bfloat16), edge, edge),
        scratch_shapes=[
            pltpu.VMEM((receivers, sources, samples), jnp.bfloat16),
            pltpu.SemaphoreType.DMA((2,)),
            pltpu.SemaphoreType.DMA((2,)),
        ],
        compiler_params=pltpu.CompilerParams(
            collective_id=3, has_side_effects=True, vmem_limit_bytes=48 * 1024 * 1024
        ),
    )(
        *spread_inputs(residual, delays),
        forward, inverse, *mix_forward, *mix_inverse, limits.reshape(sources, 1),
    )


def filter_send_kernel(
    count, stages, halves, est_ref, before_ref, after_ref, rec_ref, pair_ref, shift_ref, dup_ref, *refs
):
    tables = refs[:7]
    out_ref, done_ref, u_ref, res_ref, send_sem, recv_sem, own_sem = refs[7:]
    receivers, sources, samples = u_ref.shape
    own = sources // count
    per = receivers // halves
    me = lax.axis_index("shot")
    row = lax.axis_index("tm")
    barrier = pltpu.get_barrier_semaphore()

    def greet(step, carry):
        peer = lax.rem(me + step, count)
        pl.semaphore_signal(barrier, 1, device_id=(peer, row), device_id_type=pl.DeviceIdType.MESH)
        return carry

    lax.fori_loop(1, count, greet, 0)
    last = lax.axis_index("tm") == stages - 1
    blend_residual(rec_ref, est_ref, before_ref, after_ref, shift_ref, pair_ref, last, res_ref)
    spread_update(res_ref, shift_ref, dup_ref, est_ref, u_ref)

    def remote(half, peer, sender):
        return pltpu.make_async_remote_copy(
            src_ref=done_ref.at[pl.ds(half * per, per), pl.ds(peer * own, own), :],
            dst_ref=out_ref.at[pl.ds(sender * receivers + half * per, per), :, :],
            send_sem=send_sem.at[half, peer],
            recv_sem=recv_sem.at[half, sender],
            device_id=(peer, row),
            device_id_type=pl.DeviceIdType.MESH,
        )

    locals_ = []
    for half in range(halves):
        filter_block(u_ref, half * per, per, tables, done_ref)
        if half == 0:
            pl.semaphore_wait(barrier, count - 1)
        mine = pltpu.make_async_copy(
            done_ref.at[pl.ds(half * per, per), pl.ds(me * own, own), :],
            out_ref.at[pl.ds(me * receivers + half * per, per), :, :],
            own_sem.at[half],
        )
        mine.start()
        locals_.append(mine)

        def send(step, carry, half=half):
            remote(half, lax.rem(me + step, count), me).start()
            return carry

        lax.fori_loop(1, count, send, 0)

    for half in range(halves):

        def finish(step, carry, half=half):
            peer = lax.rem(me + step, count)
            remote(half, peer, me).wait_send()
            remote(half, me, peer).wait_recv()
            return carry

        lax.fori_loop(1, count, finish, 0)
        locals_[half].wait()


def filter_and_send(estimate, before, after, records, delays, limits, tables):
    forward, inverse, mix_forward, mix_inverse = tables
    receivers, sources, samples = estimate.shape
    count = lax.axis_size("shot")
    halves = 2
    vmem = pl.BlockSpec(memory_space=pltpu.VMEM)
    return pl.pallas_call(
        functools.partial(filter_send_kernel, count, lax.axis_size("tm"), halves),
        in_specs=[vmem] * 14,
        out_specs=pl.BlockSpec(memory_space=pl.ANY),
        out_shape=jax.ShapeDtypeStruct(
            (receivers * count, sources // count, samples), jnp.bfloat16
        ),
        scratch_shapes=[
            pltpu.VMEM(estimate.shape, jnp.bfloat16),
            pltpu.VMEM(estimate.shape, jnp.bfloat16),
            pltpu.VMEM(records.shape, jnp.bfloat16),
            pltpu.SemaphoreType.DMA((halves, count)),
            pltpu.SemaphoreType.DMA((halves, count)),
            pltpu.SemaphoreType.DMA((halves,)),
        ],
        compiler_params=pltpu.CompilerParams(
            collective_id=2, has_side_effects=True, vmem_limit_bytes=48 * 1024 * 1024
        ),
    )(
        estimate,
        before,
        after,
        records,
        jnp.asarray(np.ascontiguousarray(pairing(records.shape[1]).T)),
        *spread_inputs(records, delays)[1:],
        forward, inverse, *mix_forward, *mix_inverse, limits.reshape(sources, 1),
    )


def coherence(gathers, limits, tables):
    forward, inverse, mix_forward, mix_inverse = tables
    receivers, sources, samples = gathers.shape
    vmem = pl.BlockSpec(memory_space=pltpu.VMEM)
    return pl.pallas_call(
        filter_kernel,
        in_specs=[vmem] * 8,
        out_specs=vmem,
        out_shape=jax.ShapeDtypeStruct(gathers.shape, jnp.bfloat16),
        compiler_params=pltpu.CompilerParams(vmem_limit_bytes=48 * 1024 * 1024),
    )(gathers, forward, inverse, *mix_forward, *mix_inverse, limits.reshape(sources, 1))


def exchange_kernel(count, outgoing, incoming, src_ref, out_ref, send_sem, recv_sem, own_sem):
    me = lax.axis_index("shot")
    row = lax.axis_index("tm")
    barrier = pltpu.get_barrier_semaphore()

    def greet(step, carry):
        peer = lax.rem(me + step, count)
        pl.semaphore_signal(barrier, 1, device_id=(peer, row), device_id_type=pl.DeviceIdType.MESH)
        return carry

    lax.fori_loop(1, count, greet, 0)
    pl.semaphore_wait(barrier, count - 1)
    own = pltpu.make_async_copy(src_ref.at[outgoing(me)], out_ref.at[incoming(me)], own_sem)
    own.start()

    def remote(peer, sender):
        return pltpu.make_async_remote_copy(
            src_ref=src_ref.at[outgoing(peer)],
            dst_ref=out_ref.at[incoming(sender)],
            send_sem=send_sem.at[peer],
            recv_sem=recv_sem.at[sender],
            device_id=(peer, row),
            device_id_type=pl.DeviceIdType.MESH,
        )

    def send(step, carry):
        remote(lax.rem(me + step, count), me).start()
        return carry

    lax.fori_loop(1, count, send, 0)

    def finish(step, carry):
        peer = lax.rem(me + step, count)
        remote(peer, me).wait_send()
        remote(me, peer).wait_recv()
        return carry

    lax.fori_loop(1, count, finish, 0)
    own.wait()


def exchange(value, out_shape, outgoing, incoming, tag):
    count = lax.axis_size("shot")
    anywhere = pl.BlockSpec(memory_space=pl.ANY)
    return pl.pallas_call(
        functools.partial(exchange_kernel, count, outgoing, incoming),
        in_specs=[anywhere],
        out_specs=anywhere,
        out_shape=jax.ShapeDtypeStruct(out_shape, value.dtype),
        scratch_shapes=[
            pltpu.SemaphoreType.DMA((count,)),
            pltpu.SemaphoreType.DMA((count,)),
            pltpu.SemaphoreType.DMA,
        ],
        compiler_params=pltpu.CompilerParams(collective_id=tag, has_side_effects=True),
    )(value)


def to_sources(estimate):
    receivers, sources, samples = estimate.shape
    count = lax.axis_size("shot")
    own = sources // count
    return exchange(
        estimate,
        (receivers * count, own, samples),
        lambda peer: (slice(None), pl.ds(peer * own, own), slice(None)),
        lambda sender: (pl.ds(sender * receivers, receivers), slice(None), slice(None)),
        0,
    )


def to_receivers(records):
    receivers, own, samples = records.shape
    count = lax.axis_size("shot")
    part = receivers // count
    return exchange(
        records,
        (part, own * count, samples),
        lambda peer: (pl.ds(peer * part, part), slice(None), slice(None)),
        lambda sender: (slice(None), pl.ds(sender * own, own), slice(None)),
        1,
    )


def local(blended, delays, thresholds):
    tables = filter_tables()
    records = to_receivers(blended)
    samples = records.shape[2]
    row = lax.axis_index("tm")
    following = shifted(records[:, :, :BLK], "tm", -1)
    extended = jnp.concatenate([records, following], axis=2)
    estimate, before, after = filter_with_halos(
        extended.astype(jnp.bfloat16), delays, thresholds[0], tables
    )
    before = jnp.where(row == 0, jnp.zeros_like(before), before)
    last = row == lax.axis_size("tm") - 1
    after = jnp.where(last, jnp.zeros_like(after), after)
    return filter_and_send(estimate, before, after, extended, delays, thresholds[1], tables)


def solution(mesh):
    return jax.shard_map(
        local,
        mesh=mesh,
        in_specs=(P(None, "shot", "tm"), P(), P()),
        out_specs=P(None, "shot", "tm"),
        check_vma=False,
    )
```

```python
import functools
import math

import jax
import ml_dtypes
import numpy as np
import jax.numpy as jnp
from jax import lax
from jax.experimental import pallas as pl
from jax.experimental.pallas import tpu as pltpu
from jax.sharding import PartitionSpec as P

SRC = 64
SRC_EXP = 2
WIN = 256
BLK = 128
ITERS = 2


RELAX = 0.5


def shifted(array, axis, by):
    count = lax.axis_size(axis)
    pairs = [(i, i + by) for i in range(count) if 0 <= i + by < count]
    return lax.ppermute(array, axis, pairs)


def blend(estimate, earlier, own_delays):
    receivers, sources, samples = estimate.shape
    blocks = samples // BLK
    experiments = sources // SRC_EXP
    upper = estimate.reshape(receivers, sources, blocks, BLK)
    shifts = own_delays.reshape(-1)
    row_index = jnp.arange(BLK, dtype=jnp.int32)[None, :, None]
    column_index = jnp.arange(BLK, dtype=jnp.int32)[None, None, :]
    select_same = (row_index == column_index - shifts[:, None, None]).astype(jnp.bfloat16)
    select_prior = (row_index == BLK + column_index - shifts[:, None, None]).astype(jnp.bfloat16)
    same = jnp.einsum("rsnb,sbi->rsni", upper, select_same, preferred_element_type=jnp.float32)
    onward = jnp.einsum("rsnb,sbi->rsni", upper, select_prior, preferred_element_type=jnp.float32)
    edge_part = jnp.einsum(
        "rsb,sbi->rsi", earlier, select_prior, preferred_element_type=jnp.float32
    )
    same = jnp.sum(same.reshape(receivers, experiments, SRC_EXP, blocks, BLK), axis=2)
    onward = jnp.sum(onward.reshape(receivers, experiments, SRC_EXP, blocks, BLK), axis=2)
    edge_part = jnp.sum(edge_part.reshape(receivers, experiments, SRC_EXP, BLK), axis=2)
    carried = jnp.concatenate([edge_part[:, :, None], onward[:, :, : blocks - 1]], axis=2)
    return (same + carried).reshape(receivers, experiments, samples)


def spread(residual, later, own_delays):
    receivers, experiments, samples = residual.shape
    blocks = samples // BLK
    lower = residual.reshape(receivers, experiments, blocks, BLK)
    row_index = jnp.arange(BLK, dtype=jnp.int32)[None, None, :, None]
    column_index = jnp.arange(BLK, dtype=jnp.int32)[None, None, None, :]
    select_same = (row_index == column_index + own_delays[:, :, None, None]).astype(jnp.bfloat16)
    select_next = (row_index + BLK == column_index + own_delays[:, :, None, None]).astype(
        jnp.bfloat16
    )
    same = jnp.einsum("rena,ekai->rekni", lower, select_same, preferred_element_type=jnp.float32)
    backward = jnp.einsum(
        "rena,ekai->rekni", lower, select_next, preferred_element_type=jnp.float32
    )
    edge_part = jnp.einsum("rea,ekai->reki", later, select_next, preferred_element_type=jnp.float32)
    carried = jnp.concatenate([backward[:, :, :, 1:], edge_part[:, :, :, None]], axis=3)
    return (same + carried).reshape(receivers, experiments * SRC_EXP, samples)


def split(value):
    high = value.astype(jnp.bfloat16)
    return high, (value - high.astype(jnp.float32)).astype(jnp.bfloat16)


def exact_split(value):
    high = value.astype(ml_dtypes.bfloat16)
    low = (value - high.astype(np.float64)).astype(ml_dtypes.bfloat16)
    return jnp.asarray(high), jnp.asarray(low)


def filter_tables():
    turn = lambda n: (np.arange(n)[:, None] * np.arange(n)[None, :] % n) * (2.0 * np.pi / n)
    time_turn = turn(WIN)
    forward = jnp.asarray(
        np.concatenate([np.cos(time_turn), -np.sin(time_turn)], axis=1).astype(ml_dtypes.bfloat16)
    )
    inverse_high, inverse_low = exact_split(
        np.concatenate([np.cos(time_turn), -np.sin(time_turn)], axis=0) / math.sqrt(WIN)
    )
    inverse = jnp.concatenate([inverse_high, inverse_high, inverse_low], axis=0)
    source_turn = turn(SRC)
    cos_source = np.cos(source_turn) / math.sqrt(SRC)
    sin_source = np.sin(source_turn) / math.sqrt(SRC)
    mix_forward = exact_split(np.block([[cos_source, sin_source], [-sin_source, cos_source]]))
    mix_inverse = exact_split(np.block([[cos_source, -sin_source], [sin_source, cos_source]]))
    return forward, inverse, mix_forward, mix_inverse


def mix(table, value):
    table_high, table_low = table
    value_high, value_low = split(value)
    stacked = jnp.concatenate([value_high, value_low, value_high], axis=0)
    joined = jnp.concatenate([table_high, table_high, table_low], axis=1)
    return jnp.dot(joined, stacked, preferred_element_type=jnp.float32)


def filter_block(u_ref, first, count, tables, out_ref):
    forward_ref, inverse_ref, mfh_ref, mfl_ref, mih_ref, mil_ref, limit_ref = tables
    sources, samples = u_ref.shape[1:]
    windows = samples // WIN
    groups = [(r, w) for r in range(first, first + count) for w in range(windows)]
    scale = 1.0 / math.sqrt(WIN)
    rows = jnp.concatenate(
        [u_ref[r, :, w * WIN : (w + 1) * WIN] for r, w in groups], axis=0
    )
    spectrum = jnp.dot(rows, forward_ref[...], preferred_element_type=jnp.float32) * scale
    block = lambda g: slice(g * sources, (g + 1) * sources)
    field = jnp.concatenate(
        [
            jnp.concatenate([spectrum[block(g), :WIN], spectrum[block(g), WIN:]], axis=0)
            for g in range(len(groups))
        ],
        axis=1,
    )
    coeffs = mix((mfh_ref[...], mfl_ref[...]), field)
    real_part = coeffs[:sources]
    imag_part = coeffs[sources:]
    limit = limit_ref[...]
    magnitude = jnp.sqrt(real_part * real_part + imag_part * imag_part)
    factor = jnp.maximum(magnitude - limit, 0.0) / jnp.maximum(magnitude, limit)
    kept = jnp.concatenate([real_part * factor, imag_part * factor], axis=0)
    back = mix((mih_ref[...], mil_ref[...]), kept)
    lanes = lambda g: slice(g * WIN, (g + 1) * WIN)
    joined = jnp.concatenate(
        [
            jnp.concatenate([back[:sources, lanes(g)], back[sources:, lanes(g)]], axis=1)
            for g in range(len(groups))
        ],
        axis=0,
    )
    joined_high, joined_low = split(joined)
    restored = jnp.dot(
        jnp.concatenate([joined_high, joined_low, joined_high], axis=1),
        inverse_ref[...],
        preferred_element_type=jnp.float32,
    )
    for g, (r, w) in enumerate(groups):
        out_ref[r, :, w * WIN : (w + 1) * WIN] = restored[block(g)].astype(out_ref.dtype)


def blend_residual(rec_ref, est_ref, before_ref, after_ref, shift_ref, pair_ref, last, res_ref):
    receivers, experiments, width = rec_ref.shape
    shift = shift_ref[...]
    lane = lax.broadcasted_iota(jnp.int32, (experiments, width), 1)
    drop = jnp.logical_and(lane >= width - BLK, last)
    for r in range(receivers):
        moved = jnp.concatenate([before_ref[r], est_ref[r], after_ref[r]], axis=1).astype(jnp.float32)
        full = moved.shape[1]
        for bit in range((BLK - 1).bit_length()):
            amount = 1 << bit
            moved = jnp.where((shift & amount) != 0, pltpu.roll(moved, amount, 1), moved)
        summed = jnp.dot(
            pair_ref[...], moved[:, full - width :].astype(jnp.bfloat16),
            preferred_element_type=jnp.float32,
        )
        residual = (rec_ref[r] - summed).astype(res_ref.dtype)
        res_ref[r] = jnp.where(drop, jnp.zeros_like(residual), residual)


def spread_update(res_ref, shift_ref, dup_ref, est_ref, u_ref, last=None):
    receivers, sources, samples = u_ref.shape
    experiments, width = res_ref.shape[1:]
    shift = shift_ref[...]
    for r in range(receivers):
        residual = res_ref[r]
        if last is not None:
            lane = lax.broadcasted_iota(jnp.int32, (experiments, width), 1)
            drop = jnp.logical_and(lane >= samples, last)
            residual = jnp.where(drop, jnp.zeros_like(residual), residual).astype(jnp.bfloat16)
        moved = jnp.dot(dup_ref[...], residual, preferred_element_type=jnp.float32)
        for bit in range((BLK - 1).bit_length()):
            amount = 1 << bit
            rolled = pltpu.roll(moved, width - amount, 1)
            moved = jnp.where((shift & amount) != 0, rolled, moved)
        value = RELAX * moved[:, :samples]
        if est_ref is not None:
            value = est_ref[r].astype(jnp.float32) + value
        u_ref[r] = value.astype(u_ref.dtype)


def pairing(experiments):
    source = np.arange(experiments * SRC_EXP)[:, None] // SRC_EXP
    return (source == np.arange(experiments)[None, :]).astype(ml_dtypes.bfloat16)


def spread_inputs(residual, delays):
    return [residual, delays.reshape(-1, 1), jnp.asarray(pairing(residual.shape[1]))]


def filter_kernel(u_ref, *refs):
    filter_block(u_ref, 0, u_ref.shape[0], refs[:7], refs[7])


def filter_halo_kernel(stages, res_ref, shift_ref, dup_ref, *refs):
    tables = refs[:7]
    out_ref, before_ref, after_ref, u_ref, send_sem, recv_sem = refs[7:]
    samples = u_ref.shape[2]
    shot = lax.axis_index("shot")
    row = lax.axis_index("tm")
    has_prev = row > 0
    has_next = row < stages - 1
    barrier = pltpu.get_barrier_semaphore()
    mesh_id = pl.DeviceIdType.MESH

    @pl.when(has_prev)
    def _():
        pl.semaphore_signal(barrier, 1, device_id=(shot, row - 1), device_id_type=mesh_id)

    @pl.when(has_next)
    def _():
        pl.semaphore_signal(barrier, 1, device_id=(shot, row + 1), device_id_type=mesh_id)

    spread_update(res_ref, shift_ref, dup_ref, None, u_ref, jnp.logical_not(has_next))
    filter_block(u_ref, 0, u_ref.shape[0], tables, out_ref)
    pl.semaphore_wait(barrier, has_prev.astype(jnp.int32) + has_next.astype(jnp.int32))

    def to_prev():
        return pltpu.make_async_remote_copy(
            src_ref=out_ref.at[:, :, pl.ds(0, BLK)],
            dst_ref=after_ref,
            send_sem=send_sem.at[0],
            recv_sem=recv_sem.at[0],
            device_id=(shot, row - 1),
            device_id_type=mesh_id,
        )

    def to_next():
        return pltpu.make_async_remote_copy(
            src_ref=out_ref.at[:, :, pl.ds(samples - BLK, BLK)],
            dst_ref=before_ref,
            send_sem=send_sem.at[1],
            recv_sem=recv_sem.at[1],
            device_id=(shot, row + 1),
            device_id_type=mesh_id,
        )

    pl.when(has_prev)(lambda: to_prev().start())
    pl.when(has_next)(lambda: to_next().start())

    @pl.when(has_prev)
    def _():
        to_prev().wait_send()
        to_next().wait_recv()

    @pl.when(has_next)
    def _():
        to_next().wait_send()
        to_prev().wait_recv()


def filter_with_halos(residual, delays, limits, tables):
    forward, inverse, mix_forward, mix_inverse = tables
    receivers = residual.shape[0]
    sources = delays.size
    samples = residual.shape[2] - BLK
    stages = lax.axis_size("tm")
    vmem = pl.BlockSpec(memory_space=pltpu.VMEM)
    anywhere = pl.BlockSpec(memory_space=pl.ANY)
    edge = jax.ShapeDtypeStruct((receivers, sources, BLK), jnp.bfloat16)
    return pl.pallas_call(
        functools.partial(filter_halo_kernel, stages),
        in_specs=[vmem] * 10,
        out_specs=(vmem, anywhere, anywhere),
        out_shape=(jax.ShapeDtypeStruct((receivers, sources, samples), jnp.bfloat16), edge, edge),
        scratch_shapes=[
            pltpu.VMEM((receivers, sources, samples), jnp.bfloat16),
            pltpu.SemaphoreType.DMA((2,)),
            pltpu.SemaphoreType.DMA((2,)),
        ],
        compiler_params=pltpu.CompilerParams(
            collective_id=3, has_side_effects=True, vmem_limit_bytes=48 * 1024 * 1024
        ),
    )(
        *spread_inputs(residual, delays),
        forward, inverse, *mix_forward, *mix_inverse, limits.reshape(sources, 1),
    )


def filter_send_kernel(
    count, stages, halves, est_ref, before_ref, after_ref, rec_ref, pair_ref, shift_ref, dup_ref, *refs
):
    tables = refs[:7]
    out_ref, done_ref, u_ref, res_ref, send_sem, recv_sem, own_sem = refs[7:]
    receivers, sources, samples = u_ref.shape
    own = sources // count
    per = receivers // halves
    me = lax.axis_index("shot")
    row = lax.axis_index("tm")
    barrier = pltpu.get_barrier_semaphore()

    def greet(step, carry):
        peer = lax.rem(me + step, count)
        pl.semaphore_signal(barrier, 1, device_id=(peer, row), device_id_type=pl.DeviceIdType.MESH)
        return carry

    lax.fori_loop(1, count, greet, 0)
    last = lax.axis_index("tm") == stages - 1
    blend_residual(rec_ref, est_ref, before_ref, after_ref, shift_ref, pair_ref, last, res_ref)
    spread_update(res_ref, shift_ref, dup_ref, est_ref, u_ref)

    def remote(half, peer, sender):
        return pltpu.make_async_remote_copy(
            src_ref=done_ref.at[pl.ds(half * per, per), pl.ds(peer * own, own), :],
            dst_ref=out_ref.at[pl.ds(sender * receivers + half * per, per), :, :],
            send_sem=send_sem.at[half, peer],
            recv_sem=recv_sem.at[half, sender],
            device_id=(peer, row),
            device_id_type=pl.DeviceIdType.MESH,
        )

    locals_ = []
    for half in range(halves):
        filter_block(u_ref, half * per, per, tables, done_ref)
        if half == 0:
            pl.semaphore_wait(barrier, count - 1)
        mine = pltpu.make_async_copy(
            done_ref.at[pl.ds(half * per, per), pl.ds(me * own, own), :],
            out_ref.at[pl.ds(me * receivers + half * per, per), :, :],
            own_sem.at[half],
        )
        mine.start()
        locals_.append(mine)

        def send(step, carry, half=half):
            remote(half, lax.rem(me + step, count), me).start()
            return carry

        lax.fori_loop(1, count, send, 0)

    for half in range(halves):

        def finish(step, carry, half=half):
            peer = lax.rem(me + step, count)
            remote(half, peer, me).wait_send()
            remote(half, me, peer).wait_recv()
            return carry

        lax.fori_loop(1, count, finish, 0)
        locals_[half].wait()


def filter_and_send(estimate, before, after, records, delays, limits, tables):
    forward, inverse, mix_forward, mix_inverse = tables
    receivers, sources, samples = estimate.shape
    count = lax.axis_size("shot")
    halves = 2
    vmem = pl.BlockSpec(memory_space=pltpu.VMEM)
    return pl.pallas_call(
        functools.partial(filter_send_kernel, count, lax.axis_size("tm"), halves),
        in_specs=[vmem] * 14,
        out_specs=pl.BlockSpec(memory_space=pl.ANY),
        out_shape=jax.ShapeDtypeStruct(
            (receivers * count, sources // count, samples), jnp.bfloat16
        ),
        scratch_shapes=[
            pltpu.VMEM(estimate.shape, jnp.bfloat16),
            pltpu.VMEM(estimate.shape, jnp.bfloat16),
            pltpu.VMEM(records.shape, jnp.bfloat16),
            pltpu.SemaphoreType.DMA((halves, count)),
            pltpu.SemaphoreType.DMA((halves, count)),
            pltpu.SemaphoreType.DMA((halves,)),
        ],
        compiler_params=pltpu.CompilerParams(
            collective_id=2, has_side_effects=True, vmem_limit_bytes=48 * 1024 * 1024
        ),
    )(
        estimate,
        before,
        after,
        records,
        jnp.asarray(np.ascontiguousarray(pairing(records.shape[1]).T)),
        *spread_inputs(records, delays)[1:],
        forward, inverse, *mix_forward, *mix_inverse, limits.reshape(sources, 1),
    )


def coherence(gathers, limits, tables):
    forward, inverse, mix_forward, mix_inverse = tables
    receivers, sources, samples = gathers.shape
    vmem = pl.BlockSpec(memory_space=pltpu.VMEM)
    return pl.pallas_call(
        filter_kernel,
        in_specs=[vmem] * 8,
        out_specs=vmem,
        out_shape=jax.ShapeDtypeStruct(gathers.shape, jnp.bfloat16),
        compiler_params=pltpu.CompilerParams(vmem_limit_bytes=48 * 1024 * 1024),
    )(gathers, forward, inverse, *mix_forward, *mix_inverse, limits.reshape(sources, 1))


def exchange_kernel(count, outgoing, incoming, src_ref, out_ref, send_sem, recv_sem, own_sem):
    me = lax.axis_index("shot")
    row = lax.axis_index("tm")
    barrier = pltpu.get_barrier_semaphore()

    def greet(step, carry):
        peer = lax.rem(me + step, count)
        pl.semaphore_signal(barrier, 1, device_id=(peer, row), device_id_type=pl.DeviceIdType.MESH)
        return carry

    lax.fori_loop(1, count, greet, 0)
    pl.semaphore_wait(barrier, count - 1)
    own = pltpu.make_async_copy(src_ref.at[outgoing(me)], out_ref.at[incoming(me)], own_sem)
    own.start()

    def remote(peer, sender):
        return pltpu.make_async_remote_copy(
            src_ref=src_ref.at[outgoing(peer)],
            dst_ref=out_ref.at[incoming(sender)],
            send_sem=send_sem.at[peer],
            recv_sem=recv_sem.at[sender],
            device_id=(peer, row),
            device_id_type=pl.DeviceIdType.MESH,
        )

    def send(step, carry):
        remote(lax.rem(me + step, count), me).start()
        return carry

    lax.fori_loop(1, count, send, 0)

    def finish(step, carry):
        peer = lax.rem(me + step, count)
        remote(peer, me).wait_send()
        remote(me, peer).wait_recv()
        return carry

    lax.fori_loop(1, count, finish, 0)
    own.wait()


def exchange(value, out_shape, outgoing, incoming, tag):
    count = lax.axis_size("shot")
    anywhere = pl.BlockSpec(memory_space=pl.ANY)
    return pl.pallas_call(
        functools.partial(exchange_kernel, count, outgoing, incoming),
        in_specs=[anywhere],
        out_specs=anywhere,
        out_shape=jax.ShapeDtypeStruct(out_shape, value.dtype),
        scratch_shapes=[
            pltpu.SemaphoreType.DMA((count,)),
            pltpu.SemaphoreType.DMA((count,)),
            pltpu.SemaphoreType.DMA,
        ],
        compiler_params=pltpu.CompilerParams(collective_id=tag, has_side_effects=True),
    )(value)


def to_sources(estimate):
    receivers, sources, samples = estimate.shape
    count = lax.axis_size("shot")
    own = sources // count
    return exchange(
        estimate,
        (receivers * count, own, samples),
        lambda peer: (slice(None), pl.ds(peer * own, own), slice(None)),
        lambda sender: (pl.ds(sender * receivers, receivers), slice(None), slice(None)),
        0,
    )


def receive_kernel(count, stages, src_ref, out_ref, halo_ref, send_sem, recv_sem, edge_sem, own_sem):
    part, own, samples = out_ref.shape[0], src_ref.shape[1], src_ref.shape[2]
    me = lax.axis_index("shot")
    row = lax.axis_index("tm")
    has_prev = row > 0
    has_next = row < stages - 1
    mesh_id = pl.DeviceIdType.MESH
    barrier = pltpu.get_barrier_semaphore()

    def greet(step, carry):
        peer = lax.rem(me + step, count)
        pl.semaphore_signal(barrier, 1, device_id=(peer, row), device_id_type=mesh_id)
        return carry

    lax.fori_loop(1, count, greet, 0)

    @pl.when(has_prev)
    def _():
        pl.semaphore_signal(barrier, 1, device_id=(me, row - 1), device_id_type=mesh_id)

    @pl.when(has_next)
    def _():
        pl.semaphore_signal(barrier, 1, device_id=(me, row + 1), device_id_type=mesh_id)

    pl.semaphore_wait(
        barrier, count - 1 + has_prev.astype(jnp.int32) + has_next.astype(jnp.int32)
    )
    body = (slice(None), pl.ds(me * own, own), pl.ds(0, samples))
    tail = (slice(None), pl.ds(me * own, own), pl.ds(samples, BLK))

    def chunk(peer, sender, stage):
        source = src_ref if stage == 0 else halo_ref
        target = body if stage == 0 else tail
        target = (target[0], pl.ds(sender * own, own), target[2])
        return pltpu.make_async_remote_copy(
            src_ref=source.at[pl.ds(peer * part, part)],
            dst_ref=out_ref.at[target],
            send_sem=send_sem.at[stage, peer],
            recv_sem=recv_sem.at[stage, sender],
            device_id=(peer, row),
            device_id_type=mesh_id,
        )

    mine = pltpu.make_async_copy(src_ref.at[pl.ds(me * part, part)], out_ref.at[body], own_sem.at[0])
    mine.start()

    def send_body(step, carry):
        chunk(lax.rem(me + step, count), me, 0).start()
        return carry

    lax.fori_loop(1, count, send_body, 0)

    def edge(target_row):
        return pltpu.make_async_remote_copy(
            src_ref=src_ref.at[:, :, pl.ds(0, BLK)],
            dst_ref=halo_ref,
            send_sem=edge_sem.at[0],
            recv_sem=edge_sem.at[1],
            device_id=(me, target_row),
            device_id_type=mesh_id,
        )

    pl.when(has_prev)(lambda: edge(row - 1).start())

    @pl.when(has_next)
    def _():
        edge(row + 1).wait_recv()
        theirs = pltpu.make_async_copy(
            halo_ref.at[pl.ds(me * part, part)], out_ref.at[tail], own_sem.at[1]
        )
        theirs.start()

        def send_tail(step, carry):
            chunk(lax.rem(me + step, count), me, 1).start()
            return carry

        lax.fori_loop(1, count, send_tail, 0)

        def finish_tail(step, carry):
            peer = lax.rem(me + step, count)
            chunk(peer, me, 1).wait_send()
            chunk(me, peer, 1).wait_recv()
            return carry

        lax.fori_loop(1, count, finish_tail, 0)
        theirs.wait()

    pl.when(has_prev)(lambda: edge(row - 1).wait_send())

    def finish_body(step, carry):
        peer = lax.rem(me + step, count)
        chunk(peer, me, 0).wait_send()
        chunk(me, peer, 0).wait_recv()
        return carry

    lax.fori_loop(1, count, finish_body, 0)
    mine.wait()


def to_receivers(records):
    receivers, own, samples = records.shape
    count = lax.axis_size("shot")
    part = receivers // count
    return pl.pallas_call(
        functools.partial(receive_kernel, count, lax.axis_size("tm")),
        in_specs=[pl.BlockSpec(memory_space=pl.ANY)],
        out_specs=pl.BlockSpec(memory_space=pl.ANY),
        out_shape=jax.ShapeDtypeStruct((part, own * count, samples + BLK), records.dtype),
        scratch_shapes=[
            pltpu.VMEM((receivers, own, BLK), records.dtype),
            pltpu.SemaphoreType.DMA((2, count)),
            pltpu.SemaphoreType.DMA((2, count)),
            pltpu.SemaphoreType.DMA((2,)),
            pltpu.SemaphoreType.DMA((2,)),
        ],
        compiler_params=pltpu.CompilerParams(collective_id=1, has_side_effects=True),
    )(records)


def local(blended, delays, thresholds):
    tables = filter_tables()
    extended = to_receivers(blended)
    row = lax.axis_index("tm")
    estimate, before, after = filter_with_halos(extended, delays, thresholds[0], tables)
    before = jnp.where(row == 0, jnp.zeros_like(before), before)
    last = row == lax.axis_size("tm") - 1
    after = jnp.where(last, jnp.zeros_like(after), after)
    return filter_and_send(estimate, before, after, extended, delays, thresholds[1], tables)


def solution(mesh):
    return jax.shard_map(
        local,
        mesh=mesh,
        in_specs=(P(None, "shot", "tm"), P(), P()),
        out_specs=P(None, "shot", "tm"),
        check_vma=False,
    )
```

```python
import functools
import math

import jax
import ml_dtypes
import numpy as np
import jax.numpy as jnp
from jax import lax
from jax.experimental import pallas as pl
from jax.experimental.pallas import tpu as pltpu
from jax.sharding import PartitionSpec as P

SRC = 64
SRC_EXP = 2
WIN = 256
BLK = 128
ITERS = 2


RELAX = 0.5


def shifted(array, axis, by):
    count = lax.axis_size(axis)
    pairs = [(i, i + by) for i in range(count) if 0 <= i + by < count]
    return lax.ppermute(array, axis, pairs)


def blend(estimate, earlier, own_delays):
    receivers, sources, samples = estimate.shape
    blocks = samples // BLK
    experiments = sources // SRC_EXP
    upper = estimate.reshape(receivers, sources, blocks, BLK)
    shifts = own_delays.reshape(-1)
    row_index = jnp.arange(BLK, dtype=jnp.int32)[None, :, None]
    column_index = jnp.arange(BLK, dtype=jnp.int32)[None, None, :]
    select_same = (row_index == column_index - shifts[:, None, None]).astype(jnp.bfloat16)
    select_prior = (row_index == BLK + column_index - shifts[:, None, None]).astype(jnp.bfloat16)
    same = jnp.einsum("rsnb,sbi->rsni", upper, select_same, preferred_element_type=jnp.float32)
    onward = jnp.einsum("rsnb,sbi->rsni", upper, select_prior, preferred_element_type=jnp.float32)
    edge_part = jnp.einsum(
        "rsb,sbi->rsi", earlier, select_prior, preferred_element_type=jnp.float32
    )
    same = jnp.sum(same.reshape(receivers, experiments, SRC_EXP, blocks, BLK), axis=2)
    onward = jnp.sum(onward.reshape(receivers, experiments, SRC_EXP, blocks, BLK), axis=2)
    edge_part = jnp.sum(edge_part.reshape(receivers, experiments, SRC_EXP, BLK), axis=2)
    carried = jnp.concatenate([edge_part[:, :, None], onward[:, :, : blocks - 1]], axis=2)
    return (same + carried).reshape(receivers, experiments, samples)


def spread(residual, later, own_delays):
    receivers, experiments, samples = residual.shape
    blocks = samples // BLK
    lower = residual.reshape(receivers, experiments, blocks, BLK)
    row_index = jnp.arange(BLK, dtype=jnp.int32)[None, None, :, None]
    column_index = jnp.arange(BLK, dtype=jnp.int32)[None, None, None, :]
    select_same = (row_index == column_index + own_delays[:, :, None, None]).astype(jnp.bfloat16)
    select_next = (row_index + BLK == column_index + own_delays[:, :, None, None]).astype(
        jnp.bfloat16
    )
    same = jnp.einsum("rena,ekai->rekni", lower, select_same, preferred_element_type=jnp.float32)
    backward = jnp.einsum(
        "rena,ekai->rekni", lower, select_next, preferred_element_type=jnp.float32
    )
    edge_part = jnp.einsum("rea,ekai->reki", later, select_next, preferred_element_type=jnp.float32)
    carried = jnp.concatenate([backward[:, :, :, 1:], edge_part[:, :, :, None]], axis=3)
    return (same + carried).reshape(receivers, experiments * SRC_EXP, samples)


def split(value):
    high = value.astype(jnp.bfloat16)
    return high, (value - high.astype(jnp.float32)).astype(jnp.bfloat16)


def exact_split(value):
    high = value.astype(ml_dtypes.bfloat16)
    low = (value - high.astype(np.float64)).astype(ml_dtypes.bfloat16)
    return jnp.asarray(high), jnp.asarray(low)


def filter_tables():
    turn = lambda n: (np.arange(n)[:, None] * np.arange(n)[None, :] % n) * (2.0 * np.pi / n)
    time_turn = turn(WIN)
    forward = jnp.asarray(
        np.concatenate([np.cos(time_turn), -np.sin(time_turn)], axis=1).astype(ml_dtypes.bfloat16)
    )
    inverse_high, inverse_low = exact_split(
        np.concatenate([np.cos(time_turn), -np.sin(time_turn)], axis=0) / math.sqrt(WIN)
    )
    inverse = jnp.concatenate([inverse_high, inverse_high, inverse_low], axis=0)
    source_turn = turn(SRC)
    cos_source = np.cos(source_turn) / math.sqrt(SRC)
    sin_source = np.sin(source_turn) / math.sqrt(SRC)
    mix_forward = exact_split(np.block([[cos_source, sin_source], [-sin_source, cos_source]]))
    mix_inverse = exact_split(np.block([[cos_source, -sin_source], [sin_source, cos_source]]))
    return forward, inverse, mix_forward, mix_inverse


def mix(table, value):
    table_high, table_low = table
    value_high, value_low = split(value)
    stacked = jnp.concatenate([value_high, value_low, value_high], axis=0)
    joined = jnp.concatenate([table_high, table_high, table_low], axis=1)
    return jnp.dot(joined, stacked, preferred_element_type=jnp.float32)


def filter_block(u_ref, first, count, tables, out_ref):
    forward_ref, inverse_ref, mfh_ref, mfl_ref, mih_ref, mil_ref, limit_ref = tables
    sources, samples = u_ref.shape[1:]
    windows = samples // WIN
    groups = [(r, w) for r in range(first, first + count) for w in range(windows)]
    scale = 1.0 / math.sqrt(WIN)
    rows = jnp.concatenate(
        [u_ref[r, :, w * WIN : (w + 1) * WIN] for r, w in groups], axis=0
    )
    spectrum = jnp.dot(rows, forward_ref[...], preferred_element_type=jnp.float32) * scale
    block = lambda g: slice(g * sources, (g + 1) * sources)
    field = jnp.concatenate(
        [
            jnp.concatenate([spectrum[block(g), :WIN], spectrum[block(g), WIN:]], axis=0)
            for g in range(len(groups))
        ],
        axis=1,
    )
    coeffs = mix((mfh_ref[...], mfl_ref[...]), field)
    real_part = coeffs[:sources]
    imag_part = coeffs[sources:]
    limit = limit_ref[...]
    magnitude = jnp.sqrt(real_part * real_part + imag_part * imag_part)
    factor = jnp.maximum(magnitude - limit, 0.0) / jnp.maximum(magnitude, limit)
    kept = jnp.concatenate([real_part * factor, imag_part * factor], axis=0)
    back = mix((mih_ref[...], mil_ref[...]), kept)
    lanes = lambda g: slice(g * WIN, (g + 1) * WIN)
    joined = jnp.concatenate(
        [
            jnp.concatenate([back[:sources, lanes(g)], back[sources:, lanes(g)]], axis=1)
            for g in range(len(groups))
        ],
        axis=0,
    )
    joined_high, joined_low = split(joined)
    restored = jnp.dot(
        jnp.concatenate([joined_high, joined_low, joined_high], axis=1),
        inverse_ref[...],
        preferred_element_type=jnp.float32,
    )
    for g, (r, w) in enumerate(groups):
        out_ref[r, :, w * WIN : (w + 1) * WIN] = restored[block(g)].astype(out_ref.dtype)


def pairs(rows, cols, transpose):
    row = lax.broadcasted_iota(jnp.int32, (rows, cols), 0)
    col = lax.broadcasted_iota(jnp.int32, (rows, cols), 1)
    hit = (col // SRC_EXP == row) if transpose else (row // SRC_EXP == col)
    return jnp.where(hit, 1.0, 0.0).astype(jnp.bfloat16)


def blend_residual(rec_ref, est_ref, before_ref, after_ref, shift_ref, last, res_ref, rows):
    receivers, experiments, width = rec_ref.shape
    pair = pairs(experiments, est_ref.shape[1], True)
    shift = shift_ref[...]
    lane = lax.broadcasted_iota(jnp.int32, (experiments, width), 1)
    drop = jnp.logical_and(lane >= width - BLK, last)
    for r in rows:
        moved = jnp.concatenate([before_ref[r], est_ref[r], after_ref[r]], axis=1).astype(jnp.float32)
        full = moved.shape[1]
        for bit in range((BLK - 1).bit_length()):
            amount = 1 << bit
            moved = jnp.where((shift & amount) != 0, pltpu.roll(moved, amount, 1), moved)
        summed = jnp.dot(
            pair, moved[:, full - width :].astype(jnp.bfloat16),
            preferred_element_type=jnp.float32,
        )
        residual = (rec_ref[r] - summed).astype(res_ref.dtype)
        res_ref[r] = jnp.where(drop, jnp.zeros_like(residual), residual)


def spread_update(res_ref, shift_ref, est_ref, u_ref, rows, last=None):
    receivers, sources, samples = u_ref.shape
    experiments, width = res_ref.shape[1:]
    shift = shift_ref[...]
    dup = pairs(sources, experiments, False)
    for r in rows:
        residual = res_ref[r]
        if last is not None:
            lane = lax.broadcasted_iota(jnp.int32, (experiments, width), 1)
            drop = jnp.logical_and(lane >= samples, last)
            residual = jnp.where(drop, jnp.zeros_like(residual), residual).astype(jnp.bfloat16)
        moved = jnp.dot(dup, residual, preferred_element_type=jnp.float32)
        for bit in range((BLK - 1).bit_length()):
            amount = 1 << bit
            rolled = pltpu.roll(moved, width - amount, 1)
            moved = jnp.where((shift & amount) != 0, rolled, moved)
        value = RELAX * moved[:, :samples]
        if est_ref is not None:
            value = est_ref[r].astype(jnp.float32) + value
        u_ref[r] = value.astype(u_ref.dtype)


def spread_inputs(residual, delays):
    return [residual, delays.reshape(-1, 1)]


def filter_kernel(u_ref, *refs):
    filter_block(u_ref, 0, u_ref.shape[0], refs[:7], refs[7])


def filter_halo_kernel(stages, res_ref, shift_ref, *refs):
    tables = refs[:7]
    out_ref, before_ref, after_ref, u_ref, send_sem, recv_sem = refs[7:]
    samples = u_ref.shape[2]
    shot = lax.axis_index("shot")
    row = lax.axis_index("tm")
    has_prev = row > 0
    has_next = row < stages - 1
    barrier = pltpu.get_barrier_semaphore()
    mesh_id = pl.DeviceIdType.MESH

    @pl.when(has_prev)
    def _():
        pl.semaphore_signal(barrier, 1, device_id=(shot, row - 1), device_id_type=mesh_id)

    @pl.when(has_next)
    def _():
        pl.semaphore_signal(barrier, 1, device_id=(shot, row + 1), device_id_type=mesh_id)

    spread_update(res_ref, shift_ref, None, u_ref, range(u_ref.shape[0]), jnp.logical_not(has_next))
    filter_block(u_ref, 0, u_ref.shape[0], tables, out_ref)
    pl.semaphore_wait(barrier, has_prev.astype(jnp.int32) + has_next.astype(jnp.int32))

    def to_prev():
        return pltpu.make_async_remote_copy(
            src_ref=out_ref.at[:, :, pl.ds(0, BLK)],
            dst_ref=after_ref,
            send_sem=send_sem.at[0],
            recv_sem=recv_sem.at[0],
            device_id=(shot, row - 1),
            device_id_type=mesh_id,
        )

    def to_next():
        return pltpu.make_async_remote_copy(
            src_ref=out_ref.at[:, :, pl.ds(samples - BLK, BLK)],
            dst_ref=before_ref,
            send_sem=send_sem.at[1],
            recv_sem=recv_sem.at[1],
            device_id=(shot, row + 1),
            device_id_type=mesh_id,
        )

    pl.when(has_prev)(lambda: to_prev().start())
    pl.when(has_next)(lambda: to_next().start())

    @pl.when(has_prev)
    def _():
        to_prev().wait_send()
        to_next().wait_recv()

    @pl.when(has_next)
    def _():
        to_next().wait_send()
        to_prev().wait_recv()


def filter_with_halos(residual, delays, limits, tables):
    forward, inverse, mix_forward, mix_inverse = tables
    receivers = residual.shape[0]
    sources = delays.size
    samples = residual.shape[2] - BLK
    stages = lax.axis_size("tm")
    vmem = pl.BlockSpec(memory_space=pltpu.VMEM)
    anywhere = pl.BlockSpec(memory_space=pl.ANY)
    edge = jax.ShapeDtypeStruct((receivers, sources, BLK), jnp.bfloat16)
    return pl.pallas_call(
        functools.partial(filter_halo_kernel, stages),
        in_specs=[vmem] * 9,
        out_specs=(vmem, anywhere, anywhere),
        out_shape=(jax.ShapeDtypeStruct((receivers, sources, samples), jnp.bfloat16), edge, edge),
        scratch_shapes=[
            pltpu.VMEM((receivers, sources, samples), jnp.bfloat16),
            pltpu.SemaphoreType.DMA((2,)),
            pltpu.SemaphoreType.DMA((2,)),
        ],
        compiler_params=pltpu.CompilerParams(
            collective_id=3, has_side_effects=True, vmem_limit_bytes=48 * 1024 * 1024
        ),
    )(
        *spread_inputs(residual, delays),
        forward, inverse, *mix_forward, *mix_inverse, limits.reshape(sources, 1),
    )


def filter_send_kernel(
    count, stages, halves, est_ref, before_ref, after_ref, rec_ref, shift_ref, *refs
):
    tables = refs[:7]
    out_ref, done_ref, u_ref, res_ref, send_sem, recv_sem, own_sem = refs[7:]
    receivers, sources, samples = u_ref.shape
    own = sources // count
    per = receivers // halves
    me = lax.axis_index("shot")
    row = lax.axis_index("tm")
    barrier = pltpu.get_barrier_semaphore()

    def greet(step, carry):
        peer = lax.rem(me + step, count)
        pl.semaphore_signal(barrier, 1, device_id=(peer, row), device_id_type=pl.DeviceIdType.MESH)
        return carry

    lax.fori_loop(1, count, greet, 0)
    last = lax.axis_index("tm") == stages - 1

    def remote(half, peer, sender):
        return pltpu.make_async_remote_copy(
            src_ref=done_ref.at[pl.ds(half * per, per), pl.ds(peer * own, own), :],
            dst_ref=out_ref.at[pl.ds(sender * receivers + half * per, per), :, :],
            send_sem=send_sem.at[half, peer],
            recv_sem=recv_sem.at[half, sender],
            device_id=(peer, row),
            device_id_type=pl.DeviceIdType.MESH,
        )

    locals_ = []
    for half in range(halves):
        rows = range(half * per, (half + 1) * per)
        blend_residual(rec_ref, est_ref, before_ref, after_ref, shift_ref, last, res_ref, rows)
        spread_update(res_ref, shift_ref, est_ref, u_ref, rows)
        filter_block(u_ref, half * per, per, tables, done_ref)
        if half == 0:
            pl.semaphore_wait(barrier, count - 1)
        mine = pltpu.make_async_copy(
            done_ref.at[pl.ds(half * per, per), pl.ds(me * own, own), :],
            out_ref.at[pl.ds(me * receivers + half * per, per), :, :],
            own_sem.at[half],
        )
        mine.start()
        locals_.append(mine)

        def send(step, carry, half=half):
            remote(half, lax.rem(me + step, count), me).start()
            return carry

        lax.fori_loop(1, count, send, 0)

    for half in range(halves):

        def finish(step, carry, half=half):
            peer = lax.rem(me + step, count)
            remote(half, peer, me).wait_send()
            remote(half, me, peer).wait_recv()
            return carry

        lax.fori_loop(1, count, finish, 0)
        locals_[half].wait()


def filter_and_send(estimate, before, after, records, delays, limits, tables):
    forward, inverse, mix_forward, mix_inverse = tables
    receivers, sources, samples = estimate.shape
    count = lax.axis_size("shot")
    halves = 2
    vmem = pl.BlockSpec(memory_space=pltpu.VMEM)
    return pl.pallas_call(
        functools.partial(filter_send_kernel, count, lax.axis_size("tm"), halves),
        in_specs=[vmem] * 12,
        out_specs=pl.BlockSpec(memory_space=pl.ANY),
        out_shape=jax.ShapeDtypeStruct(
            (receivers * count, sources // count, samples), jnp.bfloat16
        ),
        scratch_shapes=[
            pltpu.VMEM(estimate.shape, jnp.bfloat16),
            pltpu.VMEM(estimate.shape, jnp.bfloat16),
            pltpu.VMEM(records.shape, jnp.bfloat16),
            pltpu.SemaphoreType.DMA((halves, count)),
            pltpu.SemaphoreType.DMA((halves, count)),
            pltpu.SemaphoreType.DMA((halves,)),
        ],
        compiler_params=pltpu.CompilerParams(
            collective_id=2, has_side_effects=True, vmem_limit_bytes=48 * 1024 * 1024
        ),
    )(
        estimate,
        before,
        after,
        records,
        *spread_inputs(records, delays)[1:],
        forward, inverse, *mix_forward, *mix_inverse, limits.reshape(sources, 1),
    )


def coherence(gathers, limits, tables):
    forward, inverse, mix_forward, mix_inverse = tables
    receivers, sources, samples = gathers.shape
    vmem = pl.BlockSpec(memory_space=pltpu.VMEM)
    return pl.pallas_call(
        filter_kernel,
        in_specs=[vmem] * 8,
        out_specs=vmem,
        out_shape=jax.ShapeDtypeStruct(gathers.shape, jnp.bfloat16),
        compiler_params=pltpu.CompilerParams(vmem_limit_bytes=48 * 1024 * 1024),
    )(gathers, forward, inverse, *mix_forward, *mix_inverse, limits.reshape(sources, 1))


def exchange_kernel(count, outgoing, incoming, src_ref, out_ref, send_sem, recv_sem, own_sem):
    me = lax.axis_index("shot")
    row = lax.axis_index("tm")
    barrier = pltpu.get_barrier_semaphore()

    def greet(step, carry):
        peer = lax.rem(me + step, count)
        pl.semaphore_signal(barrier, 1, device_id=(peer, row), device_id_type=pl.DeviceIdType.MESH)
        return carry

    lax.fori_loop(1, count, greet, 0)
    pl.semaphore_wait(barrier, count - 1)
    own = pltpu.make_async_copy(src_ref.at[outgoing(me)], out_ref.at[incoming(me)], own_sem)
    own.start()

    def remote(peer, sender):
        return pltpu.make_async_remote_copy(
            src_ref=src_ref.at[outgoing(peer)],
            dst_ref=out_ref.at[incoming(sender)],
            send_sem=send_sem.at[peer],
            recv_sem=recv_sem.at[sender],
            device_id=(peer, row),
            device_id_type=pl.DeviceIdType.MESH,
        )

    def send(step, carry):
        remote(lax.rem(me + step, count), me).start()
        return carry

    lax.fori_loop(1, count, send, 0)

    def finish(step, carry):
        peer = lax.rem(me + step, count)
        remote(peer, me).wait_send()
        remote(me, peer).wait_recv()
        return carry

    lax.fori_loop(1, count, finish, 0)
    own.wait()


def exchange(value, out_shape, outgoing, incoming, tag):
    count = lax.axis_size("shot")
    anywhere = pl.BlockSpec(memory_space=pl.ANY)
    return pl.pallas_call(
        functools.partial(exchange_kernel, count, outgoing, incoming),
        in_specs=[anywhere],
        out_specs=anywhere,
        out_shape=jax.ShapeDtypeStruct(out_shape, value.dtype),
        scratch_shapes=[
            pltpu.SemaphoreType.DMA((count,)),
            pltpu.SemaphoreType.DMA((count,)),
            pltpu.SemaphoreType.DMA,
        ],
        compiler_params=pltpu.CompilerParams(collective_id=tag, has_side_effects=True),
    )(value)


def to_sources(estimate):
    receivers, sources, samples = estimate.shape
    count = lax.axis_size("shot")
    own = sources // count
    return exchange(
        estimate,
        (receivers * count, own, samples),
        lambda peer: (slice(None), pl.ds(peer * own, own), slice(None)),
        lambda sender: (pl.ds(sender * receivers, receivers), slice(None), slice(None)),
        0,
    )


def receive_kernel(count, stages, src_ref, out_ref, halo_ref, send_sem, recv_sem, edge_sem, own_sem):
    part, own, samples = out_ref.shape[0], src_ref.shape[1], src_ref.shape[2]
    me = lax.axis_index("shot")
    row = lax.axis_index("tm")
    has_prev = row > 0
    has_next = row < stages - 1
    mesh_id = pl.DeviceIdType.MESH
    barrier = pltpu.get_barrier_semaphore()

    def greet(step, carry):
        peer = lax.rem(me + step, count)
        pl.semaphore_signal(barrier, 1, device_id=(peer, row), device_id_type=mesh_id)
        return carry

    lax.fori_loop(1, count, greet, 0)

    @pl.when(has_prev)
    def _():
        pl.semaphore_signal(barrier, 1, device_id=(me, row - 1), device_id_type=mesh_id)

    @pl.when(has_next)
    def _():
        pl.semaphore_signal(barrier, 1, device_id=(me, row + 1), device_id_type=mesh_id)

    pl.semaphore_wait(
        barrier, count - 1 + has_prev.astype(jnp.int32) + has_next.astype(jnp.int32)
    )
    body = (slice(None), pl.ds(me * own, own), pl.ds(0, samples))
    tail = (slice(None), pl.ds(me * own, own), pl.ds(samples, BLK))

    def chunk(peer, sender, stage):
        source = src_ref if stage == 0 else halo_ref
        target = body if stage == 0 else tail
        target = (target[0], pl.ds(sender * own, own), target[2])
        return pltpu.make_async_remote_copy(
            src_ref=source.at[pl.ds(peer * part, part)],
            dst_ref=out_ref.at[target],
            send_sem=send_sem.at[stage, peer],
            recv_sem=recv_sem.at[stage, sender],
            device_id=(peer, row),
            device_id_type=mesh_id,
        )

    mine = pltpu.make_async_copy(src_ref.at[pl.ds(me * part, part)], out_ref.at[body], own_sem.at[0])
    mine.start()

    def send_body(step, carry):
        chunk(lax.rem(me + step, count), me, 0).start()
        return carry

    lax.fori_loop(1, count, send_body, 0)

    def edge(target_row):
        return pltpu.make_async_remote_copy(
            src_ref=src_ref.at[:, :, pl.ds(0, BLK)],
            dst_ref=halo_ref,
            send_sem=edge_sem.at[0],
            recv_sem=edge_sem.at[1],
            device_id=(me, target_row),
            device_id_type=mesh_id,
        )

    pl.when(has_prev)(lambda: edge(row - 1).start())

    @pl.when(has_next)
    def _():
        edge(row + 1).wait_recv()
        theirs = pltpu.make_async_copy(
            halo_ref.at[pl.ds(me * part, part)], out_ref.at[tail], own_sem.at[1]
        )
        theirs.start()

        def send_tail(step, carry):
            chunk(lax.rem(me + step, count), me, 1).start()
            return carry

        lax.fori_loop(1, count, send_tail, 0)

        def finish_tail(step, carry):
            peer = lax.rem(me + step, count)
            chunk(peer, me, 1).wait_send()
            chunk(me, peer, 1).wait_recv()
            return carry

        lax.fori_loop(1, count, finish_tail, 0)
        theirs.wait()

    pl.when(has_prev)(lambda: edge(row - 1).wait_send())

    def finish_body(step, carry):
        peer = lax.rem(me + step, count)
        chunk(peer, me, 0).wait_send()
        chunk(me, peer, 0).wait_recv()
        return carry

    lax.fori_loop(1, count, finish_body, 0)
    mine.wait()


def to_receivers(records):
    receivers, own, samples = records.shape
    count = lax.axis_size("shot")
    part = receivers // count
    return pl.pallas_call(
        functools.partial(receive_kernel, count, lax.axis_size("tm")),
        in_specs=[pl.BlockSpec(memory_space=pl.ANY)],
        out_specs=pl.BlockSpec(memory_space=pl.ANY),
        out_shape=jax.ShapeDtypeStruct((part, own * count, samples + BLK), records.dtype),
        scratch_shapes=[
            pltpu.VMEM((receivers, own, BLK), records.dtype),
            pltpu.SemaphoreType.DMA((2, count)),
            pltpu.SemaphoreType.DMA((2, count)),
            pltpu.SemaphoreType.DMA((2,)),
            pltpu.SemaphoreType.DMA((2,)),
        ],
        compiler_params=pltpu.CompilerParams(collective_id=1, has_side_effects=True),
    )(records)


def local(blended, delays, thresholds):
    tables = filter_tables()
    extended = to_receivers(blended)
    row = lax.axis_index("tm")
    estimate, before, after = filter_with_halos(extended, delays, thresholds[0], tables)
    before = jnp.where(row == 0, jnp.zeros_like(before), before)
    last = row == lax.axis_size("tm") - 1
    after = jnp.where(last, jnp.zeros_like(after), after)
    return filter_and_send(estimate, before, after, extended, delays, thresholds[1], tables)


def solution(mesh):
    return jax.shard_map(
        local,
        mesh=mesh,
        in_specs=(P(None, "shot", "tm"), P(), P()),
        out_specs=P(None, "shot", "tm"),
        check_vma=False,
    )
```

```python
import functools
import math

import jax
import ml_dtypes
import numpy as np
import jax.numpy as jnp
from jax import lax
from jax.experimental import pallas as pl
from jax.experimental.pallas import tpu as pltpu
from jax.sharding import PartitionSpec as P

SRC = 64
SRC_EXP = 2
WIN = 256
BLK = 128
ITERS = 2


RELAX = 0.5


def shifted(array, axis, by):
    count = lax.axis_size(axis)
    pairs = [(i, i + by) for i in range(count) if 0 <= i + by < count]
    return lax.ppermute(array, axis, pairs)


def blend(estimate, earlier, own_delays):
    receivers, sources, samples = estimate.shape
    blocks = samples // BLK
    experiments = sources // SRC_EXP
    upper = estimate.reshape(receivers, sources, blocks, BLK)
    shifts = own_delays.reshape(-1)
    row_index = jnp.arange(BLK, dtype=jnp.int32)[None, :, None]
    column_index = jnp.arange(BLK, dtype=jnp.int32)[None, None, :]
    select_same = (row_index == column_index - shifts[:, None, None]).astype(jnp.bfloat16)
    select_prior = (row_index == BLK + column_index - shifts[:, None, None]).astype(jnp.bfloat16)
    same = jnp.einsum("rsnb,sbi->rsni", upper, select_same, preferred_element_type=jnp.float32)
    onward = jnp.einsum("rsnb,sbi->rsni", upper, select_prior, preferred_element_type=jnp.float32)
    edge_part = jnp.einsum(
        "rsb,sbi->rsi", earlier, select_prior, preferred_element_type=jnp.float32
    )
    same = jnp.sum(same.reshape(receivers, experiments, SRC_EXP, blocks, BLK), axis=2)
    onward = jnp.sum(onward.reshape(receivers, experiments, SRC_EXP, blocks, BLK), axis=2)
    edge_part = jnp.sum(edge_part.reshape(receivers, experiments, SRC_EXP, BLK), axis=2)
    carried = jnp.concatenate([edge_part[:, :, None], onward[:, :, : blocks - 1]], axis=2)
    return (same + carried).reshape(receivers, experiments, samples)


def spread(residual, later, own_delays):
    receivers, experiments, samples = residual.shape
    blocks = samples // BLK
    lower = residual.reshape(receivers, experiments, blocks, BLK)
    row_index = jnp.arange(BLK, dtype=jnp.int32)[None, None, :, None]
    column_index = jnp.arange(BLK, dtype=jnp.int32)[None, None, None, :]
    select_same = (row_index == column_index + own_delays[:, :, None, None]).astype(jnp.bfloat16)
    select_next = (row_index + BLK == column_index + own_delays[:, :, None, None]).astype(
        jnp.bfloat16
    )
    same = jnp.einsum("rena,ekai->rekni", lower, select_same, preferred_element_type=jnp.float32)
    backward = jnp.einsum(
        "rena,ekai->rekni", lower, select_next, preferred_element_type=jnp.float32
    )
    edge_part = jnp.einsum("rea,ekai->reki", later, select_next, preferred_element_type=jnp.float32)
    carried = jnp.concatenate([backward[:, :, :, 1:], edge_part[:, :, :, None]], axis=3)
    return (same + carried).reshape(receivers, experiments * SRC_EXP, samples)


def split(value):
    high = value.astype(jnp.bfloat16)
    return high, (value - high.astype(jnp.float32)).astype(jnp.bfloat16)


def exact_split(value):
    high = value.astype(ml_dtypes.bfloat16)
    low = (value - high.astype(np.float64)).astype(ml_dtypes.bfloat16)
    return jnp.asarray(high), jnp.asarray(low)


def filter_tables():
    turn = lambda n: (np.arange(n)[:, None] * np.arange(n)[None, :] % n) * (2.0 * np.pi / n)
    time_turn = turn(WIN)
    forward = jnp.asarray(
        np.concatenate([np.cos(time_turn), -np.sin(time_turn)], axis=1).astype(ml_dtypes.bfloat16)
    )
    inverse_high, inverse_low = exact_split(
        np.concatenate([np.cos(time_turn), -np.sin(time_turn)], axis=0) / math.sqrt(WIN)
    )
    inverse = jnp.concatenate([inverse_high, inverse_high, inverse_low], axis=0)
    source_turn = turn(SRC)
    cos_source = np.cos(source_turn) / math.sqrt(SRC)
    sin_source = np.sin(source_turn) / math.sqrt(SRC)
    mix_forward = exact_split(np.block([[cos_source, sin_source], [-sin_source, cos_source]]))
    mix_inverse = exact_split(np.block([[cos_source, -sin_source], [sin_source, cos_source]]))
    return forward, inverse, mix_forward, mix_inverse


def mix(table, value):
    table_high, table_low = table
    value_high, value_low = split(value)
    stacked = jnp.concatenate([value_high, value_low, value_high], axis=0)
    joined = jnp.concatenate([table_high, table_high, table_low], axis=1)
    return jnp.dot(joined, stacked, preferred_element_type=jnp.float32)


def filter_block(u_ref, first, count, tables, out_ref):
    forward_ref, inverse_ref, mfh_ref, mfl_ref, mih_ref, mil_ref, limit_ref = tables
    sources, samples = u_ref.shape[1:]
    windows = samples // WIN
    groups = [(r, w) for r in range(first, first + count) for w in range(windows)]
    scale = 1.0 / math.sqrt(WIN)
    rows = jnp.concatenate(
        [u_ref[r, :, w * WIN : (w + 1) * WIN] for r, w in groups], axis=0
    )
    spectrum = jnp.dot(rows, forward_ref[...], preferred_element_type=jnp.float32) * scale
    block = lambda g: slice(g * sources, (g + 1) * sources)
    field = jnp.concatenate(
        [
            jnp.concatenate([spectrum[block(g), :WIN], spectrum[block(g), WIN:]], axis=0)
            for g in range(len(groups))
        ],
        axis=1,
    )
    coeffs = mix((mfh_ref[...], mfl_ref[...]), field)
    real_part = coeffs[:sources]
    imag_part = coeffs[sources:]
    limit = limit_ref[...]
    magnitude = jnp.sqrt(real_part * real_part + imag_part * imag_part)
    factor = jnp.maximum(magnitude - limit, 0.0) / jnp.maximum(magnitude, limit)
    kept = jnp.concatenate([real_part * factor, imag_part * factor], axis=0)
    back = mix((mih_ref[...], mil_ref[...]), kept)
    lanes = lambda g: slice(g * WIN, (g + 1) * WIN)
    joined = jnp.concatenate(
        [
            jnp.concatenate([back[:sources, lanes(g)], back[sources:, lanes(g)]], axis=1)
            for g in range(len(groups))
        ],
        axis=0,
    )
    joined_high, joined_low = split(joined)
    restored = jnp.dot(
        jnp.concatenate([joined_high, joined_low, joined_high], axis=1),
        inverse_ref[...],
        preferred_element_type=jnp.float32,
    )
    for g, (r, w) in enumerate(groups):
        out_ref[r, :, w * WIN : (w + 1) * WIN] = restored[block(g)].astype(out_ref.dtype)


def pairs(rows, cols, transpose):
    row = lax.broadcasted_iota(jnp.int32, (rows, cols), 0)
    col = lax.broadcasted_iota(jnp.int32, (rows, cols), 1)
    hit = (col // SRC_EXP == row) if transpose else (row // SRC_EXP == col)
    return jnp.where(hit, 1.0, 0.0).astype(jnp.bfloat16)


def blend_residual(rec_ref, est_ref, before_ref, after_ref, shift_ref, last, res_ref, rows):
    receivers, experiments, width = rec_ref.shape
    pair = pairs(experiments, est_ref.shape[1], True)
    shift = shift_ref[...]
    lane = lax.broadcasted_iota(jnp.int32, (experiments, width), 1)
    drop = jnp.logical_and(lane >= width - BLK, last)
    for r in rows:
        moved = jnp.concatenate([before_ref[r], est_ref[r], after_ref[r]], axis=1).astype(jnp.float32)
        full = moved.shape[1]
        for bit in range((BLK - 1).bit_length()):
            amount = 1 << bit
            moved = jnp.where((shift & amount) != 0, pltpu.roll(moved, amount, 1), moved)
        summed = jnp.dot(
            pair, moved[:, full - width :].astype(jnp.bfloat16),
            preferred_element_type=jnp.float32,
        )
        residual = (rec_ref[r] - summed).astype(res_ref.dtype)
        res_ref[r] = jnp.where(drop, jnp.zeros_like(residual), residual)


def spread_update(res_ref, shift_ref, est_ref, u_ref, rows, last=None, wait=None):
    receivers, sources, samples = u_ref.shape
    experiments, width = res_ref.shape[1:]
    shift = shift_ref[...]
    dup = pairs(sources, experiments, False)
    for r in rows:
        if wait is not None:
            wait(r)
        residual = res_ref[r]
        if last is not None:
            lane = lax.broadcasted_iota(jnp.int32, (experiments, width), 1)
            drop = jnp.logical_and(lane >= samples, last)
            residual = jnp.where(drop, jnp.zeros_like(residual), residual).astype(jnp.bfloat16)
        moved = jnp.dot(dup, residual, preferred_element_type=jnp.float32)
        for bit in range((BLK - 1).bit_length()):
            amount = 1 << bit
            rolled = pltpu.roll(moved, width - amount, 1)
            moved = jnp.where((shift & amount) != 0, rolled, moved)
        value = RELAX * moved[:, :samples]
        if est_ref is not None:
            value = est_ref[r].astype(jnp.float32) + value
        u_ref[r] = value.astype(u_ref.dtype)


def spread_inputs(residual, delays):
    return [residual, delays.reshape(-1, 1)]


def filter_kernel(u_ref, *refs):
    filter_block(u_ref, 0, u_ref.shape[0], refs[:7], refs[7])


def filter_halo_kernel(stages, res_ref, shift_ref, *refs):
    tables = refs[:7]
    out_ref, before_ref, after_ref, u_ref, res_vmem, load_sem, send_sem, recv_sem = refs[7:]
    samples = u_ref.shape[2]
    loads = [
        pltpu.make_async_copy(res_ref.at[r], res_vmem.at[r], load_sem.at[r])
        for r in range(res_ref.shape[0])
    ]
    for load in loads:
        load.start()
    shot = lax.axis_index("shot")
    row = lax.axis_index("tm")
    has_prev = row > 0
    has_next = row < stages - 1
    barrier = pltpu.get_barrier_semaphore()
    mesh_id = pl.DeviceIdType.MESH

    @pl.when(has_prev)
    def _():
        pl.semaphore_signal(barrier, 1, device_id=(shot, row - 1), device_id_type=mesh_id)

    @pl.when(has_next)
    def _():
        pl.semaphore_signal(barrier, 1, device_id=(shot, row + 1), device_id_type=mesh_id)

    spread_update(
        res_vmem, shift_ref, None, u_ref, range(u_ref.shape[0]), jnp.logical_not(has_next),
        lambda r: loads[r].wait(),
    )
    filter_block(u_ref, 0, u_ref.shape[0], tables, out_ref)
    pl.semaphore_wait(barrier, has_prev.astype(jnp.int32) + has_next.astype(jnp.int32))

    def to_prev():
        return pltpu.make_async_remote_copy(
            src_ref=out_ref.at[:, :, pl.ds(0, BLK)],
            dst_ref=after_ref,
            send_sem=send_sem.at[0],
            recv_sem=recv_sem.at[0],
            device_id=(shot, row - 1),
            device_id_type=mesh_id,
        )

    def to_next():
        return pltpu.make_async_remote_copy(
            src_ref=out_ref.at[:, :, pl.ds(samples - BLK, BLK)],
            dst_ref=before_ref,
            send_sem=send_sem.at[1],
            recv_sem=recv_sem.at[1],
            device_id=(shot, row + 1),
            device_id_type=mesh_id,
        )

    pl.when(has_prev)(lambda: to_prev().start())
    pl.when(has_next)(lambda: to_next().start())

    @pl.when(has_prev)
    def _():
        to_prev().wait_send()
        to_next().wait_recv()

    @pl.when(has_next)
    def _():
        to_next().wait_send()
        to_prev().wait_recv()


def filter_with_halos(residual, delays, limits, tables):
    forward, inverse, mix_forward, mix_inverse = tables
    receivers = residual.shape[0]
    sources = delays.size
    samples = residual.shape[2] - BLK
    stages = lax.axis_size("tm")
    vmem = pl.BlockSpec(memory_space=pltpu.VMEM)
    anywhere = pl.BlockSpec(memory_space=pl.ANY)
    edge = jax.ShapeDtypeStruct((receivers, sources, BLK), jnp.bfloat16)
    return pl.pallas_call(
        functools.partial(filter_halo_kernel, stages),
        in_specs=[anywhere] + [vmem] * 8,
        out_specs=(vmem, anywhere, anywhere),
        out_shape=(jax.ShapeDtypeStruct((receivers, sources, samples), jnp.bfloat16), edge, edge),
        scratch_shapes=[
            pltpu.VMEM((receivers, sources, samples), jnp.bfloat16),
            pltpu.VMEM(residual.shape, residual.dtype),
            pltpu.SemaphoreType.DMA((receivers,)),
            pltpu.SemaphoreType.DMA((2,)),
            pltpu.SemaphoreType.DMA((2,)),
        ],
        compiler_params=pltpu.CompilerParams(
            collective_id=3, has_side_effects=True, vmem_limit_bytes=48 * 1024 * 1024
        ),
    )(
        *spread_inputs(residual, delays),
        forward, inverse, *mix_forward, *mix_inverse, limits.reshape(sources, 1),
    )


def filter_send_kernel(
    count, stages, halves, est_ref, before_ref, after_ref, rec_ref, shift_ref, *refs
):
    tables = refs[:7]
    out_ref, done_ref, u_ref, res_ref, send_sem, recv_sem, own_sem = refs[7:]
    receivers, sources, samples = u_ref.shape
    own = sources // count
    per = receivers // halves
    me = lax.axis_index("shot")
    row = lax.axis_index("tm")
    barrier = pltpu.get_barrier_semaphore()

    def greet(step, carry):
        peer = lax.rem(me + step, count)
        pl.semaphore_signal(barrier, 1, device_id=(peer, row), device_id_type=pl.DeviceIdType.MESH)
        return carry

    lax.fori_loop(1, count, greet, 0)
    last = lax.axis_index("tm") == stages - 1

    def remote(half, peer, sender):
        return pltpu.make_async_remote_copy(
            src_ref=done_ref.at[pl.ds(half * per, per), pl.ds(peer * own, own), :],
            dst_ref=out_ref.at[pl.ds(sender * receivers + half * per, per), :, :],
            send_sem=send_sem.at[half, peer],
            recv_sem=recv_sem.at[half, sender],
            device_id=(peer, row),
            device_id_type=pl.DeviceIdType.MESH,
        )

    locals_ = []
    for half in range(halves):
        rows = range(half * per, (half + 1) * per)
        blend_residual(rec_ref, est_ref, before_ref, after_ref, shift_ref, last, res_ref, rows)
        spread_update(res_ref, shift_ref, est_ref, u_ref, rows)
        filter_block(u_ref, half * per, per, tables, done_ref)
        if half == 0:
            pl.semaphore_wait(barrier, count - 1)
        mine = pltpu.make_async_copy(
            done_ref.at[pl.ds(half * per, per), pl.ds(me * own, own), :],
            out_ref.at[pl.ds(me * receivers + half * per, per), :, :],
            own_sem.at[half],
        )
        mine.start()
        locals_.append(mine)

        def send(step, carry, half=half):
            remote(half, lax.rem(me + step, count), me).start()
            return carry

        lax.fori_loop(1, count, send, 0)

    for half in range(halves):

        def finish(step, carry, half=half):
            peer = lax.rem(me + step, count)
            remote(half, peer, me).wait_send()
            remote(half, me, peer).wait_recv()
            return carry

        lax.fori_loop(1, count, finish, 0)
        locals_[half].wait()


def filter_and_send(estimate, before, after, records, delays, limits, tables):
    forward, inverse, mix_forward, mix_inverse = tables
    receivers, sources, samples = estimate.shape
    count = lax.axis_size("shot")
    halves = 2
    vmem = pl.BlockSpec(memory_space=pltpu.VMEM)
    return pl.pallas_call(
        functools.partial(filter_send_kernel, count, lax.axis_size("tm"), halves),
        in_specs=[vmem] * 12,
        out_specs=pl.BlockSpec(memory_space=pl.ANY),
        out_shape=jax.ShapeDtypeStruct(
            (receivers * count, sources // count, samples), jnp.bfloat16
        ),
        scratch_shapes=[
            pltpu.VMEM(estimate.shape, jnp.bfloat16),
            pltpu.VMEM(estimate.shape, jnp.bfloat16),
            pltpu.VMEM(records.shape, jnp.bfloat16),
            pltpu.SemaphoreType.DMA((halves, count)),
            pltpu.SemaphoreType.DMA((halves, count)),
            pltpu.SemaphoreType.DMA((halves,)),
        ],
        compiler_params=pltpu.CompilerParams(
            collective_id=2, has_side_effects=True, vmem_limit_bytes=48 * 1024 * 1024
        ),
    )(
        estimate,
        before,
        after,
        records,
        *spread_inputs(records, delays)[1:],
        forward, inverse, *mix_forward, *mix_inverse, limits.reshape(sources, 1),
    )


def coherence(gathers, limits, tables):
    forward, inverse, mix_forward, mix_inverse = tables
    receivers, sources, samples = gathers.shape
    vmem = pl.BlockSpec(memory_space=pltpu.VMEM)
    return pl.pallas_call(
        filter_kernel,
        in_specs=[vmem] * 8,
        out_specs=vmem,
        out_shape=jax.ShapeDtypeStruct(gathers.shape, jnp.bfloat16),
        compiler_params=pltpu.CompilerParams(vmem_limit_bytes=48 * 1024 * 1024),
    )(gathers, forward, inverse, *mix_forward, *mix_inverse, limits.reshape(sources, 1))


def exchange_kernel(count, outgoing, incoming, src_ref, out_ref, send_sem, recv_sem, own_sem):
    me = lax.axis_index("shot")
    row = lax.axis_index("tm")
    barrier = pltpu.get_barrier_semaphore()

    def greet(step, carry):
        peer = lax.rem(me + step, count)
        pl.semaphore_signal(barrier, 1, device_id=(peer, row), device_id_type=pl.DeviceIdType.MESH)
        return carry

    lax.fori_loop(1, count, greet, 0)
    pl.semaphore_wait(barrier, count - 1)
    own = pltpu.make_async_copy(src_ref.at[outgoing(me)], out_ref.at[incoming(me)], own_sem)
    own.start()

    def remote(peer, sender):
        return pltpu.make_async_remote_copy(
            src_ref=src_ref.at[outgoing(peer)],
            dst_ref=out_ref.at[incoming(sender)],
            send_sem=send_sem.at[peer],
            recv_sem=recv_sem.at[sender],
            device_id=(peer, row),
            device_id_type=pl.DeviceIdType.MESH,
        )

    def send(step, carry):
        remote(lax.rem(me + step, count), me).start()
        return carry

    lax.fori_loop(1, count, send, 0)

    def finish(step, carry):
        peer = lax.rem(me + step, count)
        remote(peer, me).wait_send()
        remote(me, peer).wait_recv()
        return carry

    lax.fori_loop(1, count, finish, 0)
    own.wait()


def exchange(value, out_shape, outgoing, incoming, tag):
    count = lax.axis_size("shot")
    anywhere = pl.BlockSpec(memory_space=pl.ANY)
    return pl.pallas_call(
        functools.partial(exchange_kernel, count, outgoing, incoming),
        in_specs=[anywhere],
        out_specs=anywhere,
        out_shape=jax.ShapeDtypeStruct(out_shape, value.dtype),
        scratch_shapes=[
            pltpu.SemaphoreType.DMA((count,)),
            pltpu.SemaphoreType.DMA((count,)),
            pltpu.SemaphoreType.DMA,
        ],
        compiler_params=pltpu.CompilerParams(collective_id=tag, has_side_effects=True),
    )(value)


def to_sources(estimate):
    receivers, sources, samples = estimate.shape
    count = lax.axis_size("shot")
    own = sources // count
    return exchange(
        estimate,
        (receivers * count, own, samples),
        lambda peer: (slice(None), pl.ds(peer * own, own), slice(None)),
        lambda sender: (pl.ds(sender * receivers, receivers), slice(None), slice(None)),
        0,
    )


def receive_kernel(count, stages, src_ref, out_ref, halo_ref, send_sem, recv_sem, edge_sem, own_sem):
    part, own, samples = out_ref.shape[0], src_ref.shape[1], src_ref.shape[2]
    me = lax.axis_index("shot")
    row = lax.axis_index("tm")
    has_prev = row > 0
    has_next = row < stages - 1
    mesh_id = pl.DeviceIdType.MESH
    barrier = pltpu.get_barrier_semaphore()

    def greet(step, carry):
        peer = lax.rem(me + step, count)
        pl.semaphore_signal(barrier, 1, device_id=(peer, row), device_id_type=mesh_id)
        return carry

    lax.fori_loop(1, count, greet, 0)

    @pl.when(has_prev)
    def _():
        pl.semaphore_signal(barrier, 1, device_id=(me, row - 1), device_id_type=mesh_id)

    @pl.when(has_next)
    def _():
        pl.semaphore_signal(barrier, 1, device_id=(me, row + 1), device_id_type=mesh_id)

    pl.semaphore_wait(
        barrier, count - 1 + has_prev.astype(jnp.int32) + has_next.astype(jnp.int32)
    )
    body = (slice(None), pl.ds(me * own, own), pl.ds(0, samples))
    tail = (slice(None), pl.ds(me * own, own), pl.ds(samples, BLK))

    def chunk(peer, sender, stage):
        source = src_ref if stage == 0 else halo_ref
        target = body if stage == 0 else tail
        target = (target[0], pl.ds(sender * own, own), target[2])
        return pltpu.make_async_remote_copy(
            src_ref=source.at[pl.ds(peer * part, part)],
            dst_ref=out_ref.at[target],
            send_sem=send_sem.at[stage, peer],
            recv_sem=recv_sem.at[stage, sender],
            device_id=(peer, row),
            device_id_type=mesh_id,
        )

    mine = pltpu.make_async_copy(src_ref.at[pl.ds(me * part, part)], out_ref.at[body], own_sem.at[0])
    mine.start()

    def send_body(step, carry):
        chunk(lax.rem(me + step, count), me, 0).start()
        return carry

    lax.fori_loop(1, count, send_body, 0)

    def edge(target_row):
        return pltpu.make_async_remote_copy(
            src_ref=src_ref.at[:, :, pl.ds(0, BLK)],
            dst_ref=halo_ref,
            send_sem=edge_sem.at[0],
            recv_sem=edge_sem.at[1],
            device_id=(me, target_row),
            device_id_type=mesh_id,
        )

    pl.when(has_prev)(lambda: edge(row - 1).start())

    @pl.when(has_next)
    def _():
        edge(row + 1).wait_recv()
        theirs = pltpu.make_async_copy(
            halo_ref.at[pl.ds(me * part, part)], out_ref.at[tail], own_sem.at[1]
        )
        theirs.start()

        def send_tail(step, carry):
            chunk(lax.rem(me + step, count), me, 1).start()
            return carry

        lax.fori_loop(1, count, send_tail, 0)

        def finish_tail(step, carry):
            peer = lax.rem(me + step, count)
            chunk(peer, me, 1).wait_send()
            chunk(me, peer, 1).wait_recv()
            return carry

        lax.fori_loop(1, count, finish_tail, 0)
        theirs.wait()

    pl.when(has_prev)(lambda: edge(row - 1).wait_send())

    def finish_body(step, carry):
        peer = lax.rem(me + step, count)
        chunk(peer, me, 0).wait_send()
        chunk(me, peer, 0).wait_recv()
        return carry

    lax.fori_loop(1, count, finish_body, 0)
    mine.wait()


def to_receivers(records):
    receivers, own, samples = records.shape
    count = lax.axis_size("shot")
    part = receivers // count
    return pl.pallas_call(
        functools.partial(receive_kernel, count, lax.axis_size("tm")),
        in_specs=[pl.BlockSpec(memory_space=pl.ANY)],
        out_specs=pl.BlockSpec(memory_space=pl.ANY),
        out_shape=jax.ShapeDtypeStruct((part, own * count, samples + BLK), records.dtype),
        scratch_shapes=[
            pltpu.VMEM((receivers, own, BLK), records.dtype),
            pltpu.SemaphoreType.DMA((2, count)),
            pltpu.SemaphoreType.DMA((2, count)),
            pltpu.SemaphoreType.DMA((2,)),
            pltpu.SemaphoreType.DMA((2,)),
        ],
        compiler_params=pltpu.CompilerParams(collective_id=1, has_side_effects=True),
    )(records)


def local(blended, delays, thresholds):
    tables = filter_tables()
    extended = to_receivers(blended)
    row = lax.axis_index("tm")
    estimate, before, after = filter_with_halos(extended, delays, thresholds[0], tables)
    before = jnp.where(row == 0, jnp.zeros_like(before), before)
    last = row == lax.axis_size("tm") - 1
    after = jnp.where(last, jnp.zeros_like(after), after)
    return filter_and_send(estimate, before, after, extended, delays, thresholds[1], tables)


def solution(mesh):
    return jax.shard_map(
        local,
        mesh=mesh,
        in_specs=(P(None, "shot", "tm"), P(), P()),
        out_specs=P(None, "shot", "tm"),
        check_vma=False,
    )
```

```python
import functools
import math

import jax
import ml_dtypes
import numpy as np
import jax.numpy as jnp
from jax import lax
from jax.experimental import pallas as pl
from jax.experimental.pallas import tpu as pltpu
from jax.sharding import PartitionSpec as P

SRC = 64
SRC_EXP = 2
WIN = 256
BLK = 128
ITERS = 2


RELAX = 0.5


def shifted(array, axis, by):
    count = lax.axis_size(axis)
    pairs = [(i, i + by) for i in range(count) if 0 <= i + by < count]
    return lax.ppermute(array, axis, pairs)


def blend(estimate, earlier, own_delays):
    receivers, sources, samples = estimate.shape
    blocks = samples // BLK
    experiments = sources // SRC_EXP
    upper = estimate.reshape(receivers, sources, blocks, BLK)
    shifts = own_delays.reshape(-1)
    row_index = jnp.arange(BLK, dtype=jnp.int32)[None, :, None]
    column_index = jnp.arange(BLK, dtype=jnp.int32)[None, None, :]
    select_same = (row_index == column_index - shifts[:, None, None]).astype(jnp.bfloat16)
    select_prior = (row_index == BLK + column_index - shifts[:, None, None]).astype(jnp.bfloat16)
    same = jnp.einsum("rsnb,sbi->rsni", upper, select_same, preferred_element_type=jnp.float32)
    onward = jnp.einsum("rsnb,sbi->rsni", upper, select_prior, preferred_element_type=jnp.float32)
    edge_part = jnp.einsum(
        "rsb,sbi->rsi", earlier, select_prior, preferred_element_type=jnp.float32
    )
    same = jnp.sum(same.reshape(receivers, experiments, SRC_EXP, blocks, BLK), axis=2)
    onward = jnp.sum(onward.reshape(receivers, experiments, SRC_EXP, blocks, BLK), axis=2)
    edge_part = jnp.sum(edge_part.reshape(receivers, experiments, SRC_EXP, BLK), axis=2)
    carried = jnp.concatenate([edge_part[:, :, None], onward[:, :, : blocks - 1]], axis=2)
    return (same + carried).reshape(receivers, experiments, samples)


def spread(residual, later, own_delays):
    receivers, experiments, samples = residual.shape
    blocks = samples // BLK
    lower = residual.reshape(receivers, experiments, blocks, BLK)
    row_index = jnp.arange(BLK, dtype=jnp.int32)[None, None, :, None]
    column_index = jnp.arange(BLK, dtype=jnp.int32)[None, None, None, :]
    select_same = (row_index == column_index + own_delays[:, :, None, None]).astype(jnp.bfloat16)
    select_next = (row_index + BLK == column_index + own_delays[:, :, None, None]).astype(
        jnp.bfloat16
    )
    same = jnp.einsum("rena,ekai->rekni", lower, select_same, preferred_element_type=jnp.float32)
    backward = jnp.einsum(
        "rena,ekai->rekni", lower, select_next, preferred_element_type=jnp.float32
    )
    edge_part = jnp.einsum("rea,ekai->reki", later, select_next, preferred_element_type=jnp.float32)
    carried = jnp.concatenate([backward[:, :, :, 1:], edge_part[:, :, :, None]], axis=3)
    return (same + carried).reshape(receivers, experiments * SRC_EXP, samples)


def split(value):
    high = value.astype(jnp.bfloat16)
    return high, (value - high.astype(jnp.float32)).astype(jnp.bfloat16)


def exact_split(value):
    high = value.astype(ml_dtypes.bfloat16)
    low = (value - high.astype(np.float64)).astype(ml_dtypes.bfloat16)
    return jnp.asarray(high), jnp.asarray(low)


def filter_tables():
    turn = lambda n: (np.arange(n)[:, None] * np.arange(n)[None, :] % n) * (2.0 * np.pi / n)
    time_turn = turn(WIN)
    forward = jnp.asarray(
        np.concatenate([np.cos(time_turn), -np.sin(time_turn)], axis=1).astype(ml_dtypes.bfloat16)
    )
    inverse_high, inverse_low = exact_split(
        np.concatenate([np.cos(time_turn), -np.sin(time_turn)], axis=0) / math.sqrt(WIN)
    )
    inverse = jnp.concatenate([inverse_high, inverse_high, inverse_low], axis=0)
    source_turn = turn(SRC)
    cos_source = np.cos(source_turn) / math.sqrt(SRC)
    sin_source = np.sin(source_turn) / math.sqrt(SRC)
    mix_forward = exact_split(np.block([[cos_source, sin_source], [-sin_source, cos_source]]))
    mix_inverse = exact_split(np.block([[cos_source, -sin_source], [sin_source, cos_source]]))
    return forward, inverse, mix_forward, mix_inverse


def mix(table, value):
    table_high, table_low = table
    value_high, value_low = split(value)
    stacked = jnp.concatenate([value_high, value_low, value_high], axis=0)
    joined = jnp.concatenate([table_high, table_high, table_low], axis=1)
    return jnp.dot(joined, stacked, preferred_element_type=jnp.float32)


def filter_block(u_ref, first, count, tables, out_ref):
    forward_ref, inverse_ref, mfh_ref, mfl_ref, mih_ref, mil_ref, limit_ref = tables
    sources, samples = u_ref.shape[1:]
    windows = samples // WIN
    groups = [(r, w) for r in range(first, first + count) for w in range(windows)]
    scale = 1.0 / math.sqrt(WIN)
    rows = jnp.concatenate(
        [u_ref[r, :, w * WIN : (w + 1) * WIN] for r, w in groups], axis=0
    )
    spectrum = jnp.dot(rows, forward_ref[...], preferred_element_type=jnp.float32) * scale
    block = lambda g: slice(g * sources, (g + 1) * sources)
    field = jnp.concatenate(
        [
            jnp.concatenate([spectrum[block(g), :WIN], spectrum[block(g), WIN:]], axis=0)
            for g in range(len(groups))
        ],
        axis=1,
    )
    coeffs = mix((mfh_ref[...], mfl_ref[...]), field)
    real_part = coeffs[:sources]
    imag_part = coeffs[sources:]
    limit = limit_ref[...]
    magnitude = jnp.sqrt(real_part * real_part + imag_part * imag_part)
    factor = jnp.maximum(magnitude - limit, 0.0) / jnp.maximum(magnitude, limit)
    kept = jnp.concatenate([real_part * factor, imag_part * factor], axis=0)
    back = mix((mih_ref[...], mil_ref[...]), kept)
    lanes = lambda g: slice(g * WIN, (g + 1) * WIN)
    joined = jnp.concatenate(
        [
            jnp.concatenate([back[:sources, lanes(g)], back[sources:, lanes(g)]], axis=1)
            for g in range(len(groups))
        ],
        axis=0,
    )
    joined_high, joined_low = split(joined)
    restored = jnp.dot(
        jnp.concatenate([joined_high, joined_low, joined_high], axis=1),
        inverse_ref[...],
        preferred_element_type=jnp.float32,
    )
    for g, (r, w) in enumerate(groups):
        out_ref[r, :, w * WIN : (w + 1) * WIN] = restored[block(g)].astype(out_ref.dtype)


def pairs(rows, cols, transpose):
    row = lax.broadcasted_iota(jnp.int32, (rows, cols), 0)
    col = lax.broadcasted_iota(jnp.int32, (rows, cols), 1)
    hit = (col // SRC_EXP == row) if transpose else (row // SRC_EXP == col)
    return jnp.where(hit, 1.0, 0.0).astype(jnp.bfloat16)


def blend_residual(rec_ref, est_ref, before_ref, after_ref, shift_ref, last, res_ref, rows):
    receivers, experiments, width = rec_ref.shape
    pair = pairs(experiments, est_ref.shape[1], True)
    shift = shift_ref[...]
    lane = lax.broadcasted_iota(jnp.int32, (experiments, width), 1)
    drop = jnp.logical_and(lane >= width - BLK, last)
    for r in rows:
        moved = jnp.concatenate([before_ref[r], est_ref[r], after_ref[r]], axis=1).astype(jnp.float32)
        full = moved.shape[1]
        for bit in range((BLK - 1).bit_length()):
            amount = 1 << bit
            moved = jnp.where((shift & amount) != 0, pltpu.roll(moved, amount, 1), moved)
        summed = jnp.dot(
            pair, moved[:, full - width :].astype(jnp.bfloat16),
            preferred_element_type=jnp.float32,
        )
        residual = (rec_ref[r] - summed).astype(res_ref.dtype)
        res_ref[r] = jnp.where(drop, jnp.zeros_like(residual), residual)


def spread_update(res_ref, shift_ref, est_ref, u_ref, rows, last=None):
    receivers, sources, samples = u_ref.shape
    experiments, width = res_ref.shape[1:]
    shift = shift_ref[...]
    dup = pairs(sources, experiments, False)
    for r in rows:
        residual = res_ref[r]
        if last is not None:
            lane = lax.broadcasted_iota(jnp.int32, (experiments, width), 1)
            drop = jnp.logical_and(lane >= samples, last)
            residual = jnp.where(drop, jnp.zeros_like(residual), residual).astype(jnp.bfloat16)
        moved = jnp.dot(dup, residual, preferred_element_type=jnp.float32)
        for bit in range((BLK - 1).bit_length()):
            amount = 1 << bit
            rolled = pltpu.roll(moved, width - amount, 1)
            moved = jnp.where((shift & amount) != 0, rolled, moved)
        value = RELAX * moved[:, :samples]
        if est_ref is not None:
            value = est_ref[r].astype(jnp.float32) + value
        u_ref[r] = value.astype(u_ref.dtype)


def spread_inputs(residual, delays):
    return [residual, delays.reshape(-1, 1)]


def filter_kernel(u_ref, *refs):
    filter_block(u_ref, 0, u_ref.shape[0], refs[:7], refs[7])


def filter_halo_kernel(stages, res_ref, shift_ref, *refs):
    tables = refs[:7]
    out_ref, before_ref, after_ref, u_ref, send_sem, recv_sem = refs[7:]
    samples = u_ref.shape[2]
    shot = lax.axis_index("shot")
    row = lax.axis_index("tm")
    has_prev = row > 0
    has_next = row < stages - 1
    barrier = pltpu.get_barrier_semaphore()
    mesh_id = pl.DeviceIdType.MESH

    @pl.when(has_prev)
    def _():
        pl.semaphore_signal(barrier, 1, device_id=(shot, row - 1), device_id_type=mesh_id)

    @pl.when(has_next)
    def _():
        pl.semaphore_signal(barrier, 1, device_id=(shot, row + 1), device_id_type=mesh_id)

    spread_update(res_ref, shift_ref, None, u_ref, range(u_ref.shape[0]), jnp.logical_not(has_next))
    filter_block(u_ref, 0, u_ref.shape[0], tables, out_ref)
    pl.semaphore_wait(barrier, has_prev.astype(jnp.int32) + has_next.astype(jnp.int32))

    def to_prev():
        return pltpu.make_async_remote_copy(
            src_ref=out_ref.at[:, :, pl.ds(0, BLK)],
            dst_ref=after_ref,
            send_sem=send_sem.at[0],
            recv_sem=recv_sem.at[0],
            device_id=(shot, row - 1),
            device_id_type=mesh_id,
        )

    def to_next():
        return pltpu.make_async_remote_copy(
            src_ref=out_ref.at[:, :, pl.ds(samples - BLK, BLK)],
            dst_ref=before_ref,
            send_sem=send_sem.at[1],
            recv_sem=recv_sem.at[1],
            device_id=(shot, row + 1),
            device_id_type=mesh_id,
        )

    pl.when(has_prev)(lambda: to_prev().start())
    pl.when(has_next)(lambda: to_next().start())

    @pl.when(has_prev)
    def _():
        to_prev().wait_send()
        to_next().wait_recv()

    @pl.when(has_next)
    def _():
        to_next().wait_send()
        to_prev().wait_recv()


def filter_with_halos(residual, delays, limits, tables):
    forward, inverse, mix_forward, mix_inverse = tables
    receivers = residual.shape[0]
    sources = delays.size
    samples = residual.shape[2] - BLK
    stages = lax.axis_size("tm")
    vmem = pl.BlockSpec(memory_space=pltpu.VMEM)
    anywhere = pl.BlockSpec(memory_space=pl.ANY)
    edge = jax.ShapeDtypeStruct((receivers, sources, BLK), jnp.bfloat16)
    return pl.pallas_call(
        functools.partial(filter_halo_kernel, stages),
        in_specs=[vmem] * 9,
        out_specs=(vmem, anywhere, anywhere),
        out_shape=(jax.ShapeDtypeStruct((receivers, sources, samples), jnp.bfloat16), edge, edge),
        scratch_shapes=[
            pltpu.VMEM((receivers, sources, samples), jnp.bfloat16),
            pltpu.SemaphoreType.DMA((2,)),
            pltpu.SemaphoreType.DMA((2,)),
        ],
        compiler_params=pltpu.CompilerParams(
            collective_id=3, has_side_effects=True, vmem_limit_bytes=48 * 1024 * 1024
        ),
    )(
        *spread_inputs(residual, delays),
        forward, inverse, *mix_forward, *mix_inverse, limits.reshape(sources, 1),
    )


def filter_send_kernel(
    count, stages, halves, est_ref, before_ref, after_ref, rec_ref, shift_ref, *refs
):
    tables = refs[:7]
    out_ref, done_ref, u_ref, res_ref, send_sem, recv_sem, own_sem = refs[7:]
    receivers, sources, samples = u_ref.shape
    own = sources // count
    per = receivers // halves
    me = lax.axis_index("shot")
    row = lax.axis_index("tm")
    barrier = pltpu.get_barrier_semaphore()

    def greet(step, carry):
        peer = lax.rem(me + step, count)
        pl.semaphore_signal(barrier, 1, device_id=(peer, row), device_id_type=pl.DeviceIdType.MESH)
        return carry

    lax.fori_loop(1, count, greet, 0)
    last = lax.axis_index("tm") == stages - 1

    def remote(half, peer, sender):
        return pltpu.make_async_remote_copy(
            src_ref=done_ref.at[pl.ds(half * per, per), pl.ds(peer * own, own), :],
            dst_ref=out_ref.at[pl.ds(sender * receivers + half * per, per), :, :],
            send_sem=send_sem.at[half, peer],
            recv_sem=recv_sem.at[half, sender],
            device_id=(peer, row),
            device_id_type=pl.DeviceIdType.MESH,
        )

    locals_ = []
    for half in range(halves):
        rows = range(half * per, (half + 1) * per)
        blend_residual(rec_ref, est_ref, before_ref, after_ref, shift_ref, last, res_ref, rows)
        spread_update(res_ref, shift_ref, est_ref, u_ref, rows)
        filter_block(u_ref, half * per, per, tables, done_ref)
        if half == 0:
            pl.semaphore_wait(barrier, count - 1)
        mine = pltpu.make_async_copy(
            done_ref.at[pl.ds(half * per, per), pl.ds(me * own, own), :],
            out_ref.at[pl.ds(me * receivers + half * per, per), :, :],
            own_sem.at[half],
        )
        mine.start()
        locals_.append(mine)

        def send(step, carry, half=half):
            remote(half, lax.rem(me + step, count), me).start()
            return carry

        lax.fori_loop(1, count, send, 0)

    for half in range(halves):

        def finish(step, carry, half=half):
            peer = lax.rem(me + step, count)
            remote(half, peer, me).wait_send()
            remote(half, me, peer).wait_recv()
            return carry

        lax.fori_loop(1, count, finish, 0)
        locals_[half].wait()


def filter_and_send(estimate, before, after, records, delays, limits, tables):
    forward, inverse, mix_forward, mix_inverse = tables
    receivers, sources, samples = estimate.shape
    count = lax.axis_size("shot")
    halves = 4
    vmem = pl.BlockSpec(memory_space=pltpu.VMEM)
    return pl.pallas_call(
        functools.partial(filter_send_kernel, count, lax.axis_size("tm"), halves),
        in_specs=[vmem] * 12,
        out_specs=pl.BlockSpec(memory_space=pl.ANY),
        out_shape=jax.ShapeDtypeStruct(
            (receivers * count, sources // count, samples), jnp.bfloat16
        ),
        scratch_shapes=[
            pltpu.VMEM(estimate.shape, jnp.bfloat16),
            pltpu.VMEM(estimate.shape, jnp.bfloat16),
            pltpu.VMEM(records.shape, jnp.bfloat16),
            pltpu.SemaphoreType.DMA((halves, count)),
            pltpu.SemaphoreType.DMA((halves, count)),
            pltpu.SemaphoreType.DMA((halves,)),
        ],
        compiler_params=pltpu.CompilerParams(
            collective_id=2, has_side_effects=True, vmem_limit_bytes=48 * 1024 * 1024
        ),
    )(
        estimate,
        before,
        after,
        records,
        *spread_inputs(records, delays)[1:],
        forward, inverse, *mix_forward, *mix_inverse, limits.reshape(sources, 1),
    )


def coherence(gathers, limits, tables):
    forward, inverse, mix_forward, mix_inverse = tables
    receivers, sources, samples = gathers.shape
    vmem = pl.BlockSpec(memory_space=pltpu.VMEM)
    return pl.pallas_call(
        filter_kernel,
        in_specs=[vmem] * 8,
        out_specs=vmem,
        out_shape=jax.ShapeDtypeStruct(gathers.shape, jnp.bfloat16),
        compiler_params=pltpu.CompilerParams(vmem_limit_bytes=48 * 1024 * 1024),
    )(gathers, forward, inverse, *mix_forward, *mix_inverse, limits.reshape(sources, 1))


def exchange_kernel(count, outgoing, incoming, src_ref, out_ref, send_sem, recv_sem, own_sem):
    me = lax.axis_index("shot")
    row = lax.axis_index("tm")
    barrier = pltpu.get_barrier_semaphore()

    def greet(step, carry):
        peer = lax.rem(me + step, count)
        pl.semaphore_signal(barrier, 1, device_id=(peer, row), device_id_type=pl.DeviceIdType.MESH)
        return carry

    lax.fori_loop(1, count, greet, 0)
    pl.semaphore_wait(barrier, count - 1)
    own = pltpu.make_async_copy(src_ref.at[outgoing(me)], out_ref.at[incoming(me)], own_sem)
    own.start()

    def remote(peer, sender):
        return pltpu.make_async_remote_copy(
            src_ref=src_ref.at[outgoing(peer)],
            dst_ref=out_ref.at[incoming(sender)],
            send_sem=send_sem.at[peer],
            recv_sem=recv_sem.at[sender],
            device_id=(peer, row),
            device_id_type=pl.DeviceIdType.MESH,
        )

    def send(step, carry):
        remote(lax.rem(me + step, count), me).start()
        return carry

    lax.fori_loop(1, count, send, 0)

    def finish(step, carry):
        peer = lax.rem(me + step, count)
        remote(peer, me).wait_send()
        remote(me, peer).wait_recv()
        return carry

    lax.fori_loop(1, count, finish, 0)
    own.wait()


def exchange(value, out_shape, outgoing, incoming, tag):
    count = lax.axis_size("shot")
    anywhere = pl.BlockSpec(memory_space=pl.ANY)
    return pl.pallas_call(
        functools.partial(exchange_kernel, count, outgoing, incoming),
        in_specs=[anywhere],
        out_specs=anywhere,
        out_shape=jax.ShapeDtypeStruct(out_shape, value.dtype),
        scratch_shapes=[
            pltpu.SemaphoreType.DMA((count,)),
            pltpu.SemaphoreType.DMA((count,)),
            pltpu.SemaphoreType.DMA,
        ],
        compiler_params=pltpu.CompilerParams(collective_id=tag, has_side_effects=True),
    )(value)


def to_sources(estimate):
    receivers, sources, samples = estimate.shape
    count = lax.axis_size("shot")
    own = sources // count
    return exchange(
        estimate,
        (receivers * count, own, samples),
        lambda peer: (slice(None), pl.ds(peer * own, own), slice(None)),
        lambda sender: (pl.ds(sender * receivers, receivers), slice(None), slice(None)),
        0,
    )


def receive_kernel(count, stages, src_ref, out_ref, halo_ref, send_sem, recv_sem, edge_sem, own_sem):
    part, own, samples = out_ref.shape[0], src_ref.shape[1], src_ref.shape[2]
    me = lax.axis_index("shot")
    row = lax.axis_index("tm")
    has_prev = row > 0
    has_next = row < stages - 1
    mesh_id = pl.DeviceIdType.MESH
    barrier = pltpu.get_barrier_semaphore()

    def greet(step, carry):
        peer = lax.rem(me + step, count)
        pl.semaphore_signal(barrier, 1, device_id=(peer, row), device_id_type=mesh_id)
        return carry

    lax.fori_loop(1, count, greet, 0)

    @pl.when(has_prev)
    def _():
        pl.semaphore_signal(barrier, 1, device_id=(me, row - 1), device_id_type=mesh_id)

    @pl.when(has_next)
    def _():
        pl.semaphore_signal(barrier, 1, device_id=(me, row + 1), device_id_type=mesh_id)

    pl.semaphore_wait(
        barrier, count - 1 + has_prev.astype(jnp.int32) + has_next.astype(jnp.int32)
    )
    body = (slice(None), pl.ds(me * own, own), pl.ds(0, samples))
    tail = (slice(None), pl.ds(me * own, own), pl.ds(samples, BLK))

    def chunk(peer, sender, stage):
        source = src_ref if stage == 0 else halo_ref
        target = body if stage == 0 else tail
        target = (target[0], pl.ds(sender * own, own), target[2])
        return pltpu.make_async_remote_copy(
            src_ref=source.at[pl.ds(peer * part, part)],
            dst_ref=out_ref.at[target],
            send_sem=send_sem.at[stage, peer],
            recv_sem=recv_sem.at[stage, sender],
            device_id=(peer, row),
            device_id_type=mesh_id,
        )

    mine = pltpu.make_async_copy(src_ref.at[pl.ds(me * part, part)], out_ref.at[body], own_sem.at[0])
    mine.start()

    def send_body(step, carry):
        chunk(lax.rem(me + step, count), me, 0).start()
        return carry

    lax.fori_loop(1, count, send_body, 0)

    def edge(target_row):
        return pltpu.make_async_remote_copy(
            src_ref=src_ref.at[:, :, pl.ds(0, BLK)],
            dst_ref=halo_ref,
            send_sem=edge_sem.at[0],
            recv_sem=edge_sem.at[1],
            device_id=(me, target_row),
            device_id_type=mesh_id,
        )

    pl.when(has_prev)(lambda: edge(row - 1).start())

    @pl.when(has_next)
    def _():
        edge(row + 1).wait_recv()
        theirs = pltpu.make_async_copy(
            halo_ref.at[pl.ds(me * part, part)], out_ref.at[tail], own_sem.at[1]
        )
        theirs.start()

        def send_tail(step, carry):
            chunk(lax.rem(me + step, count), me, 1).start()
            return carry

        lax.fori_loop(1, count, send_tail, 0)

        def finish_tail(step, carry):
            peer = lax.rem(me + step, count)
            chunk(peer, me, 1).wait_send()
            chunk(me, peer, 1).wait_recv()
            return carry

        lax.fori_loop(1, count, finish_tail, 0)
        theirs.wait()

    pl.when(has_prev)(lambda: edge(row - 1).wait_send())

    def finish_body(step, carry):
        peer = lax.rem(me + step, count)
        chunk(peer, me, 0).wait_send()
        chunk(me, peer, 0).wait_recv()
        return carry

    lax.fori_loop(1, count, finish_body, 0)
    mine.wait()


def to_receivers(records):
    receivers, own, samples = records.shape
    count = lax.axis_size("shot")
    part = receivers // count
    return pl.pallas_call(
        functools.partial(receive_kernel, count, lax.axis_size("tm")),
        in_specs=[pl.BlockSpec(memory_space=pl.ANY)],
        out_specs=pl.BlockSpec(memory_space=pl.ANY),
        out_shape=jax.ShapeDtypeStruct((part, own * count, samples + BLK), records.dtype),
        scratch_shapes=[
            pltpu.VMEM((receivers, own, BLK), records.dtype),
            pltpu.SemaphoreType.DMA((2, count)),
            pltpu.SemaphoreType.DMA((2, count)),
            pltpu.SemaphoreType.DMA((2,)),
            pltpu.SemaphoreType.DMA((2,)),
        ],
        compiler_params=pltpu.CompilerParams(collective_id=1, has_side_effects=True),
    )(records)


def local(blended, delays, thresholds):
    tables = filter_tables()
    extended = to_receivers(blended)
    row = lax.axis_index("tm")
    estimate, before, after = filter_with_halos(extended, delays, thresholds[0], tables)
    before = jnp.where(row == 0, jnp.zeros_like(before), before)
    last = row == lax.axis_size("tm") - 1
    after = jnp.where(last, jnp.zeros_like(after), after)
    return filter_and_send(estimate, before, after, extended, delays, thresholds[1], tables)


def solution(mesh):
    return jax.shard_map(
        local,
        mesh=mesh,
        in_specs=(P(None, "shot", "tm"), P(), P()),
        out_specs=P(None, "shot", "tm"),
        check_vma=False,
    )
```

```python
import functools
import math

import jax
import ml_dtypes
import numpy as np
import jax.numpy as jnp
from jax import lax
from jax.experimental import pallas as pl
from jax.experimental.pallas import tpu as pltpu
from jax.sharding import PartitionSpec as P

SRC = 64
SRC_EXP = 2
WIN = 256
BLK = 128
ITERS = 2


RELAX = 0.5


def shifted(array, axis, by):
    count = lax.axis_size(axis)
    pairs = [(i, i + by) for i in range(count) if 0 <= i + by < count]
    return lax.ppermute(array, axis, pairs)


def blend(estimate, earlier, own_delays):
    receivers, sources, samples = estimate.shape
    blocks = samples // BLK
    experiments = sources // SRC_EXP
    upper = estimate.reshape(receivers, sources, blocks, BLK)
    shifts = own_delays.reshape(-1)
    row_index = jnp.arange(BLK, dtype=jnp.int32)[None, :, None]
    column_index = jnp.arange(BLK, dtype=jnp.int32)[None, None, :]
    select_same = (row_index == column_index - shifts[:, None, None]).astype(jnp.bfloat16)
    select_prior = (row_index == BLK + column_index - shifts[:, None, None]).astype(jnp.bfloat16)
    same = jnp.einsum("rsnb,sbi->rsni", upper, select_same, preferred_element_type=jnp.float32)
    onward = jnp.einsum("rsnb,sbi->rsni", upper, select_prior, preferred_element_type=jnp.float32)
    edge_part = jnp.einsum(
        "rsb,sbi->rsi", earlier, select_prior, preferred_element_type=jnp.float32
    )
    same = jnp.sum(same.reshape(receivers, experiments, SRC_EXP, blocks, BLK), axis=2)
    onward = jnp.sum(onward.reshape(receivers, experiments, SRC_EXP, blocks, BLK), axis=2)
    edge_part = jnp.sum(edge_part.reshape(receivers, experiments, SRC_EXP, BLK), axis=2)
    carried = jnp.concatenate([edge_part[:, :, None], onward[:, :, : blocks - 1]], axis=2)
    return (same + carried).reshape(receivers, experiments, samples)


def spread(residual, later, own_delays):
    receivers, experiments, samples = residual.shape
    blocks = samples // BLK
    lower = residual.reshape(receivers, experiments, blocks, BLK)
    row_index = jnp.arange(BLK, dtype=jnp.int32)[None, None, :, None]
    column_index = jnp.arange(BLK, dtype=jnp.int32)[None, None, None, :]
    select_same = (row_index == column_index + own_delays[:, :, None, None]).astype(jnp.bfloat16)
    select_next = (row_index + BLK == column_index + own_delays[:, :, None, None]).astype(
        jnp.bfloat16
    )
    same = jnp.einsum("rena,ekai->rekni", lower, select_same, preferred_element_type=jnp.float32)
    backward = jnp.einsum(
        "rena,ekai->rekni", lower, select_next, preferred_element_type=jnp.float32
    )
    edge_part = jnp.einsum("rea,ekai->reki", later, select_next, preferred_element_type=jnp.float32)
    carried = jnp.concatenate([backward[:, :, :, 1:], edge_part[:, :, :, None]], axis=3)
    return (same + carried).reshape(receivers, experiments * SRC_EXP, samples)


def split(value):
    high = value.astype(jnp.bfloat16)
    return high, (value - high.astype(jnp.float32)).astype(jnp.bfloat16)


def exact_split(value):
    high = value.astype(ml_dtypes.bfloat16)
    low = (value - high.astype(np.float64)).astype(ml_dtypes.bfloat16)
    return jnp.asarray(high), jnp.asarray(low)


def filter_tables():
    turn = lambda n: (np.arange(n)[:, None] * np.arange(n)[None, :] % n) * (2.0 * np.pi / n)
    time_turn = turn(WIN)
    forward = jnp.asarray(
        np.concatenate([np.cos(time_turn), -np.sin(time_turn)], axis=1).astype(ml_dtypes.bfloat16)
    )
    inverse_high, inverse_low = exact_split(
        np.concatenate([np.cos(time_turn), -np.sin(time_turn)], axis=0) / math.sqrt(WIN)
    )
    inverse = jnp.concatenate([inverse_high, inverse_high, inverse_low], axis=0)
    source_turn = turn(SRC)
    cos_source = np.cos(source_turn) / math.sqrt(SRC)
    sin_source = np.sin(source_turn) / math.sqrt(SRC)
    mix_forward = exact_split(np.block([[cos_source, sin_source], [-sin_source, cos_source]]))
    mix_inverse = exact_split(np.block([[cos_source, -sin_source], [sin_source, cos_source]]))
    return forward, inverse, mix_forward, mix_inverse


def mix(table, value):
    table_high, table_low = table
    value_high, value_low = split(value)
    stacked = jnp.concatenate([value_high, value_low, value_high], axis=0)
    joined = jnp.concatenate([table_high, table_high, table_low], axis=1)
    return jnp.dot(joined, stacked, preferred_element_type=jnp.float32)


def filter_block(u_ref, first, count, tables, out_ref):
    forward_ref, inverse_ref, mfh_ref, mfl_ref, mih_ref, mil_ref, limit_ref = tables
    sources, samples = u_ref.shape[1:]
    windows = samples // WIN
    groups = [(r, w) for r in range(first, first + count) for w in range(windows)]
    scale = 1.0 / math.sqrt(WIN)
    rows = jnp.concatenate(
        [u_ref[r, :, w * WIN : (w + 1) * WIN] for r, w in groups], axis=0
    )
    spectrum = jnp.dot(rows, forward_ref[...], preferred_element_type=jnp.float32) * scale
    block = lambda g: slice(g * sources, (g + 1) * sources)
    field = jnp.concatenate(
        [
            jnp.concatenate([spectrum[block(g), :WIN], spectrum[block(g), WIN:]], axis=0)
            for g in range(len(groups))
        ],
        axis=1,
    )
    coeffs = mix((mfh_ref[...], mfl_ref[...]), field)
    real_part = coeffs[:sources]
    imag_part = coeffs[sources:]
    limit = limit_ref[...]
    magnitude = jnp.sqrt(real_part * real_part + imag_part * imag_part)
    factor = jnp.maximum(magnitude - limit, 0.0) / jnp.maximum(magnitude, limit)
    kept = jnp.concatenate([real_part * factor, imag_part * factor], axis=0)
    back = mix((mih_ref[...], mil_ref[...]), kept)
    lanes = lambda g: slice(g * WIN, (g + 1) * WIN)
    joined = jnp.concatenate(
        [
            jnp.concatenate([back[:sources, lanes(g)], back[sources:, lanes(g)]], axis=1)
            for g in range(len(groups))
        ],
        axis=0,
    )
    joined_high, joined_low = split(joined)
    restored = jnp.dot(
        jnp.concatenate([joined_high, joined_low, joined_high], axis=1),
        inverse_ref[...],
        preferred_element_type=jnp.float32,
    )
    for g, (r, w) in enumerate(groups):
        out_ref[r, :, w * WIN : (w + 1) * WIN] = restored[block(g)].astype(out_ref.dtype)


def pairs(rows, cols, transpose):
    row = lax.broadcasted_iota(jnp.int32, (rows, cols), 0)
    col = lax.broadcasted_iota(jnp.int32, (rows, cols), 1)
    hit = (col // SRC_EXP == row) if transpose else (row // SRC_EXP == col)
    return jnp.where(hit, 1.0, 0.0).astype(jnp.bfloat16)


def blend_residual(rec_ref, est_ref, before_ref, after_ref, shift_ref, last, res_ref, rows):
    receivers, experiments, width = rec_ref.shape
    pair = pairs(experiments, est_ref.shape[1], True)
    shift = shift_ref[...]
    lane = lax.broadcasted_iota(jnp.int32, (experiments, width), 1)
    drop = jnp.logical_and(lane >= width - BLK, last)
    for r in rows:
        moved = jnp.concatenate([before_ref[r], est_ref[r], after_ref[r]], axis=1).astype(jnp.float32)
        full = moved.shape[1]
        for bit in range((BLK - 1).bit_length()):
            amount = 1 << bit
            moved = jnp.where((shift & amount) != 0, pltpu.roll(moved, amount, 1), moved)
        summed = jnp.dot(
            pair, moved[:, full - width :].astype(jnp.bfloat16),
            preferred_element_type=jnp.float32,
        )
        residual = (rec_ref[r] - summed).astype(res_ref.dtype)
        res_ref[r] = jnp.where(drop, jnp.zeros_like(residual), residual)


def spread_update(res_ref, shift_ref, est_ref, u_ref, rows, last=None):
    receivers, sources, samples = u_ref.shape
    experiments, width = res_ref.shape[1:]
    shift = shift_ref[...]
    dup = pairs(sources, experiments, False)
    for r in rows:
        residual = res_ref[r]
        if last is not None:
            lane = lax.broadcasted_iota(jnp.int32, (experiments, width), 1)
            drop = jnp.logical_and(lane >= samples, last)
            residual = jnp.where(drop, jnp.zeros_like(residual), residual).astype(jnp.bfloat16)
        moved = jnp.dot(dup, residual, preferred_element_type=jnp.float32)
        for bit in range((BLK - 1).bit_length()):
            amount = 1 << bit
            rolled = pltpu.roll(moved, width - amount, 1)
            moved = jnp.where((shift & amount) != 0, rolled, moved)
        value = RELAX * moved[:, :samples]
        if est_ref is not None:
            value = est_ref[r].astype(jnp.float32) + value
        u_ref[r] = value.astype(u_ref.dtype)


def spread_inputs(residual, delays):
    return [residual, delays.reshape(-1, 1)]


def filter_kernel(u_ref, *refs):
    filter_block(u_ref, 0, u_ref.shape[0], refs[:7], refs[7])


def filter_halo_kernel(stages, res_ref, shift_ref, *refs):
    tables = refs[:7]
    out_ref, before_ref, after_ref, u_ref, send_sem, recv_sem = refs[7:]
    samples = u_ref.shape[2]
    shot = lax.axis_index("shot")
    row = lax.axis_index("tm")
    has_prev = row > 0
    has_next = row < stages - 1
    barrier = pltpu.get_barrier_semaphore()
    mesh_id = pl.DeviceIdType.MESH

    @pl.when(has_prev)
    def _():
        pl.semaphore_signal(barrier, 1, device_id=(shot, row - 1), device_id_type=mesh_id)

    @pl.when(has_next)
    def _():
        pl.semaphore_signal(barrier, 1, device_id=(shot, row + 1), device_id_type=mesh_id)

    spread_update(res_ref, shift_ref, None, u_ref, range(u_ref.shape[0]), jnp.logical_not(has_next))
    filter_block(u_ref, 0, u_ref.shape[0], tables, out_ref)
    pl.semaphore_wait(barrier, has_prev.astype(jnp.int32) + has_next.astype(jnp.int32))

    def to_prev():
        return pltpu.make_async_remote_copy(
            src_ref=out_ref.at[:, :, pl.ds(0, BLK)],
            dst_ref=after_ref,
            send_sem=send_sem.at[0],
            recv_sem=recv_sem.at[0],
            device_id=(shot, row - 1),
            device_id_type=mesh_id,
        )

    def to_next():
        return pltpu.make_async_remote_copy(
            src_ref=out_ref.at[:, :, pl.ds(samples - BLK, BLK)],
            dst_ref=before_ref,
            send_sem=send_sem.at[1],
            recv_sem=recv_sem.at[1],
            device_id=(shot, row + 1),
            device_id_type=mesh_id,
        )

    pl.when(has_prev)(lambda: to_prev().start())
    pl.when(has_next)(lambda: to_next().start())

    @pl.when(has_prev)
    def _():
        to_prev().wait_send()
        to_next().wait_recv()

    @pl.when(has_next)
    def _():
        to_next().wait_send()
        to_prev().wait_recv()


def filter_with_halos(residual, delays, limits, tables):
    forward, inverse, mix_forward, mix_inverse = tables
    receivers = residual.shape[0]
    sources = delays.size
    samples = residual.shape[2] - BLK
    stages = lax.axis_size("tm")
    vmem = pl.BlockSpec(memory_space=pltpu.VMEM)
    anywhere = pl.BlockSpec(memory_space=pl.ANY)
    edge = jax.ShapeDtypeStruct((receivers, sources, BLK), jnp.bfloat16)
    return pl.pallas_call(
        functools.partial(filter_halo_kernel, stages),
        in_specs=[vmem] * 9,
        out_specs=(vmem, anywhere, anywhere),
        out_shape=(jax.ShapeDtypeStruct((receivers, sources, samples), jnp.bfloat16), edge, edge),
        scratch_shapes=[
            pltpu.VMEM((receivers, sources, samples), jnp.bfloat16),
            pltpu.SemaphoreType.DMA((2,)),
            pltpu.SemaphoreType.DMA((2,)),
        ],
        compiler_params=pltpu.CompilerParams(
            collective_id=3, has_side_effects=True, vmem_limit_bytes=48 * 1024 * 1024
        ),
    )(
        *spread_inputs(residual, delays),
        forward, inverse, *mix_forward, *mix_inverse, limits.reshape(sources, 1),
    )


def filter_send_kernel(
    count, stages, halves, est_ref, before_ref, after_ref, rec_ref, shift_ref, *refs
):
    tables = refs[:7]
    out_ref, done_ref, u_ref, res_ref, send_sem, recv_sem, own_sem = refs[7:]
    receivers, sources, samples = u_ref.shape
    own = sources // count
    per = receivers // halves
    me = lax.axis_index("shot")
    row = lax.axis_index("tm")
    barrier = pltpu.get_barrier_semaphore()

    def greet(step, carry):
        peer = lax.rem(me + step, count)
        pl.semaphore_signal(barrier, 1, device_id=(peer, row), device_id_type=pl.DeviceIdType.MESH)
        return carry

    lax.fori_loop(1, count, greet, 0)
    last = lax.axis_index("tm") == stages - 1

    def remote(half, peer, sender):
        return pltpu.make_async_remote_copy(
            src_ref=done_ref.at[pl.ds(half * per, per), pl.ds(peer * own, own), :],
            dst_ref=out_ref.at[pl.ds(sender * receivers + half * per, per), :, :],
            send_sem=send_sem.at[half, peer],
            recv_sem=recv_sem.at[half, sender],
            device_id=(peer, row),
            device_id_type=pl.DeviceIdType.MESH,
        )

    locals_ = []
    for half in range(halves):
        rows = range(half * per, (half + 1) * per)
        blend_residual(rec_ref, est_ref, before_ref, after_ref, shift_ref, last, res_ref, rows)
        spread_update(res_ref, shift_ref, est_ref, u_ref, rows)
        filter_block(u_ref, half * per, per, tables, done_ref)
        if half == 0:
            pl.semaphore_wait(barrier, count - 1)
        mine = pltpu.make_async_copy(
            done_ref.at[pl.ds(half * per, per), pl.ds(me * own, own), :],
            out_ref.at[pl.ds(me * receivers + half * per, per), :, :],
            own_sem.at[half],
        )
        mine.start()
        locals_.append(mine)

        def send(step, carry, half=half):
            remote(half, lax.rem(me + step, count), me).start()
            return carry

        lax.fori_loop(1, count, send, 0)

    for half in range(halves):

        def finish(step, carry, half=half):
            peer = lax.rem(me + step, count)
            remote(half, peer, me).wait_send()
            remote(half, me, peer).wait_recv()
            return carry

        lax.fori_loop(1, count, finish, 0)
        locals_[half].wait()


def filter_and_send(estimate, before, after, records, delays, limits, tables):
    forward, inverse, mix_forward, mix_inverse = tables
    receivers, sources, samples = estimate.shape
    count = lax.axis_size("shot")
    halves = 2
    vmem = pl.BlockSpec(memory_space=pltpu.VMEM)
    return pl.pallas_call(
        functools.partial(filter_send_kernel, count, lax.axis_size("tm"), halves),
        in_specs=[vmem] * 12,
        out_specs=pl.BlockSpec(memory_space=pl.ANY),
        out_shape=jax.ShapeDtypeStruct(
            (receivers * count, sources // count, samples), jnp.bfloat16
        ),
        scratch_shapes=[
            pltpu.VMEM(estimate.shape, jnp.bfloat16),
            pltpu.VMEM(estimate.shape, jnp.bfloat16),
            pltpu.VMEM(records.shape, jnp.bfloat16),
            pltpu.SemaphoreType.DMA((halves, count)),
            pltpu.SemaphoreType.DMA((halves, count)),
            pltpu.SemaphoreType.DMA((halves,)),
        ],
        compiler_params=pltpu.CompilerParams(
            collective_id=2, has_side_effects=True, vmem_limit_bytes=48 * 1024 * 1024
        ),
    )(
        estimate,
        before,
        after,
        records,
        *spread_inputs(records, delays)[1:],
        forward, inverse, *mix_forward, *mix_inverse, limits.reshape(sources, 1),
    )


def coherence(gathers, limits, tables):
    forward, inverse, mix_forward, mix_inverse = tables
    receivers, sources, samples = gathers.shape
    vmem = pl.BlockSpec(memory_space=pltpu.VMEM)
    return pl.pallas_call(
        filter_kernel,
        in_specs=[vmem] * 8,
        out_specs=vmem,
        out_shape=jax.ShapeDtypeStruct(gathers.shape, jnp.bfloat16),
        compiler_params=pltpu.CompilerParams(vmem_limit_bytes=48 * 1024 * 1024),
    )(gathers, forward, inverse, *mix_forward, *mix_inverse, limits.reshape(sources, 1))


def exchange_kernel(count, outgoing, incoming, src_ref, out_ref, send_sem, recv_sem, own_sem):
    me = lax.axis_index("shot")
    row = lax.axis_index("tm")
    barrier = pltpu.get_barrier_semaphore()

    def greet(step, carry):
        peer = lax.rem(me + step, count)
        pl.semaphore_signal(barrier, 1, device_id=(peer, row), device_id_type=pl.DeviceIdType.MESH)
        return carry

    lax.fori_loop(1, count, greet, 0)
    pl.semaphore_wait(barrier, count - 1)
    own = pltpu.make_async_copy(src_ref.at[outgoing(me)], out_ref.at[incoming(me)], own_sem)
    own.start()

    def remote(peer, sender):
        return pltpu.make_async_remote_copy(
            src_ref=src_ref.at[outgoing(peer)],
            dst_ref=out_ref.at[incoming(sender)],
            send_sem=send_sem.at[peer],
            recv_sem=recv_sem.at[sender],
            device_id=(peer, row),
            device_id_type=pl.DeviceIdType.MESH,
        )

    def send(step, carry):
        remote(lax.rem(me + step, count), me).start()
        return carry

    lax.fori_loop(1, count, send, 0)

    def finish(step, carry):
        peer = lax.rem(me + step, count)
        remote(peer, me).wait_send()
        remote(me, peer).wait_recv()
        return carry

    lax.fori_loop(1, count, finish, 0)
    own.wait()


def exchange(value, out_shape, outgoing, incoming, tag):
    count = lax.axis_size("shot")
    anywhere = pl.BlockSpec(memory_space=pl.ANY)
    return pl.pallas_call(
        functools.partial(exchange_kernel, count, outgoing, incoming),
        in_specs=[anywhere],
        out_specs=anywhere,
        out_shape=jax.ShapeDtypeStruct(out_shape, value.dtype),
        scratch_shapes=[
            pltpu.SemaphoreType.DMA((count,)),
            pltpu.SemaphoreType.DMA((count,)),
            pltpu.SemaphoreType.DMA,
        ],
        compiler_params=pltpu.CompilerParams(collective_id=tag, has_side_effects=True),
    )(value)


def to_sources(estimate):
    receivers, sources, samples = estimate.shape
    count = lax.axis_size("shot")
    own = sources // count
    return exchange(
        estimate,
        (receivers * count, own, samples),
        lambda peer: (slice(None), pl.ds(peer * own, own), slice(None)),
        lambda sender: (pl.ds(sender * receivers, receivers), slice(None), slice(None)),
        0,
    )


def receive_kernel(count, stages, src_ref, out_ref, halo_ref, send_sem, recv_sem, edge_sem, own_sem):
    part, own, samples = out_ref.shape[0], src_ref.shape[1], src_ref.shape[2]
    me = lax.axis_index("shot")
    row = lax.axis_index("tm")
    has_prev = row > 0
    has_next = row < stages - 1
    mesh_id = pl.DeviceIdType.MESH
    barrier = pltpu.get_barrier_semaphore()

    def greet(step, carry):
        peer = lax.rem(me + step, count)
        pl.semaphore_signal(barrier, 1, device_id=(peer, row), device_id_type=mesh_id)
        return carry

    lax.fori_loop(1, count, greet, 0)

    @pl.when(has_prev)
    def _():
        pl.semaphore_signal(barrier, 1, device_id=(me, row - 1), device_id_type=mesh_id)

    @pl.when(has_next)
    def _():
        pl.semaphore_signal(barrier, 1, device_id=(me, row + 1), device_id_type=mesh_id)

    pl.semaphore_wait(
        barrier, count - 1 + has_prev.astype(jnp.int32) + has_next.astype(jnp.int32)
    )
    body = (slice(None), pl.ds(me * own, own), pl.ds(0, samples))
    tail = (slice(None), pl.ds(me * own, own), pl.ds(samples, BLK))

    def chunk(peer, sender, stage):
        source = src_ref if stage == 0 else halo_ref
        target = body if stage == 0 else tail
        target = (target[0], pl.ds(sender * own, own), target[2])
        return pltpu.make_async_remote_copy(
            src_ref=source.at[pl.ds(peer * part, part)],
            dst_ref=out_ref.at[target],
            send_sem=send_sem.at[stage, peer],
            recv_sem=recv_sem.at[stage, sender],
            device_id=(peer, row),
            device_id_type=mesh_id,
        )

    def edge(target_row):
        return pltpu.make_async_remote_copy(
            src_ref=src_ref.at[:, :, pl.ds(0, BLK)],
            dst_ref=halo_ref,
            send_sem=edge_sem.at[0],
            recv_sem=edge_sem.at[1],
            device_id=(me, target_row),
            device_id_type=mesh_id,
        )

    pl.when(has_prev)(lambda: edge(row - 1).start())

    mine = pltpu.make_async_copy(src_ref.at[pl.ds(me * part, part)], out_ref.at[body], own_sem.at[0])
    mine.start()

    def send_body(step, carry):
        chunk(lax.rem(me + step, count), me, 0).start()
        return carry

    lax.fori_loop(1, count, send_body, 0)


    @pl.when(has_next)
    def _():
        edge(row + 1).wait_recv()
        theirs = pltpu.make_async_copy(
            halo_ref.at[pl.ds(me * part, part)], out_ref.at[tail], own_sem.at[1]
        )
        theirs.start()

        def send_tail(step, carry):
            chunk(lax.rem(me + step, count), me, 1).start()
            return carry

        lax.fori_loop(1, count, send_tail, 0)

        def finish_tail(step, carry):
            peer = lax.rem(me + step, count)
            chunk(peer, me, 1).wait_send()
            chunk(me, peer, 1).wait_recv()
            return carry

        lax.fori_loop(1, count, finish_tail, 0)
        theirs.wait()

    pl.when(has_prev)(lambda: edge(row - 1).wait_send())

    def finish_body(step, carry):
        peer = lax.rem(me + step, count)
        chunk(peer, me, 0).wait_send()
        chunk(me, peer, 0).wait_recv()
        return carry

    lax.fori_loop(1, count, finish_body, 0)
    mine.wait()


def to_receivers(records):
    receivers, own, samples = records.shape
    count = lax.axis_size("shot")
    part = receivers // count
    return pl.pallas_call(
        functools.partial(receive_kernel, count, lax.axis_size("tm")),
        in_specs=[pl.BlockSpec(memory_space=pl.ANY)],
        out_specs=pl.BlockSpec(memory_space=pl.ANY),
        out_shape=jax.ShapeDtypeStruct((part, own * count, samples + BLK), records.dtype),
        scratch_shapes=[
            pltpu.VMEM((receivers, own, BLK), records.dtype),
            pltpu.SemaphoreType.DMA((2, count)),
            pltpu.SemaphoreType.DMA((2, count)),
            pltpu.SemaphoreType.DMA((2,)),
            pltpu.SemaphoreType.DMA((2,)),
        ],
        compiler_params=pltpu.CompilerParams(collective_id=1, has_side_effects=True),
    )(records)


def local(blended, delays, thresholds):
    tables = filter_tables()
    extended = to_receivers(blended)
    row = lax.axis_index("tm")
    estimate, before, after = filter_with_halos(extended, delays, thresholds[0], tables)
    before = jnp.where(row == 0, jnp.zeros_like(before), before)
    last = row == lax.axis_size("tm") - 1
    after = jnp.where(last, jnp.zeros_like(after), after)
    return filter_and_send(estimate, before, after, extended, delays, thresholds[1], tables)


def solution(mesh):
    return jax.shard_map(
        local,
        mesh=mesh,
        in_specs=(P(None, "shot", "tm"), P(), P()),
        out_specs=P(None, "shot", "tm"),
        check_vma=False,
    )
```

```python
import functools
import math

import jax
import ml_dtypes
import numpy as np
import jax.numpy as jnp
from jax import lax
from jax.experimental import pallas as pl
from jax.experimental.pallas import tpu as pltpu
from jax.sharding import PartitionSpec as P

SRC = 64
SRC_EXP = 2
WIN = 256
BLK = 128
ITERS = 2


RELAX = 0.5


def shifted(array, axis, by):
    count = lax.axis_size(axis)
    pairs = [(i, i + by) for i in range(count) if 0 <= i + by < count]
    return lax.ppermute(array, axis, pairs)


def blend(estimate, earlier, own_delays):
    receivers, sources, samples = estimate.shape
    blocks = samples // BLK
    experiments = sources // SRC_EXP
    upper = estimate.reshape(receivers, sources, blocks, BLK)
    shifts = own_delays.reshape(-1)
    row_index = jnp.arange(BLK, dtype=jnp.int32)[None, :, None]
    column_index = jnp.arange(BLK, dtype=jnp.int32)[None, None, :]
    select_same = (row_index == column_index - shifts[:, None, None]).astype(jnp.bfloat16)
    select_prior = (row_index == BLK + column_index - shifts[:, None, None]).astype(jnp.bfloat16)
    same = jnp.einsum("rsnb,sbi->rsni", upper, select_same, preferred_element_type=jnp.float32)
    onward = jnp.einsum("rsnb,sbi->rsni", upper, select_prior, preferred_element_type=jnp.float32)
    edge_part = jnp.einsum(
        "rsb,sbi->rsi", earlier, select_prior, preferred_element_type=jnp.float32
    )
    same = jnp.sum(same.reshape(receivers, experiments, SRC_EXP, blocks, BLK), axis=2)
    onward = jnp.sum(onward.reshape(receivers, experiments, SRC_EXP, blocks, BLK), axis=2)
    edge_part = jnp.sum(edge_part.reshape(receivers, experiments, SRC_EXP, BLK), axis=2)
    carried = jnp.concatenate([edge_part[:, :, None], onward[:, :, : blocks - 1]], axis=2)
    return (same + carried).reshape(receivers, experiments, samples)


def spread(residual, later, own_delays):
    receivers, experiments, samples = residual.shape
    blocks = samples // BLK
    lower = residual.reshape(receivers, experiments, blocks, BLK)
    row_index = jnp.arange(BLK, dtype=jnp.int32)[None, None, :, None]
    column_index = jnp.arange(BLK, dtype=jnp.int32)[None, None, None, :]
    select_same = (row_index == column_index + own_delays[:, :, None, None]).astype(jnp.bfloat16)
    select_next = (row_index + BLK == column_index + own_delays[:, :, None, None]).astype(
        jnp.bfloat16
    )
    same = jnp.einsum("rena,ekai->rekni", lower, select_same, preferred_element_type=jnp.float32)
    backward = jnp.einsum(
        "rena,ekai->rekni", lower, select_next, preferred_element_type=jnp.float32
    )
    edge_part = jnp.einsum("rea,ekai->reki", later, select_next, preferred_element_type=jnp.float32)
    carried = jnp.concatenate([backward[:, :, :, 1:], edge_part[:, :, :, None]], axis=3)
    return (same + carried).reshape(receivers, experiments * SRC_EXP, samples)


def split(value):
    high = value.astype(jnp.bfloat16)
    return high, (value - high.astype(jnp.float32)).astype(jnp.bfloat16)


def exact_split(value):
    high = value.astype(ml_dtypes.bfloat16)
    low = (value - high.astype(np.float64)).astype(ml_dtypes.bfloat16)
    return jnp.asarray(high), jnp.asarray(low)


def filter_tables():
    turn = lambda n: (np.arange(n)[:, None] * np.arange(n)[None, :] % n) * (2.0 * np.pi / n)
    time_turn = turn(WIN)
    forward = jnp.asarray(
        np.concatenate([np.cos(time_turn), -np.sin(time_turn)], axis=1).astype(ml_dtypes.bfloat16)
    )
    inverse_high, inverse_low = exact_split(
        np.concatenate([np.cos(time_turn), -np.sin(time_turn)], axis=0) / math.sqrt(WIN)
    )
    inverse = jnp.concatenate([inverse_high, inverse_high, inverse_low], axis=0)
    source_turn = turn(SRC)
    cos_source = np.cos(source_turn) / math.sqrt(SRC)
    sin_source = np.sin(source_turn) / math.sqrt(SRC)
    mix_forward = exact_split(np.block([[cos_source, sin_source], [-sin_source, cos_source]]))
    mix_inverse = exact_split(np.block([[cos_source, -sin_source], [sin_source, cos_source]]))
    return forward, inverse, mix_forward, mix_inverse


def mix(table, value):
    table_high, table_low = table
    value_high, value_low = split(value)
    stacked = jnp.concatenate([value_high, value_low, value_high], axis=0)
    joined = jnp.concatenate([table_high, table_high, table_low], axis=1)
    return jnp.dot(joined, stacked, preferred_element_type=jnp.float32)


def filter_block(u_ref, first, count, tables, out_ref, picked=None):
    forward_ref, inverse_ref, mfh_ref, mfl_ref, mih_ref, mil_ref, limit_ref = tables
    sources, samples = u_ref.shape[1:]
    windows = samples // WIN
    picked = range(windows) if picked is None else picked
    groups = [(r, w) for r in range(first, first + count) for w in picked]
    scale = 1.0 / math.sqrt(WIN)
    rows = jnp.concatenate(
        [u_ref[r, :, w * WIN : (w + 1) * WIN] for r, w in groups], axis=0
    )
    spectrum = jnp.dot(rows, forward_ref[...], preferred_element_type=jnp.float32) * scale
    block = lambda g: slice(g * sources, (g + 1) * sources)
    field = jnp.concatenate(
        [
            jnp.concatenate([spectrum[block(g), :WIN], spectrum[block(g), WIN:]], axis=0)
            for g in range(len(groups))
        ],
        axis=1,
    )
    coeffs = mix((mfh_ref[...], mfl_ref[...]), field)
    real_part = coeffs[:sources]
    imag_part = coeffs[sources:]
    limit = limit_ref[...]
    magnitude = jnp.sqrt(real_part * real_part + imag_part * imag_part)
    factor = jnp.maximum(magnitude - limit, 0.0) / jnp.maximum(magnitude, limit)
    kept = jnp.concatenate([real_part * factor, imag_part * factor], axis=0)
    back = mix((mih_ref[...], mil_ref[...]), kept)
    lanes = lambda g: slice(g * WIN, (g + 1) * WIN)
    joined = jnp.concatenate(
        [
            jnp.concatenate([back[:sources, lanes(g)], back[sources:, lanes(g)]], axis=1)
            for g in range(len(groups))
        ],
        axis=0,
    )
    joined_high, joined_low = split(joined)
    restored = jnp.dot(
        jnp.concatenate([joined_high, joined_low, joined_high], axis=1),
        inverse_ref[...],
        preferred_element_type=jnp.float32,
    )
    for g, (r, w) in enumerate(groups):
        out_ref[r, :, w * WIN : (w + 1) * WIN] = restored[block(g)].astype(out_ref.dtype)


def pairs(rows, cols, transpose):
    row = lax.broadcasted_iota(jnp.int32, (rows, cols), 0)
    col = lax.broadcasted_iota(jnp.int32, (rows, cols), 1)
    hit = (col // SRC_EXP == row) if transpose else (row // SRC_EXP == col)
    return jnp.where(hit, 1.0, 0.0).astype(jnp.bfloat16)


def blend_residual(rec_ref, est_ref, before_ref, after_ref, shift_ref, last, res_ref, rows):
    receivers, experiments, width = rec_ref.shape
    pair = pairs(experiments, est_ref.shape[1], True)
    shift = shift_ref[...]
    lane = lax.broadcasted_iota(jnp.int32, (experiments, width), 1)
    drop = jnp.logical_and(lane >= width - BLK, last)
    for r in rows:
        moved = jnp.concatenate([before_ref[r], est_ref[r], after_ref[r]], axis=1).astype(jnp.float32)
        full = moved.shape[1]
        for bit in range((BLK - 1).bit_length()):
            amount = 1 << bit
            moved = jnp.where((shift & amount) != 0, pltpu.roll(moved, amount, 1), moved)
        summed = jnp.dot(
            pair, moved[:, full - width :].astype(jnp.bfloat16),
            preferred_element_type=jnp.float32,
        )
        residual = (rec_ref[r] - summed).astype(res_ref.dtype)
        res_ref[r] = jnp.where(drop, jnp.zeros_like(residual), residual)


def spread_update(res_ref, shift_ref, est_ref, u_ref, rows, last=None):
    receivers, sources, samples = u_ref.shape
    experiments, width = res_ref.shape[1:]
    shift = shift_ref[...]
    dup = pairs(sources, experiments, False)
    for r in rows:
        residual = res_ref[r]
        if last is not None:
            lane = lax.broadcasted_iota(jnp.int32, (experiments, width), 1)
            drop = jnp.logical_and(lane >= samples, last)
            residual = jnp.where(drop, jnp.zeros_like(residual), residual).astype(jnp.bfloat16)
        moved = jnp.dot(dup, residual, preferred_element_type=jnp.float32)
        for bit in range((BLK - 1).bit_length()):
            amount = 1 << bit
            rolled = pltpu.roll(moved, width - amount, 1)
            moved = jnp.where((shift & amount) != 0, rolled, moved)
        value = RELAX * moved[:, :samples]
        if est_ref is not None:
            value = est_ref[r].astype(jnp.float32) + value
        u_ref[r] = value.astype(u_ref.dtype)


def spread_inputs(residual, delays):
    return [residual, delays.reshape(-1, 1)]


def filter_kernel(u_ref, *refs):
    filter_block(u_ref, 0, u_ref.shape[0], refs[:7], refs[7])


def filter_halo_kernel(stages, res_ref, shift_ref, *refs):
    tables = refs[:7]
    out_ref, before_ref, after_ref, u_ref, send_sem, recv_sem = refs[7:]
    samples = u_ref.shape[2]
    shot = lax.axis_index("shot")
    row = lax.axis_index("tm")
    has_prev = row > 0
    has_next = row < stages - 1
    barrier = pltpu.get_barrier_semaphore()
    mesh_id = pl.DeviceIdType.MESH

    @pl.when(has_prev)
    def _():
        pl.semaphore_signal(barrier, 1, device_id=(shot, row - 1), device_id_type=mesh_id)

    @pl.when(has_next)
    def _():
        pl.semaphore_signal(barrier, 1, device_id=(shot, row + 1), device_id_type=mesh_id)

    spread_update(res_ref, shift_ref, None, u_ref, range(u_ref.shape[0]), jnp.logical_not(has_next))
    windows = samples // WIN
    filter_block(u_ref, 0, u_ref.shape[0], tables, out_ref, (0, windows - 1))
    pl.semaphore_wait(barrier, has_prev.astype(jnp.int32) + has_next.astype(jnp.int32))

    def to_prev():
        return pltpu.make_async_remote_copy(
            src_ref=out_ref.at[:, :, pl.ds(0, BLK)],
            dst_ref=after_ref,
            send_sem=send_sem.at[0],
            recv_sem=recv_sem.at[0],
            device_id=(shot, row - 1),
            device_id_type=mesh_id,
        )

    def to_next():
        return pltpu.make_async_remote_copy(
            src_ref=out_ref.at[:, :, pl.ds(samples - BLK, BLK)],
            dst_ref=before_ref,
            send_sem=send_sem.at[1],
            recv_sem=recv_sem.at[1],
            device_id=(shot, row + 1),
            device_id_type=mesh_id,
        )

    pl.when(has_prev)(lambda: to_prev().start())
    pl.when(has_next)(lambda: to_next().start())
    filter_block(u_ref, 0, u_ref.shape[0], tables, out_ref, tuple(range(1, windows - 1)))

    @pl.when(has_prev)
    def _():
        to_prev().wait_send()
        to_next().wait_recv()

    @pl.when(has_next)
    def _():
        to_next().wait_send()
        to_prev().wait_recv()


def filter_with_halos(residual, delays, limits, tables):
    forward, inverse, mix_forward, mix_inverse = tables
    receivers = residual.shape[0]
    sources = delays.size
    samples = residual.shape[2] - BLK
    stages = lax.axis_size("tm")
    vmem = pl.BlockSpec(memory_space=pltpu.VMEM)
    anywhere = pl.BlockSpec(memory_space=pl.ANY)
    edge = jax.ShapeDtypeStruct((receivers, sources, BLK), jnp.bfloat16)
    return pl.pallas_call(
        functools.partial(filter_halo_kernel, stages),
        in_specs=[vmem] * 9,
        out_specs=(vmem, anywhere, anywhere),
        out_shape=(jax.ShapeDtypeStruct((receivers, sources, samples), jnp.bfloat16), edge, edge),
        scratch_shapes=[
            pltpu.VMEM((receivers, sources, samples), jnp.bfloat16),
            pltpu.SemaphoreType.DMA((2,)),
            pltpu.SemaphoreType.DMA((2,)),
        ],
        compiler_params=pltpu.CompilerParams(
            collective_id=3, has_side_effects=True, vmem_limit_bytes=48 * 1024 * 1024
        ),
    )(
        *spread_inputs(residual, delays),
        forward, inverse, *mix_forward, *mix_inverse, limits.reshape(sources, 1),
    )


def filter_send_kernel(
    count, stages, halves, est_ref, before_ref, after_ref, rec_ref, shift_ref, *refs
):
    tables = refs[:7]
    out_ref, done_ref, u_ref, res_ref, send_sem, recv_sem, own_sem = refs[7:]
    receivers, sources, samples = u_ref.shape
    own = sources // count
    per = receivers // halves
    me = lax.axis_index("shot")
    row = lax.axis_index("tm")
    barrier = pltpu.get_barrier_semaphore()

    def greet(step, carry):
        peer = lax.rem(me + step, count)
        pl.semaphore_signal(barrier, 1, device_id=(peer, row), device_id_type=pl.DeviceIdType.MESH)
        return carry

    lax.fori_loop(1, count, greet, 0)
    last = lax.axis_index("tm") == stages - 1

    def remote(half, peer, sender):
        return pltpu.make_async_remote_copy(
            src_ref=done_ref.at[pl.ds(half * per, per), pl.ds(peer * own, own), :],
            dst_ref=out_ref.at[pl.ds(sender * receivers + half * per, per), :, :],
            send_sem=send_sem.at[half, peer],
            recv_sem=recv_sem.at[half, sender],
            device_id=(peer, row),
            device_id_type=pl.DeviceIdType.MESH,
        )

    locals_ = []
    for half in range(halves):
        rows = range(half * per, (half + 1) * per)
        blend_residual(rec_ref, est_ref, before_ref, after_ref, shift_ref, last, res_ref, rows)
        spread_update(res_ref, shift_ref, est_ref, u_ref, rows)
        filter_block(u_ref, half * per, per, tables, done_ref)
        if half == 0:
            pl.semaphore_wait(barrier, count - 1)
        mine = pltpu.make_async_copy(
            done_ref.at[pl.ds(half * per, per), pl.ds(me * own, own), :],
            out_ref.at[pl.ds(me * receivers + half * per, per), :, :],
            own_sem.at[half],
        )
        mine.start()
        locals_.append(mine)

        def send(step, carry, half=half):
            remote(half, lax.rem(me + step, count), me).start()
            return carry

        lax.fori_loop(1, count, send, 0)

    for half in range(halves):

        def finish(step, carry, half=half):
            peer = lax.rem(me + step, count)
            remote(half, peer, me).wait_send()
            remote(half, me, peer).wait_recv()
            return carry

        lax.fori_loop(1, count, finish, 0)
        locals_[half].wait()


def filter_and_send(estimate, before, after, records, delays, limits, tables):
    forward, inverse, mix_forward, mix_inverse = tables
    receivers, sources, samples = estimate.shape
    count = lax.axis_size("shot")
    halves = 2
    vmem = pl.BlockSpec(memory_space=pltpu.VMEM)
    return pl.pallas_call(
        functools.partial(filter_send_kernel, count, lax.axis_size("tm"), halves),
        in_specs=[vmem] * 12,
        out_specs=pl.BlockSpec(memory_space=pl.ANY),
        out_shape=jax.ShapeDtypeStruct(
            (receivers * count, sources // count, samples), jnp.bfloat16
        ),
        scratch_shapes=[
            pltpu.VMEM(estimate.shape, jnp.bfloat16),
            pltpu.VMEM(estimate.shape, jnp.bfloat16),
            pltpu.VMEM(records.shape, jnp.bfloat16),
            pltpu.SemaphoreType.DMA((halves, count)),
            pltpu.SemaphoreType.DMA((halves, count)),
            pltpu.SemaphoreType.DMA((halves,)),
        ],
        compiler_params=pltpu.CompilerParams(
            collective_id=2, has_side_effects=True, vmem_limit_bytes=48 * 1024 * 1024
        ),
    )(
        estimate,
        before,
        after,
        records,
        *spread_inputs(records, delays)[1:],
        forward, inverse, *mix_forward, *mix_inverse, limits.reshape(sources, 1),
    )


def coherence(gathers, limits, tables):
    forward, inverse, mix_forward, mix_inverse = tables
    receivers, sources, samples = gathers.shape
    vmem = pl.BlockSpec(memory_space=pltpu.VMEM)
    return pl.pallas_call(
        filter_kernel,
        in_specs=[vmem] * 8,
        out_specs=vmem,
        out_shape=jax.ShapeDtypeStruct(gathers.shape, jnp.bfloat16),
        compiler_params=pltpu.CompilerParams(vmem_limit_bytes=48 * 1024 * 1024),
    )(gathers, forward, inverse, *mix_forward, *mix_inverse, limits.reshape(sources, 1))


def exchange_kernel(count, outgoing, incoming, src_ref, out_ref, send_sem, recv_sem, own_sem):
    me = lax.axis_index("shot")
    row = lax.axis_index("tm")
    barrier = pltpu.get_barrier_semaphore()

    def greet(step, carry):
        peer = lax.rem(me + step, count)
        pl.semaphore_signal(barrier, 1, device_id=(peer, row), device_id_type=pl.DeviceIdType.MESH)
        return carry

    lax.fori_loop(1, count, greet, 0)
    pl.semaphore_wait(barrier, count - 1)
    own = pltpu.make_async_copy(src_ref.at[outgoing(me)], out_ref.at[incoming(me)], own_sem)
    own.start()

    def remote(peer, sender):
        return pltpu.make_async_remote_copy(
            src_ref=src_ref.at[outgoing(peer)],
            dst_ref=out_ref.at[incoming(sender)],
            send_sem=send_sem.at[peer],
            recv_sem=recv_sem.at[sender],
            device_id=(peer, row),
            device_id_type=pl.DeviceIdType.MESH,
        )

    def send(step, carry):
        remote(lax.rem(me + step, count), me).start()
        return carry

    lax.fori_loop(1, count, send, 0)

    def finish(step, carry):
        peer = lax.rem(me + step, count)
        remote(peer, me).wait_send()
        remote(me, peer).wait_recv()
        return carry

    lax.fori_loop(1, count, finish, 0)
    own.wait()


def exchange(value, out_shape, outgoing, incoming, tag):
    count = lax.axis_size("shot")
    anywhere = pl.BlockSpec(memory_space=pl.ANY)
    return pl.pallas_call(
        functools.partial(exchange_kernel, count, outgoing, incoming),
        in_specs=[anywhere],
        out_specs=anywhere,
        out_shape=jax.ShapeDtypeStruct(out_shape, value.dtype),
        scratch_shapes=[
            pltpu.SemaphoreType.DMA((count,)),
            pltpu.SemaphoreType.DMA((count,)),
            pltpu.SemaphoreType.DMA,
        ],
        compiler_params=pltpu.CompilerParams(collective_id=tag, has_side_effects=True),
    )(value)


def to_sources(estimate):
    receivers, sources, samples = estimate.shape
    count = lax.axis_size("shot")
    own = sources // count
    return exchange(
        estimate,
        (receivers * count, own, samples),
        lambda peer: (slice(None), pl.ds(peer * own, own), slice(None)),
        lambda sender: (pl.ds(sender * receivers, receivers), slice(None), slice(None)),
        0,
    )


def receive_kernel(count, stages, src_ref, out_ref, halo_ref, send_sem, recv_sem, edge_sem, own_sem):
    part, own, samples = out_ref.shape[0], src_ref.shape[1], src_ref.shape[2]
    me = lax.axis_index("shot")
    row = lax.axis_index("tm")
    has_prev = row > 0
    has_next = row < stages - 1
    mesh_id = pl.DeviceIdType.MESH
    barrier = pltpu.get_barrier_semaphore()

    def greet(step, carry):
        peer = lax.rem(me + step, count)
        pl.semaphore_signal(barrier, 1, device_id=(peer, row), device_id_type=mesh_id)
        return carry

    lax.fori_loop(1, count, greet, 0)

    @pl.when(has_prev)
    def _():
        pl.semaphore_signal(barrier, 1, device_id=(me, row - 1), device_id_type=mesh_id)

    @pl.when(has_next)
    def _():
        pl.semaphore_signal(barrier, 1, device_id=(me, row + 1), device_id_type=mesh_id)

    pl.semaphore_wait(
        barrier, count - 1 + has_prev.astype(jnp.int32) + has_next.astype(jnp.int32)
    )
    body = (slice(None), pl.ds(me * own, own), pl.ds(0, samples))
    tail = (slice(None), pl.ds(me * own, own), pl.ds(samples, BLK))

    def chunk(peer, sender, stage):
        source = src_ref if stage == 0 else halo_ref
        target = body if stage == 0 else tail
        target = (target[0], pl.ds(sender * own, own), target[2])
        return pltpu.make_async_remote_copy(
            src_ref=source.at[pl.ds(peer * part, part)],
            dst_ref=out_ref.at[target],
            send_sem=send_sem.at[stage, peer],
            recv_sem=recv_sem.at[stage, sender],
            device_id=(peer, row),
            device_id_type=mesh_id,
        )

    mine = pltpu.make_async_copy(src_ref.at[pl.ds(me * part, part)], out_ref.at[body], own_sem.at[0])
    mine.start()

    def send_body(step, carry):
        chunk(lax.rem(me + step, count), me, 0).start()
        return carry

    lax.fori_loop(1, count, send_body, 0)

    def edge(target_row):
        return pltpu.make_async_remote_copy(
            src_ref=src_ref.at[:, :, pl.ds(0, BLK)],
            dst_ref=halo_ref,
            send_sem=edge_sem.at[0],
            recv_sem=edge_sem.at[1],
            device_id=(me, target_row),
            device_id_type=mesh_id,
        )

    pl.when(has_prev)(lambda: edge(row - 1).start())

    @pl.when(has_next)
    def _():
        edge(row + 1).wait_recv()
        theirs = pltpu.make_async_copy(
            halo_ref.at[pl.ds(me * part, part)], out_ref.at[tail], own_sem.at[1]
        )
        theirs.start()

        def send_tail(step, carry):
            chunk(lax.rem(me + step, count), me, 1).start()
            return carry

        lax.fori_loop(1, count, send_tail, 0)

        def finish_tail(step, carry):
            peer = lax.rem(me + step, count)
            chunk(peer, me, 1).wait_send()
            chunk(me, peer, 1).wait_recv()
            return carry

        lax.fori_loop(1, count, finish_tail, 0)
        theirs.wait()

    pl.when(has_prev)(lambda: edge(row - 1).wait_send())

    def finish_body(step, carry):
        peer = lax.rem(me + step, count)
        chunk(peer, me, 0).wait_send()
        chunk(me, peer, 0).wait_recv()
        return carry

    lax.fori_loop(1, count, finish_body, 0)
    mine.wait()


def to_receivers(records):
    receivers, own, samples = records.shape
    count = lax.axis_size("shot")
    part = receivers // count
    return pl.pallas_call(
        functools.partial(receive_kernel, count, lax.axis_size("tm")),
        in_specs=[pl.BlockSpec(memory_space=pl.ANY)],
        out_specs=pl.BlockSpec(memory_space=pl.ANY),
        out_shape=jax.ShapeDtypeStruct((part, own * count, samples + BLK), records.dtype),
        scratch_shapes=[
            pltpu.VMEM((receivers, own, BLK), records.dtype),
            pltpu.SemaphoreType.DMA((2, count)),
            pltpu.SemaphoreType.DMA((2, count)),
            pltpu.SemaphoreType.DMA((2,)),
            pltpu.SemaphoreType.DMA((2,)),
        ],
        compiler_params=pltpu.CompilerParams(collective_id=1, has_side_effects=True),
    )(records)


def local(blended, delays, thresholds):
    tables = filter_tables()
    extended = to_receivers(blended)
    row = lax.axis_index("tm")
    estimate, before, after = filter_with_halos(extended, delays, thresholds[0], tables)
    before = jnp.where(row == 0, jnp.zeros_like(before), before)
    last = row == lax.axis_size("tm") - 1
    after = jnp.where(last, jnp.zeros_like(after), after)
    return filter_and_send(estimate, before, after, extended, delays, thresholds[1], tables)


def solution(mesh):
    return jax.shard_map(
        local,
        mesh=mesh,
        in_specs=(P(None, "shot", "tm"), P(), P()),
        out_specs=P(None, "shot", "tm"),
        check_vma=False,
    )
```

```python
import functools
import math

import jax
import ml_dtypes
import numpy as np
import jax.numpy as jnp
from jax import lax
from jax.experimental import pallas as pl
from jax.experimental.pallas import tpu as pltpu
from jax.sharding import PartitionSpec as P

SRC = 64
SRC_EXP = 2
WIN = 256
BLK = 128
ITERS = 2


RELAX = 0.5


def shifted(array, axis, by):
    count = lax.axis_size(axis)
    pairs = [(i, i + by) for i in range(count) if 0 <= i + by < count]
    return lax.ppermute(array, axis, pairs)


def blend(estimate, earlier, own_delays):
    receivers, sources, samples = estimate.shape
    blocks = samples // BLK
    experiments = sources // SRC_EXP
    upper = estimate.reshape(receivers, sources, blocks, BLK)
    shifts = own_delays.reshape(-1)
    row_index = jnp.arange(BLK, dtype=jnp.int32)[None, :, None]
    column_index = jnp.arange(BLK, dtype=jnp.int32)[None, None, :]
    select_same = (row_index == column_index - shifts[:, None, None]).astype(jnp.bfloat16)
    select_prior = (row_index == BLK + column_index - shifts[:, None, None]).astype(jnp.bfloat16)
    same = jnp.einsum("rsnb,sbi->rsni", upper, select_same, preferred_element_type=jnp.float32)
    onward = jnp.einsum("rsnb,sbi->rsni", upper, select_prior, preferred_element_type=jnp.float32)
    edge_part = jnp.einsum(
        "rsb,sbi->rsi", earlier, select_prior, preferred_element_type=jnp.float32
    )
    same = jnp.sum(same.reshape(receivers, experiments, SRC_EXP, blocks, BLK), axis=2)
    onward = jnp.sum(onward.reshape(receivers, experiments, SRC_EXP, blocks, BLK), axis=2)
    edge_part = jnp.sum(edge_part.reshape(receivers, experiments, SRC_EXP, BLK), axis=2)
    carried = jnp.concatenate([edge_part[:, :, None], onward[:, :, : blocks - 1]], axis=2)
    return (same + carried).reshape(receivers, experiments, samples)


def spread(residual, later, own_delays):
    receivers, experiments, samples = residual.shape
    blocks = samples // BLK
    lower = residual.reshape(receivers, experiments, blocks, BLK)
    row_index = jnp.arange(BLK, dtype=jnp.int32)[None, None, :, None]
    column_index = jnp.arange(BLK, dtype=jnp.int32)[None, None, None, :]
    select_same = (row_index == column_index + own_delays[:, :, None, None]).astype(jnp.bfloat16)
    select_next = (row_index + BLK == column_index + own_delays[:, :, None, None]).astype(
        jnp.bfloat16
    )
    same = jnp.einsum("rena,ekai->rekni", lower, select_same, preferred_element_type=jnp.float32)
    backward = jnp.einsum(
        "rena,ekai->rekni", lower, select_next, preferred_element_type=jnp.float32
    )
    edge_part = jnp.einsum("rea,ekai->reki", later, select_next, preferred_element_type=jnp.float32)
    carried = jnp.concatenate([backward[:, :, :, 1:], edge_part[:, :, :, None]], axis=3)
    return (same + carried).reshape(receivers, experiments * SRC_EXP, samples)


def split(value):
    high = value.astype(jnp.bfloat16)
    return high, (value - high.astype(jnp.float32)).astype(jnp.bfloat16)


def exact_split(value):
    high = value.astype(ml_dtypes.bfloat16)
    low = (value - high.astype(np.float64)).astype(ml_dtypes.bfloat16)
    return jnp.asarray(high), jnp.asarray(low)


def filter_tables():
    turn = lambda n: (np.arange(n)[:, None] * np.arange(n)[None, :] % n) * (2.0 * np.pi / n)
    time_turn = turn(WIN)
    forward = jnp.asarray(
        np.concatenate([np.cos(time_turn), -np.sin(time_turn)], axis=1).astype(ml_dtypes.bfloat16)
    )
    inverse_high, inverse_low = exact_split(
        np.concatenate([np.cos(time_turn), -np.sin(time_turn)], axis=0) / math.sqrt(WIN)
    )
    inverse = jnp.concatenate([inverse_high, inverse_high, inverse_low], axis=0)
    source_turn = turn(SRC)
    cos_source = np.cos(source_turn) / math.sqrt(SRC)
    sin_source = np.sin(source_turn) / math.sqrt(SRC)
    mix_forward = exact_split(np.block([[cos_source, sin_source], [-sin_source, cos_source]]))
    mix_inverse = exact_split(np.block([[cos_source, -sin_source], [sin_source, cos_source]]))
    return forward, inverse, mix_forward, mix_inverse


def mix(table, value):
    table_high, table_low = table
    value_high, value_low = split(value)
    stacked = jnp.concatenate([value_high, value_low, value_high], axis=0)
    joined = jnp.concatenate([table_high, table_high, table_low], axis=1)
    return jnp.dot(joined, stacked, preferred_element_type=jnp.float32)


def filter_block(u_ref, first, count, tables, out_ref, picked=None):
    forward_ref, inverse_ref, mfh_ref, mfl_ref, mih_ref, mil_ref, limit_ref = tables
    sources, samples = u_ref.shape[1:]
    windows = samples // WIN
    picked = range(windows) if picked is None else picked
    groups = [(r, w) for r in range(first, first + count) for w in picked]
    scale = 1.0 / math.sqrt(WIN)
    rows = jnp.concatenate(
        [u_ref[r, :, w * WIN : (w + 1) * WIN] for r, w in groups], axis=0
    )
    spectrum = jnp.dot(rows, forward_ref[...], preferred_element_type=jnp.float32) * scale
    block = lambda g: slice(g * sources, (g + 1) * sources)
    field = jnp.concatenate(
        [
            jnp.concatenate([spectrum[block(g), :WIN], spectrum[block(g), WIN:]], axis=0)
            for g in range(len(groups))
        ],
        axis=1,
    )
    coeffs = mix((mfh_ref[...], mfl_ref[...]), field)
    real_part = coeffs[:sources]
    imag_part = coeffs[sources:]
    limit = limit_ref[...]
    magnitude = jnp.sqrt(real_part * real_part + imag_part * imag_part)
    factor = jnp.maximum(magnitude - limit, 0.0) / jnp.maximum(magnitude, limit)
    kept = jnp.concatenate([real_part * factor, imag_part * factor], axis=0)
    back = mix((mih_ref[...], mil_ref[...]), kept)
    lanes = lambda g: slice(g * WIN, (g + 1) * WIN)
    joined = jnp.concatenate(
        [
            jnp.concatenate([back[:sources, lanes(g)], back[sources:, lanes(g)]], axis=1)
            for g in range(len(groups))
        ],
        axis=0,
    )
    joined_high, joined_low = split(joined)
    restored = jnp.dot(
        jnp.concatenate([joined_high, joined_low, joined_high], axis=1),
        inverse_ref[...],
        preferred_element_type=jnp.float32,
    )
    for g, (r, w) in enumerate(groups):
        out_ref[r, :, w * WIN : (w + 1) * WIN] = restored[block(g)].astype(out_ref.dtype)


def pairs(rows, cols, transpose):
    row = lax.broadcasted_iota(jnp.int32, (rows, cols), 0)
    col = lax.broadcasted_iota(jnp.int32, (rows, cols), 1)
    hit = (col // SRC_EXP == row) if transpose else (row // SRC_EXP == col)
    return jnp.where(hit, 1.0, 0.0).astype(jnp.bfloat16)


def blend_residual(rec_ref, est_ref, before_ref, after_ref, shift_ref, last, res_ref, rows):
    receivers, experiments, width = rec_ref.shape
    pair = pairs(experiments, est_ref.shape[1], True)
    shift = shift_ref[...]
    lane = lax.broadcasted_iota(jnp.int32, (experiments, width), 1)
    drop = jnp.logical_and(lane >= width - BLK, last)
    for r in rows:
        moved = jnp.concatenate([before_ref[r], est_ref[r], after_ref[r]], axis=1).astype(jnp.float32)
        full = moved.shape[1]
        for bit in range((BLK - 1).bit_length()):
            amount = 1 << bit
            moved = jnp.where((shift & amount) != 0, pltpu.roll(moved, amount, 1), moved)
        summed = jnp.dot(
            pair, moved[:, full - width :].astype(jnp.bfloat16),
            preferred_element_type=jnp.float32,
        )
        residual = (rec_ref[r] - summed).astype(res_ref.dtype)
        res_ref[r] = jnp.where(drop, jnp.zeros_like(residual), residual)


def spread_update(res_ref, shift_ref, est_ref, u_ref, rows, last=None):
    receivers, sources, samples = u_ref.shape
    experiments, width = res_ref.shape[1:]
    shift = shift_ref[...]
    dup = pairs(sources, experiments, False)
    for r in rows:
        residual = res_ref[r]
        if last is not None:
            lane = lax.broadcasted_iota(jnp.int32, (experiments, width), 1)
            drop = jnp.logical_and(lane >= samples, last)
            residual = jnp.where(drop, jnp.zeros_like(residual), residual).astype(jnp.bfloat16)
        moved = jnp.dot(dup, residual, preferred_element_type=jnp.float32)
        for bit in range((BLK - 1).bit_length()):
            amount = 1 << bit
            rolled = pltpu.roll(moved, width - amount, 1)
            moved = jnp.where((shift & amount) != 0, rolled, moved)
        value = RELAX * moved[:, :samples]
        if est_ref is not None:
            value = est_ref[r].astype(jnp.float32) + value
        u_ref[r] = value.astype(u_ref.dtype)


def spread_inputs(residual, delays):
    return [residual, delays.reshape(-1, 1)]


def filter_kernel(u_ref, *refs):
    filter_block(u_ref, 0, u_ref.shape[0], refs[:7], refs[7])


def filter_halo_kernel(stages, res_ref, shift_ref, *refs):
    tables = refs[:7]
    out_ref, before_ref, after_ref, u_ref, send_sem, recv_sem = refs[7:]
    samples = u_ref.shape[2]
    shot = lax.axis_index("shot")
    row = lax.axis_index("tm")
    has_prev = row > 0
    has_next = row < stages - 1
    barrier = pltpu.get_barrier_semaphore()
    mesh_id = pl.DeviceIdType.MESH

    @pl.when(has_prev)
    def _():
        pl.semaphore_signal(barrier, 1, device_id=(shot, row - 1), device_id_type=mesh_id)

    @pl.when(has_next)
    def _():
        pl.semaphore_signal(barrier, 1, device_id=(shot, row + 1), device_id_type=mesh_id)

    spread_update(res_ref, shift_ref, None, u_ref, range(u_ref.shape[0]), jnp.logical_not(has_next))
    windows = samples // WIN
    filter_block(u_ref, 0, u_ref.shape[0], tables, out_ref, (0, windows - 1))
    pl.semaphore_wait(barrier, has_prev.astype(jnp.int32) + has_next.astype(jnp.int32))

    def to_prev():
        return pltpu.make_async_remote_copy(
            src_ref=out_ref.at[:, :, pl.ds(0, BLK)],
            dst_ref=after_ref,
            send_sem=send_sem.at[0],
            recv_sem=recv_sem.at[0],
            device_id=(shot, row - 1),
            device_id_type=mesh_id,
        )

    def to_next():
        return pltpu.make_async_remote_copy(
            src_ref=out_ref.at[:, :, pl.ds(samples - BLK, BLK)],
            dst_ref=before_ref,
            send_sem=send_sem.at[1],
            recv_sem=recv_sem.at[1],
            device_id=(shot, row + 1),
            device_id_type=mesh_id,
        )

    pl.when(has_prev)(lambda: to_prev().start())
    pl.when(has_next)(lambda: to_next().start())
    filter_block(u_ref, 0, u_ref.shape[0], tables, out_ref, tuple(range(1, windows - 1)))

    @pl.when(has_prev)
    def _():
        to_prev().wait_send()
        to_next().wait_recv()

    @pl.when(has_next)
    def _():
        to_next().wait_send()
        to_prev().wait_recv()


def filter_with_halos(residual, delays, limits, tables):
    forward, inverse, mix_forward, mix_inverse = tables
    receivers = residual.shape[0]
    sources = delays.size
    samples = residual.shape[2] - BLK
    stages = lax.axis_size("tm")
    vmem = pl.BlockSpec(memory_space=pltpu.VMEM)
    anywhere = pl.BlockSpec(memory_space=pl.ANY)
    edge = jax.ShapeDtypeStruct((receivers, sources, BLK), jnp.bfloat16)
    return pl.pallas_call(
        functools.partial(filter_halo_kernel, stages),
        in_specs=[vmem] * 9,
        out_specs=(vmem, anywhere, anywhere),
        out_shape=(jax.ShapeDtypeStruct((receivers, sources, samples), jnp.bfloat16), edge, edge),
        scratch_shapes=[
            pltpu.VMEM((receivers, sources, samples), jnp.bfloat16),
            pltpu.SemaphoreType.DMA((2,)),
            pltpu.SemaphoreType.DMA((2,)),
        ],
        compiler_params=pltpu.CompilerParams(
            collective_id=3, has_side_effects=True, vmem_limit_bytes=48 * 1024 * 1024
        ),
    )(
        *spread_inputs(residual, delays),
        forward, inverse, *mix_forward, *mix_inverse, limits.reshape(sources, 1),
    )


def filter_send_kernel(
    count, stages, halves, est_ref, before_ref, after_ref, rec_ref, shift_ref, *refs
):
    tables = refs[:7]
    out_ref, done_ref, u_ref, res_ref, send_sem, recv_sem, own_sem = refs[7:]
    receivers, sources, samples = u_ref.shape
    own = sources // count
    per = receivers // halves
    me = lax.axis_index("shot")
    row = lax.axis_index("tm")
    barrier = pltpu.get_barrier_semaphore()

    def greet(step, carry):
        peer = lax.rem(me + step, count)
        pl.semaphore_signal(barrier, 1, device_id=(peer, row), device_id_type=pl.DeviceIdType.MESH)
        return carry

    lax.fori_loop(1, count, greet, 0)
    last = lax.axis_index("tm") == stages - 1

    def remote(half, peer, sender):
        return pltpu.make_async_remote_copy(
            src_ref=done_ref.at[pl.ds(half * per, per), pl.ds(peer * own, own), :],
            dst_ref=out_ref.at[pl.ds(sender * receivers + half * per, per), :, :],
            send_sem=send_sem.at[half, peer],
            recv_sem=recv_sem.at[half, sender],
            device_id=(peer, row),
            device_id_type=pl.DeviceIdType.MESH,
        )

    locals_ = []
    for half in range(halves):
        rows = range(half * per, (half + 1) * per)
        blend_residual(rec_ref, est_ref, before_ref, after_ref, shift_ref, last, res_ref, rows)
        spread_update(res_ref, shift_ref, est_ref, u_ref, rows)
        filter_block(u_ref, half * per, per, tables, done_ref)
        if half == 0:
            pl.semaphore_wait(barrier, count - 1)
        mine = pltpu.make_async_copy(
            done_ref.at[pl.ds(half * per, per), pl.ds(me * own, own), :],
            out_ref.at[pl.ds(me * receivers + half * per, per), :, :],
            own_sem.at[half],
        )
        mine.start()
        locals_.append(mine)

        def send(step, carry, half=half):
            remote(half, lax.rem(me + step, count), me).start()
            return carry

        lax.fori_loop(1, count, send, 0)

    for half in range(halves):

        def finish(step, carry, half=half):
            peer = lax.rem(me + step, count)
            remote(half, peer, me).wait_send()
            remote(half, me, peer).wait_recv()
            return carry

        lax.fori_loop(1, count, finish, 0)
        locals_[half].wait()


def filter_and_send(estimate, before, after, records, delays, limits, tables):
    forward, inverse, mix_forward, mix_inverse = tables
    receivers, sources, samples = estimate.shape
    count = lax.axis_size("shot")
    halves = 2
    vmem = pl.BlockSpec(memory_space=pltpu.VMEM)
    return pl.pallas_call(
        functools.partial(filter_send_kernel, count, lax.axis_size("tm"), halves),
        in_specs=[vmem] * 12,
        out_specs=pl.BlockSpec(memory_space=pl.ANY),
        out_shape=jax.ShapeDtypeStruct(
            (receivers * count, sources // count, samples), jnp.bfloat16
        ),
        scratch_shapes=[
            pltpu.VMEM(estimate.shape, jnp.bfloat16),
            pltpu.VMEM(estimate.shape, jnp.bfloat16),
            pltpu.VMEM(records.shape, jnp.bfloat16),
            pltpu.SemaphoreType.DMA((halves, count)),
            pltpu.SemaphoreType.DMA((halves, count)),
            pltpu.SemaphoreType.DMA((halves,)),
        ],
        compiler_params=pltpu.CompilerParams(
            collective_id=2, has_side_effects=True, vmem_limit_bytes=48 * 1024 * 1024
        ),
    )(
        estimate,
        before,
        after,
        records,
        *spread_inputs(records, delays)[1:],
        forward, inverse, *mix_forward, *mix_inverse, limits.reshape(sources, 1),
    )


def coherence(gathers, limits, tables):
    forward, inverse, mix_forward, mix_inverse = tables
    receivers, sources, samples = gathers.shape
    vmem = pl.BlockSpec(memory_space=pltpu.VMEM)
    return pl.pallas_call(
        filter_kernel,
        in_specs=[vmem] * 8,
        out_specs=vmem,
        out_shape=jax.ShapeDtypeStruct(gathers.shape, jnp.bfloat16),
        compiler_params=pltpu.CompilerParams(vmem_limit_bytes=48 * 1024 * 1024),
    )(gathers, forward, inverse, *mix_forward, *mix_inverse, limits.reshape(sources, 1))


def exchange_kernel(count, outgoing, incoming, src_ref, out_ref, send_sem, recv_sem, own_sem):
    me = lax.axis_index("shot")
    row = lax.axis_index("tm")
    barrier = pltpu.get_barrier_semaphore()

    def greet(step, carry):
        peer = lax.rem(me + step, count)
        pl.semaphore_signal(barrier, 1, device_id=(peer, row), device_id_type=pl.DeviceIdType.MESH)
        return carry

    lax.fori_loop(1, count, greet, 0)
    pl.semaphore_wait(barrier, count - 1)
    own = pltpu.make_async_copy(src_ref.at[outgoing(me)], out_ref.at[incoming(me)], own_sem)
    own.start()

    def remote(peer, sender):
        return pltpu.make_async_remote_copy(
            src_ref=src_ref.at[outgoing(peer)],
            dst_ref=out_ref.at[incoming(sender)],
            send_sem=send_sem.at[peer],
            recv_sem=recv_sem.at[sender],
            device_id=(peer, row),
            device_id_type=pl.DeviceIdType.MESH,
        )

    def send(step, carry):
        remote(lax.rem(me + step, count), me).start()
        return carry

    lax.fori_loop(1, count, send, 0)

    def finish(step, carry):
        peer = lax.rem(me + step, count)
        remote(peer, me).wait_send()
        remote(me, peer).wait_recv()
        return carry

    lax.fori_loop(1, count, finish, 0)
    own.wait()


def exchange(value, out_shape, outgoing, incoming, tag):
    count = lax.axis_size("shot")
    anywhere = pl.BlockSpec(memory_space=pl.ANY)
    return pl.pallas_call(
        functools.partial(exchange_kernel, count, outgoing, incoming),
        in_specs=[anywhere],
        out_specs=anywhere,
        out_shape=jax.ShapeDtypeStruct(out_shape, value.dtype),
        scratch_shapes=[
            pltpu.SemaphoreType.DMA((count,)),
            pltpu.SemaphoreType.DMA((count,)),
            pltpu.SemaphoreType.DMA,
        ],
        compiler_params=pltpu.CompilerParams(collective_id=tag, has_side_effects=True),
    )(value)


def to_sources(estimate):
    receivers, sources, samples = estimate.shape
    count = lax.axis_size("shot")
    own = sources // count
    return exchange(
        estimate,
        (receivers * count, own, samples),
        lambda peer: (slice(None), pl.ds(peer * own, own), slice(None)),
        lambda sender: (pl.ds(sender * receivers, receivers), slice(None), slice(None)),
        0,
    )


def receive_kernel(count, stages, src_ref, out_ref, send_sem, recv_sem, own_sem):
    part, own, samples = out_ref.shape[0], src_ref.shape[1], src_ref.shape[2]
    me = lax.axis_index("shot")
    row = lax.axis_index("tm")
    has_prev = row > 0
    has_next = row < stages - 1
    mesh_id = pl.DeviceIdType.MESH
    barrier = pltpu.get_barrier_semaphore()

    def greet(step, carry):
        peer = lax.rem(me + step, count)
        pl.semaphore_signal(barrier, 1, device_id=(peer, row), device_id_type=mesh_id)
        return carry

    lax.fori_loop(1, count, greet, 0)

    def greet_row(target_row):
        def one(peer, carry):
            pl.semaphore_signal(barrier, 1, device_id=(peer, target_row), device_id_type=mesh_id)
            return carry

        lax.fori_loop(0, count, one, 0)

    pl.when(has_prev)(lambda: greet_row(row - 1))
    pl.when(has_next)(lambda: greet_row(row + 1))
    pl.semaphore_wait(
        barrier,
        count - 1 + count * (has_prev.astype(jnp.int32) + has_next.astype(jnp.int32)),
    )

    def body(sender):
        return (slice(None), pl.ds(sender * own, own), pl.ds(0, samples))

    def tail(sender):
        return (slice(None), pl.ds(sender * own, own), pl.ds(samples, BLK))

    def chunk(peer, sender):
        return pltpu.make_async_remote_copy(
            src_ref=src_ref.at[pl.ds(peer * part, part)],
            dst_ref=out_ref.at[body(sender)],
            send_sem=send_sem.at[0, peer],
            recv_sem=recv_sem.at[0, sender],
            device_id=(peer, row),
            device_id_type=mesh_id,
        )

    def edge(peer, sender, target_row):
        return pltpu.make_async_remote_copy(
            src_ref=src_ref.at[pl.ds(peer * part, part), :, pl.ds(0, BLK)],
            dst_ref=out_ref.at[tail(sender)],
            send_sem=send_sem.at[1, peer],
            recv_sem=recv_sem.at[1, sender],
            device_id=(peer, target_row),
            device_id_type=mesh_id,
        )

    @pl.when(has_prev)
    def _():
        def send_edge(peer, carry):
            edge(peer, me, row - 1).start()
            return carry

        lax.fori_loop(0, count, send_edge, 0)

    mine = pltpu.make_async_copy(src_ref.at[pl.ds(me * part, part)], out_ref.at[body(me)], own_sem)
    mine.start()

    def send_body(step, carry):
        chunk(lax.rem(me + step, count), me).start()
        return carry

    lax.fori_loop(1, count, send_body, 0)

    @pl.when(has_prev)
    def _():
        def finish_edge(peer, carry):
            edge(peer, me, row - 1).wait_send()
            return carry

        lax.fori_loop(0, count, finish_edge, 0)

    @pl.when(has_next)
    def _():
        def land_edge(sender, carry):
            edge(me, sender, row + 1).wait_recv()
            return carry

        lax.fori_loop(0, count, land_edge, 0)

    def finish_body(step, carry):
        peer = lax.rem(me + step, count)
        chunk(peer, me).wait_send()
        chunk(me, peer).wait_recv()
        return carry

    lax.fori_loop(1, count, finish_body, 0)
    mine.wait()


def to_receivers(records):
    receivers, own, samples = records.shape
    count = lax.axis_size("shot")
    part = receivers // count
    return pl.pallas_call(
        functools.partial(receive_kernel, count, lax.axis_size("tm")),
        in_specs=[pl.BlockSpec(memory_space=pl.ANY)],
        out_specs=pl.BlockSpec(memory_space=pl.ANY),
        out_shape=jax.ShapeDtypeStruct((part, own * count, samples + BLK), records.dtype),
        scratch_shapes=[
            pltpu.SemaphoreType.DMA((2, count)),
            pltpu.SemaphoreType.DMA((2, count)),
            pltpu.SemaphoreType.DMA,
        ],
        compiler_params=pltpu.CompilerParams(collective_id=1, has_side_effects=True),
    )(records)


def local(blended, delays, thresholds):
    tables = filter_tables()
    extended = to_receivers(blended)
    row = lax.axis_index("tm")
    estimate, before, after = filter_with_halos(extended, delays, thresholds[0], tables)
    before = jnp.where(row == 0, jnp.zeros_like(before), before)
    last = row == lax.axis_size("tm") - 1
    after = jnp.where(last, jnp.zeros_like(after), after)
    return filter_and_send(estimate, before, after, extended, delays, thresholds[1], tables)


def solution(mesh):
    return jax.shard_map(
        local,
        mesh=mesh,
        in_specs=(P(None, "shot", "tm"), P(), P()),
        out_specs=P(None, "shot", "tm"),
        check_vma=False,
    )
```

```python
import functools
import math

import jax
import ml_dtypes
import numpy as np
import jax.numpy as jnp
from jax import lax
from jax.experimental import pallas as pl
from jax.experimental.pallas import tpu as pltpu
from jax.sharding import PartitionSpec as P

SRC = 64
SRC_EXP = 2
WIN = 256
BLK = 128
ITERS = 2


RELAX = 0.5


def shifted(array, axis, by):
    count = lax.axis_size(axis)
    pairs = [(i, i + by) for i in range(count) if 0 <= i + by < count]
    return lax.ppermute(array, axis, pairs)


def blend(estimate, earlier, own_delays):
    receivers, sources, samples = estimate.shape
    blocks = samples // BLK
    experiments = sources // SRC_EXP
    upper = estimate.reshape(receivers, sources, blocks, BLK)
    shifts = own_delays.reshape(-1)
    row_index = jnp.arange(BLK, dtype=jnp.int32)[None, :, None]
    column_index = jnp.arange(BLK, dtype=jnp.int32)[None, None, :]
    select_same = (row_index == column_index - shifts[:, None, None]).astype(jnp.bfloat16)
    select_prior = (row_index == BLK + column_index - shifts[:, None, None]).astype(jnp.bfloat16)
    same = jnp.einsum("rsnb,sbi->rsni", upper, select_same, preferred_element_type=jnp.float32)
    onward = jnp.einsum("rsnb,sbi->rsni", upper, select_prior, preferred_element_type=jnp.float32)
    edge_part = jnp.einsum(
        "rsb,sbi->rsi", earlier, select_prior, preferred_element_type=jnp.float32
    )
    same = jnp.sum(same.reshape(receivers, experiments, SRC_EXP, blocks, BLK), axis=2)
    onward = jnp.sum(onward.reshape(receivers, experiments, SRC_EXP, blocks, BLK), axis=2)
    edge_part = jnp.sum(edge_part.reshape(receivers, experiments, SRC_EXP, BLK), axis=2)
    carried = jnp.concatenate([edge_part[:, :, None], onward[:, :, : blocks - 1]], axis=2)
    return (same + carried).reshape(receivers, experiments, samples)


def spread(residual, later, own_delays):
    receivers, experiments, samples = residual.shape
    blocks = samples // BLK
    lower = residual.reshape(receivers, experiments, blocks, BLK)
    row_index = jnp.arange(BLK, dtype=jnp.int32)[None, None, :, None]
    column_index = jnp.arange(BLK, dtype=jnp.int32)[None, None, None, :]
    select_same = (row_index == column_index + own_delays[:, :, None, None]).astype(jnp.bfloat16)
    select_next = (row_index + BLK == column_index + own_delays[:, :, None, None]).astype(
        jnp.bfloat16
    )
    same = jnp.einsum("rena,ekai->rekni", lower, select_same, preferred_element_type=jnp.float32)
    backward = jnp.einsum(
        "rena,ekai->rekni", lower, select_next, preferred_element_type=jnp.float32
    )
    edge_part = jnp.einsum("rea,ekai->reki", later, select_next, preferred_element_type=jnp.float32)
    carried = jnp.concatenate([backward[:, :, :, 1:], edge_part[:, :, :, None]], axis=3)
    return (same + carried).reshape(receivers, experiments * SRC_EXP, samples)


def split(value):
    high = value.astype(jnp.bfloat16)
    return high, (value - high.astype(jnp.float32)).astype(jnp.bfloat16)


def exact_split(value):
    high = value.astype(ml_dtypes.bfloat16)
    low = (value - high.astype(np.float64)).astype(ml_dtypes.bfloat16)
    return jnp.asarray(high), jnp.asarray(low)


def filter_tables():
    turn = lambda n: (np.arange(n)[:, None] * np.arange(n)[None, :] % n) * (2.0 * np.pi / n)
    time_turn = turn(WIN)
    forward = jnp.asarray(
        np.concatenate([np.cos(time_turn), -np.sin(time_turn)], axis=1).astype(ml_dtypes.bfloat16)
    )
    inverse_high, inverse_low = exact_split(
        np.concatenate([np.cos(time_turn), -np.sin(time_turn)], axis=0) / math.sqrt(WIN)
    )
    inverse = jnp.concatenate([inverse_high, inverse_high, inverse_low], axis=0)
    source_turn = turn(SRC)
    cos_source = np.cos(source_turn) / math.sqrt(SRC)
    sin_source = np.sin(source_turn) / math.sqrt(SRC)
    mix_forward = exact_split(np.block([[cos_source, sin_source], [-sin_source, cos_source]]))
    mix_inverse = exact_split(np.block([[cos_source, -sin_source], [sin_source, cos_source]]))
    return forward, inverse, mix_forward, mix_inverse


def mix(table, value):
    table_high, table_low = table
    value_high, value_low = split(value)
    stacked = jnp.concatenate([value_high, value_low, value_high], axis=0)
    joined = jnp.concatenate([table_high, table_high, table_low], axis=1)
    return jnp.dot(joined, stacked, preferred_element_type=jnp.float32)


def filter_block(u_ref, first, count, tables, out_ref, picked=None):
    forward_ref, inverse_ref, mfh_ref, mfl_ref, mih_ref, mil_ref, limit_ref = tables
    sources, samples = u_ref.shape[1:]
    windows = samples // WIN
    picked = range(windows) if picked is None else picked
    groups = [(r, w) for r in range(first, first + count) for w in picked]
    scale = 1.0 / math.sqrt(WIN)
    rows = jnp.concatenate(
        [u_ref[r, :, w * WIN : (w + 1) * WIN] for r, w in groups], axis=0
    )
    spectrum = jnp.dot(rows, forward_ref[...], preferred_element_type=jnp.float32) * scale
    block = lambda g: slice(g * sources, (g + 1) * sources)
    field = jnp.concatenate(
        [
            jnp.concatenate([spectrum[block(g), :WIN], spectrum[block(g), WIN:]], axis=0)
            for g in range(len(groups))
        ],
        axis=1,
    )
    coeffs = mix((mfh_ref[...], mfl_ref[...]), field)
    real_part = coeffs[:sources]
    imag_part = coeffs[sources:]
    limit = limit_ref[...]
    magnitude = jnp.sqrt(real_part * real_part + imag_part * imag_part)
    factor = jnp.maximum(magnitude - limit, 0.0) / jnp.maximum(magnitude, limit)
    kept = jnp.concatenate([real_part * factor, imag_part * factor], axis=0)
    back = mix((mih_ref[...], mil_ref[...]), kept)
    lanes = lambda g: slice(g * WIN, (g + 1) * WIN)
    joined = jnp.concatenate(
        [
            jnp.concatenate([back[:sources, lanes(g)], back[sources:, lanes(g)]], axis=1)
            for g in range(len(groups))
        ],
        axis=0,
    )
    joined_high, joined_low = split(joined)
    restored = jnp.dot(
        jnp.concatenate([joined_high, joined_low, joined_high], axis=1),
        inverse_ref[...],
        preferred_element_type=jnp.float32,
    )
    for g, (r, w) in enumerate(groups):
        out_ref[r, :, w * WIN : (w + 1) * WIN] = restored[block(g)].astype(out_ref.dtype)


def pairs(rows, cols, transpose):
    row = lax.broadcasted_iota(jnp.int32, (rows, cols), 0)
    col = lax.broadcasted_iota(jnp.int32, (rows, cols), 1)
    hit = (col // SRC_EXP == row) if transpose else (row // SRC_EXP == col)
    return jnp.where(hit, 1.0, 0.0).astype(jnp.bfloat16)


def blend_residual(rec_ref, est_ref, before_ref, after_ref, shift_ref, last, res_ref, rows):
    receivers, experiments, width = rec_ref.shape
    pair = pairs(experiments, est_ref.shape[1], True)
    shift = shift_ref[...]
    lane = lax.broadcasted_iota(jnp.int32, (experiments, width), 1)
    drop = jnp.logical_and(lane >= width - BLK, last)
    for r in rows:
        moved = jnp.concatenate([before_ref[r], est_ref[r], after_ref[r]], axis=1).astype(jnp.float32)
        full = moved.shape[1]
        for bit in range((BLK - 1).bit_length()):
            amount = 1 << bit
            moved = jnp.where((shift & amount) != 0, pltpu.roll(moved, amount, 1), moved)
        summed = jnp.dot(
            pair, moved[:, full - width :].astype(jnp.bfloat16),
            preferred_element_type=jnp.float32,
        )
        residual = (rec_ref[r] - summed).astype(res_ref.dtype)
        res_ref[r] = jnp.where(drop, jnp.zeros_like(residual), residual)


def spread_update(res_ref, shift_ref, est_ref, u_ref, rows, last=None):
    receivers, sources, samples = u_ref.shape
    experiments, width = res_ref.shape[1:]
    shift = shift_ref[...]
    dup = pairs(sources, experiments, False)
    for r in rows:
        residual = res_ref[r]
        if last is not None:
            lane = lax.broadcasted_iota(jnp.int32, (experiments, width), 1)
            drop = jnp.logical_and(lane >= samples, last)
            residual = jnp.where(drop, jnp.zeros_like(residual), residual).astype(jnp.bfloat16)
        moved = jnp.dot(dup, residual, preferred_element_type=jnp.float32)
        for bit in range((BLK - 1).bit_length()):
            amount = 1 << bit
            rolled = pltpu.roll(moved, width - amount, 1)
            moved = jnp.where((shift & amount) != 0, rolled, moved)
        value = RELAX * moved[:, :samples]
        if est_ref is not None:
            value = est_ref[r].astype(jnp.float32) + value
        u_ref[r] = value.astype(u_ref.dtype)


def spread_inputs(residual, delays):
    return [residual, delays.reshape(-1, 1)]


def filter_kernel(u_ref, *refs):
    filter_block(u_ref, 0, u_ref.shape[0], refs[:7], refs[7])


def filter_halo_kernel(stages, res_ref, shift_ref, *refs):
    tables = refs[:7]
    out_ref, before_ref, after_ref, u_ref, send_sem, recv_sem = refs[7:]
    samples = u_ref.shape[2]
    shot = lax.axis_index("shot")
    row = lax.axis_index("tm")
    has_prev = row > 0
    has_next = row < stages - 1
    barrier = pltpu.get_barrier_semaphore()
    mesh_id = pl.DeviceIdType.MESH

    @pl.when(has_prev)
    def _():
        pl.semaphore_signal(barrier, 1, device_id=(shot, row - 1), device_id_type=mesh_id)

    @pl.when(has_next)
    def _():
        pl.semaphore_signal(barrier, 1, device_id=(shot, row + 1), device_id_type=mesh_id)

    spread_update(res_ref, shift_ref, None, u_ref, range(u_ref.shape[0]), jnp.logical_not(has_next))
    windows = samples // WIN
    filter_block(u_ref, 0, u_ref.shape[0], tables, out_ref, (0, windows - 1))
    pl.semaphore_wait(barrier, has_prev.astype(jnp.int32) + has_next.astype(jnp.int32))

    def to_prev():
        return pltpu.make_async_remote_copy(
            src_ref=out_ref.at[:, :, pl.ds(0, BLK)],
            dst_ref=after_ref,
            send_sem=send_sem.at[0],
            recv_sem=recv_sem.at[0],
            device_id=(shot, row - 1),
            device_id_type=mesh_id,
        )

    def to_next():
        return pltpu.make_async_remote_copy(
            src_ref=out_ref.at[:, :, pl.ds(samples - BLK, BLK)],
            dst_ref=before_ref,
            send_sem=send_sem.at[1],
            recv_sem=recv_sem.at[1],
            device_id=(shot, row + 1),
            device_id_type=mesh_id,
        )

    pl.when(has_prev)(lambda: to_prev().start())
    pl.when(has_next)(lambda: to_next().start())
    filter_block(u_ref, 0, u_ref.shape[0], tables, out_ref, tuple(range(1, windows - 1)))

    @pl.when(has_prev)
    def _():
        to_prev().wait_send()
        to_next().wait_recv()

    @pl.when(has_next)
    def _():
        to_next().wait_send()
        to_prev().wait_recv()


def filter_with_halos(residual, delays, limits, tables):
    forward, inverse, mix_forward, mix_inverse = tables
    receivers = residual.shape[0]
    sources = delays.size
    samples = residual.shape[2] - BLK
    stages = lax.axis_size("tm")
    vmem = pl.BlockSpec(memory_space=pltpu.VMEM)
    anywhere = pl.BlockSpec(memory_space=pl.ANY)
    edge = jax.ShapeDtypeStruct((receivers, sources, BLK), jnp.bfloat16)
    return pl.pallas_call(
        functools.partial(filter_halo_kernel, stages),
        in_specs=[vmem] * 9,
        out_specs=(vmem, anywhere, anywhere),
        out_shape=(jax.ShapeDtypeStruct((receivers, sources, samples), jnp.bfloat16), edge, edge),
        scratch_shapes=[
            pltpu.VMEM((receivers, sources, samples), jnp.bfloat16),
            pltpu.SemaphoreType.DMA((2,)),
            pltpu.SemaphoreType.DMA((2,)),
        ],
        compiler_params=pltpu.CompilerParams(
            collective_id=3, has_side_effects=True, vmem_limit_bytes=48 * 1024 * 1024
        ),
    )(
        *spread_inputs(residual, delays),
        forward, inverse, *mix_forward, *mix_inverse, limits.reshape(sources, 1),
    )


def filter_send_kernel(
    count, stages, halves, est_ref, before_ref, after_ref, rec_ref, shift_ref, *refs
):
    tables = refs[:7]
    out_ref, done_ref, u_ref, res_ref, send_sem, recv_sem, own_sem = refs[7:]
    receivers, sources, samples = u_ref.shape
    own = sources // count
    parts = [(0, 1), (1, receivers - 1)]
    me = lax.axis_index("shot")
    row = lax.axis_index("tm")
    barrier = pltpu.get_barrier_semaphore()

    def greet(step, carry):
        peer = lax.rem(me + step, count)
        pl.semaphore_signal(barrier, 1, device_id=(peer, row), device_id_type=pl.DeviceIdType.MESH)
        return carry

    lax.fori_loop(1, count, greet, 0)
    last = lax.axis_index("tm") == stages - 1

    def remote(half, peer, sender):
        return pltpu.make_async_remote_copy(
            src_ref=done_ref.at[pl.ds(parts[half][0], parts[half][1]), pl.ds(peer * own, own), :],
            dst_ref=out_ref.at[pl.ds(sender * receivers + parts[half][0], parts[half][1]), :, :],
            send_sem=send_sem.at[half, peer],
            recv_sem=recv_sem.at[half, sender],
            device_id=(peer, row),
            device_id_type=pl.DeviceIdType.MESH,
        )

    locals_ = []
    for half in range(halves):
        first, size = parts[half]
        rows = range(first, first + size)
        blend_residual(rec_ref, est_ref, before_ref, after_ref, shift_ref, last, res_ref, rows)
        spread_update(res_ref, shift_ref, est_ref, u_ref, rows)
        filter_block(u_ref, first, size, tables, done_ref)
        if half == 0:
            pl.semaphore_wait(barrier, count - 1)
        mine = pltpu.make_async_copy(
            done_ref.at[pl.ds(first, size), pl.ds(me * own, own), :],
            out_ref.at[pl.ds(me * receivers + first, size), :, :],
            own_sem.at[half],
        )
        mine.start()
        locals_.append(mine)

        def send(step, carry, half=half):
            remote(half, lax.rem(me + step, count), me).start()
            return carry

        lax.fori_loop(1, count, send, 0)

    for half in range(halves):

        def finish(step, carry, half=half):
            peer = lax.rem(me + step, count)
            remote(half, peer, me).wait_send()
            remote(half, me, peer).wait_recv()
            return carry

        lax.fori_loop(1, count, finish, 0)
        locals_[half].wait()


def filter_and_send(estimate, before, after, records, delays, limits, tables):
    forward, inverse, mix_forward, mix_inverse = tables
    receivers, sources, samples = estimate.shape
    count = lax.axis_size("shot")
    halves = 2
    vmem = pl.BlockSpec(memory_space=pltpu.VMEM)
    return pl.pallas_call(
        functools.partial(filter_send_kernel, count, lax.axis_size("tm"), halves),
        in_specs=[vmem] * 12,
        out_specs=pl.BlockSpec(memory_space=pl.ANY),
        out_shape=jax.ShapeDtypeStruct(
            (receivers * count, sources // count, samples), jnp.bfloat16
        ),
        scratch_shapes=[
            pltpu.VMEM(estimate.shape, jnp.bfloat16),
            pltpu.VMEM(estimate.shape, jnp.bfloat16),
            pltpu.VMEM(records.shape, jnp.bfloat16),
            pltpu.SemaphoreType.DMA((halves, count)),
            pltpu.SemaphoreType.DMA((halves, count)),
            pltpu.SemaphoreType.DMA((halves,)),
        ],
        compiler_params=pltpu.CompilerParams(
            collective_id=2, has_side_effects=True, vmem_limit_bytes=48 * 1024 * 1024
        ),
    )(
        estimate,
        before,
        after,
        records,
        *spread_inputs(records, delays)[1:],
        forward, inverse, *mix_forward, *mix_inverse, limits.reshape(sources, 1),
    )


def coherence(gathers, limits, tables):
    forward, inverse, mix_forward, mix_inverse = tables
    receivers, sources, samples = gathers.shape
    vmem = pl.BlockSpec(memory_space=pltpu.VMEM)
    return pl.pallas_call(
        filter_kernel,
        in_specs=[vmem] * 8,
        out_specs=vmem,
        out_shape=jax.ShapeDtypeStruct(gathers.shape, jnp.bfloat16),
        compiler_params=pltpu.CompilerParams(vmem_limit_bytes=48 * 1024 * 1024),
    )(gathers, forward, inverse, *mix_forward, *mix_inverse, limits.reshape(sources, 1))


def exchange_kernel(count, outgoing, incoming, src_ref, out_ref, send_sem, recv_sem, own_sem):
    me = lax.axis_index("shot")
    row = lax.axis_index("tm")
    barrier = pltpu.get_barrier_semaphore()

    def greet(step, carry):
        peer = lax.rem(me + step, count)
        pl.semaphore_signal(barrier, 1, device_id=(peer, row), device_id_type=pl.DeviceIdType.MESH)
        return carry

    lax.fori_loop(1, count, greet, 0)
    pl.semaphore_wait(barrier, count - 1)
    own = pltpu.make_async_copy(src_ref.at[outgoing(me)], out_ref.at[incoming(me)], own_sem)
    own.start()

    def remote(peer, sender):
        return pltpu.make_async_remote_copy(
            src_ref=src_ref.at[outgoing(peer)],
            dst_ref=out_ref.at[incoming(sender)],
            send_sem=send_sem.at[peer],
            recv_sem=recv_sem.at[sender],
            device_id=(peer, row),
            device_id_type=pl.DeviceIdType.MESH,
        )

    def send(step, carry):
        remote(lax.rem(me + step, count), me).start()
        return carry

    lax.fori_loop(1, count, send, 0)

    def finish(step, carry):
        peer = lax.rem(me + step, count)
        remote(peer, me).wait_send()
        remote(me, peer).wait_recv()
        return carry

    lax.fori_loop(1, count, finish, 0)
    own.wait()


def exchange(value, out_shape, outgoing, incoming, tag):
    count = lax.axis_size("shot")
    anywhere = pl.BlockSpec(memory_space=pl.ANY)
    return pl.pallas_call(
        functools.partial(exchange_kernel, count, outgoing, incoming),
        in_specs=[anywhere],
        out_specs=anywhere,
        out_shape=jax.ShapeDtypeStruct(out_shape, value.dtype),
        scratch_shapes=[
            pltpu.SemaphoreType.DMA((count,)),
            pltpu.SemaphoreType.DMA((count,)),
            pltpu.SemaphoreType.DMA,
        ],
        compiler_params=pltpu.CompilerParams(collective_id=tag, has_side_effects=True),
    )(value)


def to_sources(estimate):
    receivers, sources, samples = estimate.shape
    count = lax.axis_size("shot")
    own = sources // count
    return exchange(
        estimate,
        (receivers * count, own, samples),
        lambda peer: (slice(None), pl.ds(peer * own, own), slice(None)),
        lambda sender: (pl.ds(sender * receivers, receivers), slice(None), slice(None)),
        0,
    )


def receive_kernel(count, stages, src_ref, out_ref, send_sem, recv_sem, own_sem):
    part, own, samples = out_ref.shape[0], src_ref.shape[1], src_ref.shape[2]
    me = lax.axis_index("shot")
    row = lax.axis_index("tm")
    has_prev = row > 0
    has_next = row < stages - 1
    mesh_id = pl.DeviceIdType.MESH
    barrier = pltpu.get_barrier_semaphore()

    def greet(step, carry):
        peer = lax.rem(me + step, count)
        pl.semaphore_signal(barrier, 1, device_id=(peer, row), device_id_type=mesh_id)
        return carry

    lax.fori_loop(1, count, greet, 0)

    def greet_row(target_row):
        def one(peer, carry):
            pl.semaphore_signal(barrier, 1, device_id=(peer, target_row), device_id_type=mesh_id)
            return carry

        lax.fori_loop(0, count, one, 0)

    pl.when(has_prev)(lambda: greet_row(row - 1))
    pl.when(has_next)(lambda: greet_row(row + 1))
    pl.semaphore_wait(
        barrier,
        count - 1 + count * (has_prev.astype(jnp.int32) + has_next.astype(jnp.int32)),
    )

    def body(sender):
        return (slice(None), pl.ds(sender * own, own), pl.ds(0, samples))

    def tail(sender):
        return (slice(None), pl.ds(sender * own, own), pl.ds(samples, BLK))

    def chunk(peer, sender):
        return pltpu.make_async_remote_copy(
            src_ref=src_ref.at[pl.ds(peer * part, part)],
            dst_ref=out_ref.at[body(sender)],
            send_sem=send_sem.at[0, peer],
            recv_sem=recv_sem.at[0, sender],
            device_id=(peer, row),
            device_id_type=mesh_id,
        )

    def edge(peer, sender, target_row):
        return pltpu.make_async_remote_copy(
            src_ref=src_ref.at[pl.ds(peer * part, part), :, pl.ds(0, BLK)],
            dst_ref=out_ref.at[tail(sender)],
            send_sem=send_sem.at[1, peer],
            recv_sem=recv_sem.at[1, sender],
            device_id=(peer, target_row),
            device_id_type=mesh_id,
        )

    @pl.when(has_prev)
    def _():
        def send_edge(peer, carry):
            edge(peer, me, row - 1).start()
            return carry

        lax.fori_loop(0, count, send_edge, 0)

    mine = pltpu.make_async_copy(src_ref.at[pl.ds(me * part, part)], out_ref.at[body(me)], own_sem)
    mine.start()

    def send_body(step, carry):
        chunk(lax.rem(me + step, count), me).start()
        return carry

    lax.fori_loop(1, count, send_body, 0)

    @pl.when(has_prev)
    def _():
        def finish_edge(peer, carry):
            edge(peer, me, row - 1).wait_send()
            return carry

        lax.fori_loop(0, count, finish_edge, 0)

    @pl.when(has_next)
    def _():
        def land_edge(sender, carry):
            edge(me, sender, row + 1).wait_recv()
            return carry

        lax.fori_loop(0, count, land_edge, 0)

    def finish_body(step, carry):
        peer = lax.rem(me + step, count)
        chunk(peer, me).wait_send()
        chunk(me, peer).wait_recv()
        return carry

    lax.fori_loop(1, count, finish_body, 0)
    mine.wait()


def to_receivers(records):
    receivers, own, samples = records.shape
    count = lax.axis_size("shot")
    part = receivers // count
    return pl.pallas_call(
        functools.partial(receive_kernel, count, lax.axis_size("tm")),
        in_specs=[pl.BlockSpec(memory_space=pl.ANY)],
        out_specs=pl.BlockSpec(memory_space=pl.ANY),
        out_shape=jax.ShapeDtypeStruct((part, own * count, samples + BLK), records.dtype),
        scratch_shapes=[
            pltpu.SemaphoreType.DMA((2, count)),
            pltpu.SemaphoreType.DMA((2, count)),
            pltpu.SemaphoreType.DMA,
        ],
        compiler_params=pltpu.CompilerParams(collective_id=1, has_side_effects=True),
    )(records)


def local(blended, delays, thresholds):
    tables = filter_tables()
    extended = to_receivers(blended)
    row = lax.axis_index("tm")
    estimate, before, after = filter_with_halos(extended, delays, thresholds[0], tables)
    before = jnp.where(row == 0, jnp.zeros_like(before), before)
    last = row == lax.axis_size("tm") - 1
    after = jnp.where(last, jnp.zeros_like(after), after)
    return filter_and_send(estimate, before, after, extended, delays, thresholds[1], tables)


def solution(mesh):
    return jax.shard_map(
        local,
        mesh=mesh,
        in_specs=(P(None, "shot", "tm"), P(), P()),
        out_specs=P(None, "shot", "tm"),
        check_vma=False,
    )
```

```python
import functools
import math

import jax
import ml_dtypes
import numpy as np
import jax.numpy as jnp
from jax import lax
from jax.experimental import pallas as pl
from jax.experimental.pallas import tpu as pltpu
from jax.sharding import PartitionSpec as P

SRC = 64
SRC_EXP = 2
WIN = 256
BLK = 128
ITERS = 2


RELAX = 0.5


def shifted(array, axis, by):
    count = lax.axis_size(axis)
    pairs = [(i, i + by) for i in range(count) if 0 <= i + by < count]
    return lax.ppermute(array, axis, pairs)


def blend(estimate, earlier, own_delays):
    receivers, sources, samples = estimate.shape
    blocks = samples // BLK
    experiments = sources // SRC_EXP
    upper = estimate.reshape(receivers, sources, blocks, BLK)
    shifts = own_delays.reshape(-1)
    row_index = jnp.arange(BLK, dtype=jnp.int32)[None, :, None]
    column_index = jnp.arange(BLK, dtype=jnp.int32)[None, None, :]
    select_same = (row_index == column_index - shifts[:, None, None]).astype(jnp.bfloat16)
    select_prior = (row_index == BLK + column_index - shifts[:, None, None]).astype(jnp.bfloat16)
    same = jnp.einsum("rsnb,sbi->rsni", upper, select_same, preferred_element_type=jnp.float32)
    onward = jnp.einsum("rsnb,sbi->rsni", upper, select_prior, preferred_element_type=jnp.float32)
    edge_part = jnp.einsum(
        "rsb,sbi->rsi", earlier, select_prior, preferred_element_type=jnp.float32
    )
    same = jnp.sum(same.reshape(receivers, experiments, SRC_EXP, blocks, BLK), axis=2)
    onward = jnp.sum(onward.reshape(receivers, experiments, SRC_EXP, blocks, BLK), axis=2)
    edge_part = jnp.sum(edge_part.reshape(receivers, experiments, SRC_EXP, BLK), axis=2)
    carried = jnp.concatenate([edge_part[:, :, None], onward[:, :, : blocks - 1]], axis=2)
    return (same + carried).reshape(receivers, experiments, samples)


def spread(residual, later, own_delays):
    receivers, experiments, samples = residual.shape
    blocks = samples // BLK
    lower = residual.reshape(receivers, experiments, blocks, BLK)
    row_index = jnp.arange(BLK, dtype=jnp.int32)[None, None, :, None]
    column_index = jnp.arange(BLK, dtype=jnp.int32)[None, None, None, :]
    select_same = (row_index == column_index + own_delays[:, :, None, None]).astype(jnp.bfloat16)
    select_next = (row_index + BLK == column_index + own_delays[:, :, None, None]).astype(
        jnp.bfloat16
    )
    same = jnp.einsum("rena,ekai->rekni", lower, select_same, preferred_element_type=jnp.float32)
    backward = jnp.einsum(
        "rena,ekai->rekni", lower, select_next, preferred_element_type=jnp.float32
    )
    edge_part = jnp.einsum("rea,ekai->reki", later, select_next, preferred_element_type=jnp.float32)
    carried = jnp.concatenate([backward[:, :, :, 1:], edge_part[:, :, :, None]], axis=3)
    return (same + carried).reshape(receivers, experiments * SRC_EXP, samples)


def split(value):
    high = value.astype(jnp.bfloat16)
    return high, (value - high.astype(jnp.float32)).astype(jnp.bfloat16)


def exact_split(value):
    high = value.astype(ml_dtypes.bfloat16)
    low = (value - high.astype(np.float64)).astype(ml_dtypes.bfloat16)
    return jnp.asarray(high), jnp.asarray(low)


def filter_tables():
    turn = lambda n: (np.arange(n)[:, None] * np.arange(n)[None, :] % n) * (2.0 * np.pi / n)
    time_turn = turn(WIN)
    forward = jnp.asarray(
        np.concatenate([np.cos(time_turn), -np.sin(time_turn)], axis=1).astype(ml_dtypes.bfloat16)
    )
    inverse_high, inverse_low = exact_split(
        np.concatenate([np.cos(time_turn), -np.sin(time_turn)], axis=0) / math.sqrt(WIN)
    )
    inverse = jnp.concatenate([inverse_high, inverse_high, inverse_low], axis=0)
    source_turn = turn(SRC)
    cos_source = np.cos(source_turn) / math.sqrt(SRC)
    sin_source = np.sin(source_turn) / math.sqrt(SRC)
    mix_forward = exact_split(np.block([[cos_source, sin_source], [-sin_source, cos_source]]))
    mix_inverse = exact_split(np.block([[cos_source, -sin_source], [sin_source, cos_source]]))
    return forward, inverse, mix_forward, mix_inverse


def mix(table, value):
    table_high, table_low = table
    value_high, value_low = split(value)
    stacked = jnp.concatenate([value_high, value_low, value_high], axis=0)
    joined = jnp.concatenate([table_high, table_high, table_low], axis=1)
    return jnp.dot(joined, stacked, preferred_element_type=jnp.float32)


def filter_block(u_ref, first, count, tables, out_ref, picked=None):
    forward_ref, inverse_ref, mfh_ref, mfl_ref, mih_ref, mil_ref, limit_ref = tables
    sources, samples = u_ref.shape[1:]
    windows = samples // WIN
    picked = range(windows) if picked is None else picked
    groups = [(r, w) for r in range(first, first + count) for w in picked]
    scale = 1.0 / math.sqrt(WIN)
    rows = jnp.concatenate(
        [u_ref[r, :, w * WIN : (w + 1) * WIN] for r, w in groups], axis=0
    )
    spectrum = jnp.dot(rows, forward_ref[...], preferred_element_type=jnp.float32) * scale
    block = lambda g: slice(g * sources, (g + 1) * sources)
    field = jnp.concatenate(
        [
            jnp.concatenate([spectrum[block(g), :WIN], spectrum[block(g), WIN:]], axis=0)
            for g in range(len(groups))
        ],
        axis=1,
    )
    coeffs = mix((mfh_ref[...], mfl_ref[...]), field)
    real_part = coeffs[:sources]
    imag_part = coeffs[sources:]
    limit = limit_ref[...]
    magnitude = jnp.sqrt(real_part * real_part + imag_part * imag_part)
    factor = jnp.maximum(magnitude - limit, 0.0) / jnp.maximum(magnitude, limit)
    kept = jnp.concatenate([real_part * factor, imag_part * factor], axis=0)
    back = mix((mih_ref[...], mil_ref[...]), kept)
    lanes = lambda g: slice(g * WIN, (g + 1) * WIN)
    joined = jnp.concatenate(
        [
            jnp.concatenate([back[:sources, lanes(g)], back[sources:, lanes(g)]], axis=1)
            for g in range(len(groups))
        ],
        axis=0,
    )
    joined_high, joined_low = split(joined)
    restored = jnp.dot(
        jnp.concatenate([joined_high, joined_low, joined_high], axis=1),
        inverse_ref[...],
        preferred_element_type=jnp.float32,
    )
    for g, (r, w) in enumerate(groups):
        out_ref[r, :, w * WIN : (w + 1) * WIN] = restored[block(g)].astype(out_ref.dtype)


def pairs(rows, cols, transpose):
    row = lax.broadcasted_iota(jnp.int32, (rows, cols), 0)
    col = lax.broadcasted_iota(jnp.int32, (rows, cols), 1)
    hit = (col // SRC_EXP == row) if transpose else (row // SRC_EXP == col)
    return jnp.where(hit, 1.0, 0.0).astype(jnp.bfloat16)


def blend_residual(rec_ref, est_ref, before_ref, after_ref, shift_ref, last, res_ref, rows, wait):
    receivers, experiments, width = rec_ref.shape
    pair = pairs(experiments, est_ref.shape[1], True)
    shift = shift_ref[...]
    lane = lax.broadcasted_iota(jnp.int32, (experiments, width), 1)
    drop = jnp.logical_and(lane >= width - BLK, last)
    for r in rows:
        moved = jnp.concatenate([before_ref[r], est_ref[r], after_ref[r]], axis=1).astype(jnp.float32)
        full = moved.shape[1]
        for bit in range((BLK - 1).bit_length()):
            amount = 1 << bit
            moved = jnp.where((shift & amount) != 0, pltpu.roll(moved, amount, 1), moved)
        summed = jnp.dot(
            pair, moved[:, full - width :].astype(jnp.bfloat16),
            preferred_element_type=jnp.float32,
        )
        wait(r)
        residual = (rec_ref[r] - summed).astype(res_ref.dtype)
        res_ref[r] = jnp.where(drop, jnp.zeros_like(residual), residual)


def spread_update(res_ref, shift_ref, est_ref, u_ref, rows, last=None, wait=None):
    receivers, sources, samples = u_ref.shape
    experiments, width = res_ref.shape[1:]
    shift = shift_ref[...]
    dup = pairs(sources, experiments, False)
    for r in rows:
        if wait is not None:
            wait(r)
        residual = res_ref[r]
        if last is not None:
            lane = lax.broadcasted_iota(jnp.int32, (experiments, width), 1)
            drop = jnp.logical_and(lane >= samples, last)
            residual = jnp.where(drop, jnp.zeros_like(residual), residual).astype(jnp.bfloat16)
        moved = jnp.dot(dup, residual, preferred_element_type=jnp.float32)
        for bit in range((BLK - 1).bit_length()):
            amount = 1 << bit
            rolled = pltpu.roll(moved, width - amount, 1)
            moved = jnp.where((shift & amount) != 0, rolled, moved)
        value = RELAX * moved[:, :samples]
        if est_ref is not None:
            value = est_ref[r].astype(jnp.float32) + value
        u_ref[r] = value.astype(u_ref.dtype)


def spread_inputs(residual, delays):
    return [residual, delays.reshape(-1, 1)]


def filter_kernel(u_ref, *refs):
    filter_block(u_ref, 0, u_ref.shape[0], refs[:7], refs[7])


def filter_halo_kernel(stages, res_ref, shift_ref, *refs):
    tables = refs[:7]
    out_ref, before_ref, after_ref, u_ref, res_vmem, load_sem, send_sem, recv_sem = refs[7:]
    samples = u_ref.shape[2]
    loads = [
        pltpu.make_async_copy(res_ref.at[r], res_vmem.at[r], load_sem.at[r])
        for r in range(res_ref.shape[0])
    ]
    for load in loads:
        load.start()
    shot = lax.axis_index("shot")
    row = lax.axis_index("tm")
    has_prev = row > 0
    has_next = row < stages - 1
    barrier = pltpu.get_barrier_semaphore()
    mesh_id = pl.DeviceIdType.MESH

    @pl.when(has_prev)
    def _():
        pl.semaphore_signal(barrier, 1, device_id=(shot, row - 1), device_id_type=mesh_id)

    @pl.when(has_next)
    def _():
        pl.semaphore_signal(barrier, 1, device_id=(shot, row + 1), device_id_type=mesh_id)

    spread_update(
        res_vmem, shift_ref, None, u_ref, range(u_ref.shape[0]), jnp.logical_not(has_next),
        lambda r: loads[r].wait(),
    )
    windows = samples // WIN
    filter_block(u_ref, 0, u_ref.shape[0], tables, out_ref, (0, windows - 1))
    pl.semaphore_wait(barrier, has_prev.astype(jnp.int32) + has_next.astype(jnp.int32))

    def to_prev():
        return pltpu.make_async_remote_copy(
            src_ref=out_ref.at[:, :, pl.ds(0, BLK)],
            dst_ref=after_ref,
            send_sem=send_sem.at[0],
            recv_sem=recv_sem.at[0],
            device_id=(shot, row - 1),
            device_id_type=mesh_id,
        )

    def to_next():
        return pltpu.make_async_remote_copy(
            src_ref=out_ref.at[:, :, pl.ds(samples - BLK, BLK)],
            dst_ref=before_ref,
            send_sem=send_sem.at[1],
            recv_sem=recv_sem.at[1],
            device_id=(shot, row + 1),
            device_id_type=mesh_id,
        )

    pl.when(has_prev)(lambda: to_prev().start())
    pl.when(has_next)(lambda: to_next().start())
    filter_block(u_ref, 0, u_ref.shape[0], tables, out_ref, tuple(range(1, windows - 1)))

    @pl.when(has_prev)
    def _():
        to_prev().wait_send()
        to_next().wait_recv()

    @pl.when(has_next)
    def _():
        to_next().wait_send()
        to_prev().wait_recv()


def filter_with_halos(residual, delays, limits, tables):
    forward, inverse, mix_forward, mix_inverse = tables
    receivers = residual.shape[0]
    sources = delays.size
    samples = residual.shape[2] - BLK
    stages = lax.axis_size("tm")
    vmem = pl.BlockSpec(memory_space=pltpu.VMEM)
    anywhere = pl.BlockSpec(memory_space=pl.ANY)
    edge = jax.ShapeDtypeStruct((receivers, sources, BLK), jnp.bfloat16)
    return pl.pallas_call(
        functools.partial(filter_halo_kernel, stages),
        in_specs=[anywhere] + [vmem] * 8,
        out_specs=(vmem, anywhere, anywhere),
        out_shape=(jax.ShapeDtypeStruct((receivers, sources, samples), jnp.bfloat16), edge, edge),
        scratch_shapes=[
            pltpu.VMEM((receivers, sources, samples), jnp.bfloat16),
            pltpu.VMEM(residual.shape, residual.dtype),
            pltpu.SemaphoreType.DMA((receivers,)),
            pltpu.SemaphoreType.DMA((2,)),
            pltpu.SemaphoreType.DMA((2,)),
        ],
        compiler_params=pltpu.CompilerParams(
            collective_id=3, has_side_effects=True
        ),
    )(
        *spread_inputs(residual, delays),
        forward, inverse, *mix_forward, *mix_inverse, limits.reshape(sources, 1),
    )


def filter_send_kernel(
    count, stages, halves, est_ref, before_ref, after_ref, rec_ref, shift_ref, *refs
):
    tables = refs[:7]
    out_ref, done_ref, u_ref, res_ref, rec_vmem, load_sem, send_sem, recv_sem, own_sem = refs[7:]
    loads = [
        pltpu.make_async_copy(rec_ref.at[r], rec_vmem.at[r], load_sem.at[r])
        for r in range(rec_ref.shape[0])
    ]
    for load in loads:
        load.start()
    receivers, sources, samples = u_ref.shape
    own = sources // count
    per = receivers // halves
    me = lax.axis_index("shot")
    row = lax.axis_index("tm")
    barrier = pltpu.get_barrier_semaphore()

    def greet(step, carry):
        peer = lax.rem(me + step, count)
        pl.semaphore_signal(barrier, 1, device_id=(peer, row), device_id_type=pl.DeviceIdType.MESH)
        return carry

    lax.fori_loop(1, count, greet, 0)
    last = lax.axis_index("tm") == stages - 1

    def remote(half, peer, sender):
        return pltpu.make_async_remote_copy(
            src_ref=done_ref.at[pl.ds(half * per, per), pl.ds(peer * own, own), :],
            dst_ref=out_ref.at[pl.ds(sender * receivers + half * per, per), :, :],
            send_sem=send_sem.at[half, peer],
            recv_sem=recv_sem.at[half, sender],
            device_id=(peer, row),
            device_id_type=pl.DeviceIdType.MESH,
        )

    locals_ = []
    for half in range(halves):
        rows = range(half * per, (half + 1) * per)
        blend_residual(
            rec_vmem, est_ref, before_ref, after_ref, shift_ref, last, res_ref, rows,
            lambda r: loads[r].wait(),
        )
        spread_update(res_ref, shift_ref, est_ref, u_ref, rows)
        filter_block(u_ref, half * per, per, tables, done_ref)
        if half == 0:
            pl.semaphore_wait(barrier, count - 1)
        mine = pltpu.make_async_copy(
            done_ref.at[pl.ds(half * per, per), pl.ds(me * own, own), :],
            out_ref.at[pl.ds(me * receivers + half * per, per), :, :],
            own_sem.at[half],
        )
        mine.start()
        locals_.append(mine)

        def send(step, carry, half=half):
            remote(half, lax.rem(me + step, count), me).start()
            return carry

        lax.fori_loop(1, count, send, 0)

    for half in range(halves):

        def finish(step, carry, half=half):
            peer = lax.rem(me + step, count)
            remote(half, peer, me).wait_send()
            remote(half, me, peer).wait_recv()
            return carry

        lax.fori_loop(1, count, finish, 0)
        locals_[half].wait()


def filter_and_send(estimate, before, after, records, delays, limits, tables):
    forward, inverse, mix_forward, mix_inverse = tables
    receivers, sources, samples = estimate.shape
    count = lax.axis_size("shot")
    halves = 2
    vmem = pl.BlockSpec(memory_space=pltpu.VMEM)
    return pl.pallas_call(
        functools.partial(filter_send_kernel, count, lax.axis_size("tm"), halves),
        in_specs=[vmem] * 3 + [pl.BlockSpec(memory_space=pl.ANY)] + [vmem] * 8,
        out_specs=pl.BlockSpec(memory_space=pl.ANY),
        out_shape=jax.ShapeDtypeStruct(
            (receivers * count, sources // count, samples), jnp.bfloat16
        ),
        scratch_shapes=[
            pltpu.VMEM(estimate.shape, jnp.bfloat16),
            pltpu.VMEM(estimate.shape, jnp.bfloat16),
            pltpu.VMEM(records.shape, jnp.bfloat16),
            pltpu.VMEM(records.shape, records.dtype),
            pltpu.SemaphoreType.DMA((records.shape[0],)),
            pltpu.SemaphoreType.DMA((halves, count)),
            pltpu.SemaphoreType.DMA((halves, count)),
            pltpu.SemaphoreType.DMA((halves,)),
        ],
        compiler_params=pltpu.CompilerParams(
            collective_id=2, has_side_effects=True
        ),
    )(
        estimate,
        before,
        after,
        records,
        *spread_inputs(records, delays)[1:],
        forward, inverse, *mix_forward, *mix_inverse, limits.reshape(sources, 1),
    )


def coherence(gathers, limits, tables):
    forward, inverse, mix_forward, mix_inverse = tables
    receivers, sources, samples = gathers.shape
    vmem = pl.BlockSpec(memory_space=pltpu.VMEM)
    return pl.pallas_call(
        filter_kernel,
        in_specs=[vmem] * 8,
        out_specs=vmem,
        out_shape=jax.ShapeDtypeStruct(gathers.shape, jnp.bfloat16),
        compiler_params=pltpu.CompilerParams(vmem_limit_bytes=48 * 1024 * 1024),
    )(gathers, forward, inverse, *mix_forward, *mix_inverse, limits.reshape(sources, 1))


def exchange_kernel(count, outgoing, incoming, src_ref, out_ref, send_sem, recv_sem, own_sem):
    me = lax.axis_index("shot")
    row = lax.axis_index("tm")
    barrier = pltpu.get_barrier_semaphore()

    def greet(step, carry):
        peer = lax.rem(me + step, count)
        pl.semaphore_signal(barrier, 1, device_id=(peer, row), device_id_type=pl.DeviceIdType.MESH)
        return carry

    lax.fori_loop(1, count, greet, 0)
    pl.semaphore_wait(barrier, count - 1)
    own = pltpu.make_async_copy(src_ref.at[outgoing(me)], out_ref.at[incoming(me)], own_sem)
    own.start()

    def remote(peer, sender):
        return pltpu.make_async_remote_copy(
            src_ref=src_ref.at[outgoing(peer)],
            dst_ref=out_ref.at[incoming(sender)],
            send_sem=send_sem.at[peer],
            recv_sem=recv_sem.at[sender],
            device_id=(peer, row),
            device_id_type=pl.DeviceIdType.MESH,
        )

    def send(step, carry):
        remote(lax.rem(me + step, count), me).start()
        return carry

    lax.fori_loop(1, count, send, 0)

    def finish(step, carry):
        peer = lax.rem(me + step, count)
        remote(peer, me).wait_send()
        remote(me, peer).wait_recv()
        return carry

    lax.fori_loop(1, count, finish, 0)
    own.wait()


def exchange(value, out_shape, outgoing, incoming, tag):
    count = lax.axis_size("shot")
    anywhere = pl.BlockSpec(memory_space=pl.ANY)
    return pl.pallas_call(
        functools.partial(exchange_kernel, count, outgoing, incoming),
        in_specs=[anywhere],
        out_specs=anywhere,
        out_shape=jax.ShapeDtypeStruct(out_shape, value.dtype),
        scratch_shapes=[
            pltpu.SemaphoreType.DMA((count,)),
            pltpu.SemaphoreType.DMA((count,)),
            pltpu.SemaphoreType.DMA,
        ],
        compiler_params=pltpu.CompilerParams(collective_id=tag, has_side_effects=True),
    )(value)


def to_sources(estimate):
    receivers, sources, samples = estimate.shape
    count = lax.axis_size("shot")
    own = sources // count
    return exchange(
        estimate,
        (receivers * count, own, samples),
        lambda peer: (slice(None), pl.ds(peer * own, own), slice(None)),
        lambda sender: (pl.ds(sender * receivers, receivers), slice(None), slice(None)),
        0,
    )


def receive_kernel(count, stages, src_ref, out_ref, send_sem, recv_sem, own_sem):
    part, own, samples = out_ref.shape[0], src_ref.shape[1], src_ref.shape[2]
    me = lax.axis_index("shot")
    row = lax.axis_index("tm")
    has_prev = row > 0
    has_next = row < stages - 1
    mesh_id = pl.DeviceIdType.MESH
    barrier = pltpu.get_barrier_semaphore()

    def greet(step, carry):
        peer = lax.rem(me + step, count)
        pl.semaphore_signal(barrier, 1, device_id=(peer, row), device_id_type=mesh_id)
        return carry

    lax.fori_loop(1, count, greet, 0)

    def greet_row(target_row):
        def one(peer, carry):
            pl.semaphore_signal(barrier, 1, device_id=(peer, target_row), device_id_type=mesh_id)
            return carry

        lax.fori_loop(0, count, one, 0)

    pl.when(has_prev)(lambda: greet_row(row - 1))
    pl.when(has_next)(lambda: greet_row(row + 1))
    pl.semaphore_wait(
        barrier,
        count - 1 + count * (has_prev.astype(jnp.int32) + has_next.astype(jnp.int32)),
    )

    def body(sender):
        return (slice(None), pl.ds(sender * own, own), pl.ds(0, samples))

    def tail(sender):
        return (slice(None), pl.ds(sender * own, own), pl.ds(samples, BLK))

    def chunk(peer, sender):
        return pltpu.make_async_remote_copy(
            src_ref=src_ref.at[pl.ds(peer * part, part)],
            dst_ref=out_ref.at[body(sender)],
            send_sem=send_sem.at[0, peer],
            recv_sem=recv_sem.at[0, sender],
            device_id=(peer, row),
            device_id_type=mesh_id,
        )

    def edge(peer, sender, target_row):
        return pltpu.make_async_remote_copy(
            src_ref=src_ref.at[pl.ds(peer * part, part), :, pl.ds(0, BLK)],
            dst_ref=out_ref.at[tail(sender)],
            send_sem=send_sem.at[1, peer],
            recv_sem=recv_sem.at[1, sender],
            device_id=(peer, target_row),
            device_id_type=mesh_id,
        )

    @pl.when(has_prev)
    def _():
        def send_edge(peer, carry):
            edge(peer, me, row - 1).start()
            return carry

        lax.fori_loop(0, count, send_edge, 0)

    mine = pltpu.make_async_copy(src_ref.at[pl.ds(me * part, part)], out_ref.at[body(me)], own_sem)
    mine.start()

    def send_body(step, carry):
        chunk(lax.rem(me + step, count), me).start()
        return carry

    lax.fori_loop(1, count, send_body, 0)

    @pl.when(has_prev)
    def _():
        def finish_edge(peer, carry):
            edge(peer, me, row - 1).wait_send()
            return carry

        lax.fori_loop(0, count, finish_edge, 0)

    @pl.when(has_next)
    def _():
        def land_edge(sender, carry):
            edge(me, sender, row + 1).wait_recv()
            return carry

        lax.fori_loop(0, count, land_edge, 0)

    def finish_body(step, carry):
        peer = lax.rem(me + step, count)
        chunk(peer, me).wait_send()
        chunk(me, peer).wait_recv()
        return carry

    lax.fori_loop(1, count, finish_body, 0)
    mine.wait()


def to_receivers(records):
    receivers, own, samples = records.shape
    count = lax.axis_size("shot")
    part = receivers // count
    return pl.pallas_call(
        functools.partial(receive_kernel, count, lax.axis_size("tm")),
        in_specs=[pl.BlockSpec(memory_space=pl.ANY)],
        out_specs=pl.BlockSpec(memory_space=pl.ANY),
        out_shape=jax.ShapeDtypeStruct((part, own * count, samples + BLK), records.dtype),
        scratch_shapes=[
            pltpu.SemaphoreType.DMA((2, count)),
            pltpu.SemaphoreType.DMA((2, count)),
            pltpu.SemaphoreType.DMA,
        ],
        compiler_params=pltpu.CompilerParams(collective_id=1, has_side_effects=True),
    )(records)


def local(blended, delays, thresholds):
    tables = filter_tables()
    extended = to_receivers(blended)
    row = lax.axis_index("tm")
    estimate, before, after = filter_with_halos(extended, delays, thresholds[0], tables)
    before = jnp.where(row == 0, jnp.zeros_like(before), before)
    last = row == lax.axis_size("tm") - 1
    after = jnp.where(last, jnp.zeros_like(after), after)
    return filter_and_send(estimate, before, after, extended, delays, thresholds[1], tables)


def solution(mesh):
    return jax.shard_map(
        local,
        mesh=mesh,
        in_specs=(P(None, "shot", "tm"), P(), P()),
        out_specs=P(None, "shot", "tm"),
        check_vma=False,
    )
```
